32 devices in a mesh: parts: 2 (over y), seq: 8 (over z, x), dp: 2 (over core).
Axes of the slice: x: 2, y: 2, z: 4, core: 2. Of those that a mesh axis runs over, the one named last changes fastest.
Arguments:
- queries: bfloat16 [4, 3072, 1024], P(('parts', 'dp'), 'seq'), parts along dimension 0, may hold values from -6 to 6
- keys: bfloat16 [4, 3072, 1024], P(('parts', 'dp'), 'seq'), parts along dimension 0, may hold values from -6 to 6
- values: bfloat16 [4, 3072, 1024], P(('parts', 'dp'), 'seq'), parts along dimension 0, may hold values from -61 to 61, as said below
- out_weight: bfloat16 [1024, 2048], replicated, may hold values from -0.1875 to 0.1875
- out_grad: bfloat16 [4, 3072, 2048], P(('parts', 'dp'), 'seq'), parts along dimension 0, may hold values from -6 to 6
Outputs:
- output: bfloat16 [4, 3072, 2048], P(('parts', 'dp'), 'seq'), parts along dimension 0
- query_grad: bfloat16 [4, 3072, 1024], P(('parts', 'dp'), 'seq'), parts along dimension 0
- key_grad: bfloat16 [4, 3072, 1024], P(('parts', 'dp'), 'seq'), parts along dimension 0
- value_grad: bfloat16 [4, 3072, 1024], P(('parts', 'dp'), 'seq'), parts along dimension 0
- weight_grad: float32 [2048, 2048], P(('parts', 'seq'), 'dp'), parts along dimension 0
The draws below stay inside these ranges and needn't reach their ends.
There are 2 independent parts, one for each index of `parts`. The reference program is written for one: setup_inputs(seed, part) draws one part's arguments, and reference() takes and returns one part's arrays. A program takes and returns all parts, laid end to end along the dimension named above; an argument that names none is the same for every part. Nothing has to cross between parts.
Inputs may be any that keep to these rules, and one draw needn't show every extreme that they name: `values`: entries are real-valued.
All inputs are finite; a program needn't handle non-finite values.
Results may differ from the reference program's by a relative error of at most 0.0055.
Values sent between devices are 32-bit elements; how exact they have to be, the bound alone decides.
No kernel may reach another device: no remote copies, remote signals or barrier semaphores. Data moves between devices by JAX's collectives and lax.ppermute only.
A program may use at most 128 MiB of HBM per device.

```python
import math
import jax
import jax.numpy as jnp
from jax import lax

D = 2048
H = 8
HD = 128
HH = 1024
LEN = 3072
BATCH = 2
ALL_TOKENS = 6144


def draw_values(key, part):
    first_key, second_key, third_key = jax.random.split(key, 3)
    array_shape = (BATCH, LEN, HH)
    entries = jnp.clip(jax.random.normal(first_key, array_shape, jnp.float32), -6.0, 6.0)
    column_scale = jnp.exp((jax.random.uniform(second_key, (HH,), jnp.float32) - 0.5) * math.log(10.0))
    row_scale = jnp.exp((jax.random.uniform(third_key, (BATCH, LEN, 1), jnp.float32) - 0.5) * math.log(10.0))
    return (entries * column_scale * row_scale).astype(jnp.bfloat16)


def steps_of(stream_key, extent, pieces, smallest, largest):
    loudness = 1.0
    for position, shards_of in pieces:
        steps = jax.random.uniform(jax.random.fold_in(jax.random.fold_in(stream_key, 6), position), (shards_of,), jnp.float32, smallest / len(pieces), largest / len(pieces))
        loudness = loudness * jnp.repeat(jnp.exp(steps), extent[position] // shards_of).reshape((-1,) + (1,) * (len(extent) - 1 - position))
    return loudness


def gaussian(rng, shape, scale, bound, pieces=(), dtype=jnp.bfloat16):
    factor_of = steps_of(rng, shape, pieces, -0.22, 0.18) if pieces else 1.0
    drawn = jax.random.normal(rng, shape, jnp.float32) * scale * factor_of
    return jnp.minimum(jnp.maximum(drawn, -bound), bound).astype(dtype)


def setup_inputs(seed: int = 0, part: int = 0) -> dict:
    key_list = jax.random.split(jax.random.key(seed), 6)
    part_splits = jax.random.split(jax.random.fold_in(key_list[5], part), 6)
    return {
        "queries": gaussian(part_splits[0], (BATCH, LEN, HH), 1.0, 6.0, ((0, 2), (1, 8))),
        "keys": gaussian(part_splits[1], (BATCH, LEN, HH), 1.0, 6.0, ((0, 2), (1, 8))),
        "values": draw_values(jax.random.fold_in(jax.random.fold_in(key_list[5], part), 71), part),
        "out_weight": gaussian(key_list[3], (HH, D), HH ** -0.5, 0.1875),
        "out_grad": gaussian(part_splits[4], (BATCH, LEN, D), 1.0, 6.0, ((0, 2), (1, 8))),
    }


PRECISE = lax.Precision.HIGHEST
EPSILON = 1e-06

def causal_mask(length):
    rows_idx = lax.broadcasted_iota(jnp.int32, (length, length), 0)
    cols_idx = lax.broadcasted_iota(jnp.int32, (length, length), 1)
    return jnp.where(rows_idx >= cols_idx, 1.0, 0.0).astype(jnp.float32)

def in_blocks(array, blocks, block_len):
    return array.reshape(blocks, block_len, H, HD)

def forward_pass(query_all, key_all, value_all, blocks, block_len, causal):

    def advance(carried, inputs):
        query_blk, key_blk, value_blk = inputs
        scores = jnp.einsum('thd,shd->hts', query_blk, key_blk, precision=PRECISE) * causal
        result = jnp.einsum('hts,she->the', scores, value_blk, precision=PRECISE)
        result = result + jnp.einsum('thd,hde->the', query_blk, carried, precision=PRECISE)
        carried = carried + jnp.einsum('thd,the->hde', key_blk, value_blk, precision=PRECISE)
        return (carried, result)
    start_state = jnp.zeros((H, HD, HD), jnp.float32)
    packed = (in_blocks(query_all, blocks, block_len), in_blocks(key_all, blocks, block_len), in_blocks(value_all, blocks, block_len))
    _, result = lax.scan(advance, start_state, packed)
    return result.reshape(LEN, H, HD)

def query_pass(grad_all, key_all, value_all, blocks, block_len, causal):

    def advance(carried, inputs):
        grad_blk, key_blk, value_blk = inputs
        cross_terms = jnp.einsum('the,she->hts', grad_blk, value_blk, precision=PRECISE) * causal
        result = jnp.einsum('hts,shd->thd', cross_terms, key_blk, precision=PRECISE)
        result = result + jnp.einsum('the,hde->thd', grad_blk, carried, precision=PRECISE)
        carried = carried + jnp.einsum('thd,the->hde', key_blk, value_blk, precision=PRECISE)
        return (carried, result)
    start_state = jnp.zeros((H, HD, HD), jnp.float32)
    packed = (in_blocks(grad_all, blocks, block_len), in_blocks(key_all, blocks, block_len), in_blocks(value_all, blocks, block_len))
    _, result = lax.scan(advance, start_state, packed)
    return result.reshape(LEN, H, HD)

def key_value_pass(grad_all, query_all, key_all, value_all, blocks, block_len, causal):

    def advance(carried, inputs):
        grad_blk, query_blk, key_blk, value_blk = inputs
        cross_terms = jnp.einsum('the,she->hts', grad_blk, value_blk, precision=PRECISE) * causal
        scores = jnp.einsum('thd,shd->hts', query_blk, key_blk, precision=PRECISE) * causal
        key_part = jnp.einsum('hts,thd->shd', cross_terms, query_blk, precision=PRECISE)
        key_part = key_part + jnp.einsum('she,hde->shd', value_blk, carried, precision=PRECISE)
        value_part = jnp.einsum('hts,the->she', scores, grad_blk, precision=PRECISE)
        value_part = value_part + jnp.einsum('shd,hde->she', key_blk, carried, precision=PRECISE)
        carried = carried + jnp.einsum('thd,the->hde', query_blk, grad_blk, precision=PRECISE)
        return (carried, (key_part, value_part))
    start_state = jnp.zeros((H, HD, HD), jnp.float32)
    packed = (in_blocks(grad_all, blocks, block_len), in_blocks(query_all, blocks, block_len), in_blocks(key_all, blocks, block_len), in_blocks(value_all, blocks, block_len))
    _, (key_part, value_part) = lax.scan(advance, start_state, packed, reverse=True)
    return (key_part.reshape(LEN, H, HD), value_part.reshape(LEN, H, HD))

def reference(queries, keys, values, out_weight, out_grad):
    block_len = math.gcd(LEN, 512)
    blocks = LEN // block_len
    causal = causal_mask(block_len)
    outputs, query_grads, key_grads, value_grads = ([], [], [], [])
    weight_sum = jnp.zeros((HH, D), jnp.float32)
    for member in range(BATCH):
        query_all = queries[member].astype(jnp.float32).reshape(LEN, H, HD)
        key_all = keys[member].astype(jnp.float32).reshape(LEN, H, HD)
        value_all = values[member].astype(jnp.float32).reshape(LEN, H, HD)
        attended = forward_pass(query_all, key_all, value_all, blocks, block_len, causal)
        inverse = lax.rsqrt(lax.optimization_barrier(jnp.mean(attended * attended, axis=-1, keepdims=True)) + EPSILON)
        normed = attended * inverse
        normed_b = normed.reshape(LEN, HH).astype(jnp.bfloat16)
        outputs.append(jnp.dot(normed_b, out_weight, preferred_element_type=jnp.float32).astype(jnp.bfloat16))
        grad_rows = out_grad[member]
        d_normed = jnp.dot(grad_rows, out_weight.T, preferred_element_type=jnp.float32).reshape(LEN, H, HD)
        d_att = inverse * (d_normed - normed * lax.optimization_barrier(jnp.mean(d_normed * normed, axis=-1, keepdims=True)))
        d_att_b = lax.optimization_barrier(d_att.astype(jnp.bfloat16))
        d_att_r = d_att_b.astype(jnp.float32)
        query_part = query_pass(d_att_r, key_all, value_all, blocks, block_len, causal)
        key_part, value_part = key_value_pass(d_att_r, query_all, key_all, value_all, blocks, block_len, causal)
        query_grads.append(query_part.reshape(LEN, HH).astype(jnp.bfloat16))
        key_grads.append(key_part.reshape(LEN, HH).astype(jnp.bfloat16))
        value_grads.append(value_part.reshape(LEN, HH).astype(jnp.bfloat16))
        weight_sum = weight_sum + jnp.dot(normed_b.T, grad_rows, preferred_element_type=jnp.float32)
    weight_grad = weight_sum / math.sqrt(ALL_TOKENS)
    return (jnp.stack(outputs), jnp.stack(query_grads), jnp.stack(key_grads), jnp.stack(value_grads), weight_grad)
```

```python
import functools
import math

import jax
import jax.numpy as jnp
from jax import lax
from jax.experimental import pallas as pl
from jax.experimental.pallas import tpu as pltpu
from jax.sharding import PartitionSpec as P

H = 8
HD = 128
PAIRS = H // 2
EPSILON = 1e-06
F32 = jnp.float32
BF16 = jnp.bfloat16
VMEM = pltpu.VMEM
VMEM_LIMIT = 48 << 20

NN = (((1,), (0,)), ((), ()))
NT = (((1,), (1,)), ((), ()))
TN = (((0,), (0,)), ((), ()))


def dot(a, b, dims):
    return lax.dot_general(a, b, dims, preferred_element_type=F32)


def halves(a):
    high = a.astype(BF16)
    return high, (a - high.astype(F32)).astype(BF16)


def two_pass(a, b, dims):
    high, low = halves(a)
    return dot(high, b, dims) + dot(low, b, dims)


def two_pass_right(a, b, dims):
    high, low = halves(b)
    return dot(a, high, dims) + dot(a, low, dims)


def causal(length, lower):
    rows = lax.broadcasted_iota(jnp.int32, (length, length), 0)
    cols = lax.broadcasted_iota(jnp.int32, (length, length), 1)
    return rows >= cols if lower else rows <= cols


def lanes(head):
    if isinstance(head, int):
        return pl.ds(head * HD, HD)
    return pl.ds(pl.multiple_of(head * HD, HD), HD)


def call(body, out_shapes, operands, flops, name):
    specs = []
    for operand in operands:
        space = pltpu.SMEM if operand.dtype == jnp.int32 else VMEM
        specs.append(pl.BlockSpec(memory_space=space))
    total = sum(math.prod(o.shape) * o.dtype.itemsize for o in operands)
    total += sum(math.prod(o.shape) * o.dtype.itemsize for o in out_shapes)
    return pl.pallas_call(
        body,
        out_shape=tuple(out_shapes),
        in_specs=specs,
        out_specs=tuple(pl.BlockSpec(memory_space=VMEM) for _ in out_shapes),
        compiler_params=pltpu.CompilerParams(vmem_limit_bytes=VMEM_LIMIT),
        cost_estimate=pl.CostEstimate(flops=flops, bytes_accessed=total, transcendentals=0),
        name=name,
    )(*operands)


def shape(dims, dtype):
    return jax.ShapeDtypeStruct(dims, dtype)


def state_body(place, k_ref, v_ref, keep_ref, send_ref):
    low = place[0]
    for j in range(PAIRS):
        for out, head in ((keep_ref, 2 * j + low), (send_ref, 2 * j + 1 - low)):
            out[j] = dot(k_ref[:, lanes(head)], v_ref[:, lanes(head)], TN)


def local_body(q_ref, k_ref, v_ref, out_ref):
    mask = causal(q_ref.shape[0], True)
    for h in range(H):
        scores = dot(q_ref[:, lanes(h)], k_ref[:, lanes(h)], NT)
        scores = jnp.where(mask, scores, 0.0)
        out_ref[:, lanes(h)] = two_pass(scores, v_ref[:, lanes(h)], NN)


def norm_body(
    place, q_ref, att_ref, dn_ref, own_ref, other_ref, nb_ref, nb32_ref, da_ref, keep_ref, send_ref
):
    low = place[0]
    for j in range(PAIRS):
        for prior, out, head in (
            (own_ref, keep_ref, 2 * j + low),
            (other_ref, send_ref, 2 * j + 1 - low),
        ):
            at = lanes(head)
            q = q_ref[:, at]
            attended = att_ref[:, at] + two_pass_right(q, prior[j], NN)
            inverse = lax.rsqrt(jnp.mean(attended * attended, axis=-1, keepdims=True) + EPSILON)
            normed = attended * inverse
            rounded = normed.astype(BF16)
            nb_ref[:, at] = rounded
            nb32_ref[:, at] = rounded.astype(F32)
            d_normed = dn_ref[:, at]
            mean = jnp.mean(d_normed * normed, axis=-1, keepdims=True)
            d_att = (inverse * (d_normed - normed * mean)).astype(BF16)
            da_ref[:, at] = d_att
            out[j] = dot(q, d_att, TN)


def grads_body(
    place, q_ref, k_ref, v_ref, da_ref, own_ref, other_ref, qg_ref, kl_ref, vl_ref
):
    low = place[0]
    lower = causal(q_ref.shape[0], True)
    upper = causal(q_ref.shape[0], False)
    for j in range(PAIRS):
        for prior, head in ((own_ref, 2 * j + low), (other_ref, 2 * j + 1 - low)):
            at = lanes(head)
            q, k, v, d_att = q_ref[:, at], k_ref[:, at], v_ref[:, at], da_ref[:, at]
            cross = jnp.where(lower, dot(d_att, v, NT), 0.0)
            part = two_pass(cross, k, NN) + two_pass_right(d_att, prior[j], NT)
            qg_ref[:, at] = part.astype(BF16)
            cross = jnp.where(upper, dot(v, d_att, NT), 0.0)
            kl_ref[:, at] = two_pass(cross, q, NN)
            scores = jnp.where(upper, dot(k, q, NT), 0.0)
            vl_ref[:, at] = two_pass(scores, d_att, NN)


def final_body(place, k_ref, v_ref, kl_ref, vl_ref, own_ref, other_ref, kg_ref, vg_ref):
    low = place[0]
    for j in range(PAIRS):
        for later, head in ((own_ref, 2 * j + low), (other_ref, 2 * j + 1 - low)):
            at = lanes(head)
            high, rest = halves(later[j])
            v, k = v_ref[:, at], k_ref[:, at]
            kg_ref[:, at] = (kl_ref[:, at] + (dot(v, high, NT) + dot(v, rest, NT))).astype(BF16)
            vg_ref[:, at] = (vl_ref[:, at] + (dot(k, high, NN) + dot(k, rest, NN))).astype(BF16)


def weight_body(
    rows, place, nb_ref, g_ref, nbo_ref, go_ref, keep0, keep1, send0, send1
):
    low, core = place[0], place[1]
    width = go_ref.shape[1] // 2
    for i, j in enumerate(rows):
        for outs, head in (((keep0, keep1), 2 * j + low), ((send0, send1), 2 * j + 1 - low)):
            mine = nb_ref[:, lanes(head)]
            theirs = nbo_ref[:, lanes(head)].astype(BF16)
            for c in range(2):
                start = pl.multiple_of((core * 2 + c) * width, width)
                ours = g_ref[:, pl.ds(start, width)]
                other = go_ref[:, c * width : (c + 1) * width].astype(BF16)
                outs[c][i] = dot(mine, ours, TN) + dot(theirs, other, TN)


def exclusive(keep, send, count, low, reverse):
    swap = [(s, s ^ 1) for s in range(count)]
    received = lax.ppermute(send, "seq", swap)
    base = keep + received
    pairs = count // 2
    shift = -2 if reverse else 2

    def links(step):
        jump = shift * step
        return [(s, s + jump) for s in range(count) if 0 <= s + jump < count]

    outside = lax.ppermute(base, "seq", links(1))
    step = 1
    total = base + outside
    while 2 * step < pairs:
        step *= 2
        if 2 * step < pairs:
            got = lax.ppermute(total, "seq", links(step))
            outside, total = outside + got, total + got
        else:
            outside = outside + lax.ppermute(total, "seq", links(step))
    first = low == (1 if reverse else 0)
    mine = jnp.where(first, outside, outside + received)
    theirs = jnp.where(first, outside + keep, outside)
    return mine, lax.ppermute(theirs, "seq", swap)


def per_device(queries, keys, values, out_weight, out_grad):
    count = lax.axis_size("seq")
    cores = lax.axis_size("dp")
    spot = lax.axis_index("seq")
    core = lax.axis_index("dp")
    low, level = spot % 2, spot // 2
    q, k, v, g = queries[0], keys[0], values[0], out_grad[0]
    length, features = q.shape
    width = g.shape[1]
    place = jnp.stack([low, core]).astype(jnp.int32)
    state = shape((PAIRS, HD, HD), F32)
    rows32 = shape((length, features), F32)
    rows16 = shape((length, features), BF16)
    unit = 2 * H * length * HD

    keep, send = call(state_body, (state, state), (place, k, v), unit * HD, "state")
    own, other = exclusive(keep, send, count, low, False)

    fast = count == 8 and cores == 2
    half = width // 2
    swap = [(0, 1), (1, 0)]
    if fast:
        away = lax.dynamic_slice_in_dim(g, (1 - core) * half, half, axis=1).astype(F32)
        go = lax.ppermute(away, "dp", swap)
    (att,) = call(local_body, (rows32,), (q, k, v), 3 * unit * length, "local")
    d_normed = lax.dot_general(g, out_weight, NT, preferred_element_type=F32)

    nb, nb32, da, gkeep, gsend = call(
        norm_body,
        (rows16, rows32, rows16, state, state),
        (place, q, att, d_normed, own, other),
        3 * unit * HD,
        "norm",
    )
    own_later, other_later = exclusive(gkeep, gsend, count, low, True)
    scale = 1.0 / math.sqrt(length * count * cores)
    if fast:
        nbo = lax.ppermute(nb32, "dp", swap)
        block = shape((2, HD, half // 2), F32)
        chunks = {}
        for name, rows in (("far", (0, 3)), ("near", (1, 2))):
            out = call(
                functools.partial(weight_body, rows),
                (block,) * 4,
                (place, nb, g, nbo, go),
                2 * length * features * half,
                "weight_" + name,
            )
            for c in range(2):
                chunks[name, c] = out[c], out[2 + c]
        weight_grad = scatter(chunks, level) * scale
    else:
        product = lax.dot_general(nb, g, TN, preferred_element_type=F32)
        product = lax.psum_scatter(product, "dp", scatter_dimension=1, tiled=True)
        weight_grad = lax.psum_scatter(product, "seq", scatter_dimension=0, tiled=True) * scale

    output = jnp.dot(nb, out_weight, preferred_element_type=F32).astype(BF16)
    query_grad, key_local, value_local = call(
        grads_body,
        (rows16, rows32, rows32),
        (place, q, k, v, da, own, other),
        9 * unit * length,
        "grads",
    )
    key_grad, value_grad = call(
        final_body,
        (rows16, rows16),
        (place, k, v, key_local, value_local, own_later, other_later),
        4 * unit * HD,
        "final",
    )
    return output[None], query_grad[None], key_grad[None], value_grad[None], weight_grad


def scatter(chunks, level):
    swap = [(s, s ^ 1) for s in range(8)]

    def on(links):
        return [(2 * a + i, 2 * b + i) for a, b in links for i in range(2)]

    inward = on([(0, 1), (3, 2)])
    middle = on([(1, 2), (2, 1)])
    outward = on([(2, 3), (1, 0)])
    lower = level < 2
    parts = []
    for c in range(2):
        keep, send = chunks["far", c]
        base = keep + lax.ppermute(send, "seq", swap)
        up = jnp.where(lower, base[1], base[0])
        down = jnp.where(lower, base[0], base[1])
        got = lax.ppermute(up, "seq", inward)
        got = lax.ppermute(up + got, "seq", middle)
        got = lax.ppermute(down + got, "seq", outward)
        far = down + got

        keep, send = chunks["near", c]
        base = keep + lax.ppermute(send, "seq", swap)
        up = jnp.where(lower, base[1], base[0])
        down = jnp.where(lower, base[0], base[1])
        got = lax.ppermute(up, "seq", inward)
        direct = lax.ppermute(down, "seq", inward)
        got = lax.ppermute(up + got, "seq", middle)
        near = (down + direct) + got
        outer = (level == 0) | (level == 3)
        parts.append(jnp.where(outer, far, near))
    return jnp.concatenate(parts, axis=1)


def solution(mesh):
    rows = P(("parts", "dp"), "seq", None)
    return jax.shard_map(
        per_device,
        mesh=mesh,
        in_specs=(rows, rows, rows, P(), rows),
        out_specs=(rows, rows, rows, rows, P(("parts", "seq"), "dp")),
        check_vma=False,
    )
```

```python
import functools
import math

import jax
import jax.numpy as jnp
from jax import lax
from jax.experimental import pallas as pl
from jax.experimental.pallas import tpu as pltpu
from jax.sharding import PartitionSpec as P

H = 8
HD = 128
PAIR = 2 * HD
GROUPS = ((0, 3), (1, 2))
EPSILON = 1e-06
F32 = jnp.float32
BF16 = jnp.bfloat16
VMEM = pltpu.VMEM
VMEM_LIMIT = 16 << 20
COST = 16

NN = (((1,), (0,)), ((), ()))
NT = (((1,), (1,)), ((), ()))
TN = (((0,), (0,)), ((), ()))


def dot(a, b, dims):
    return lax.dot_general(a, b, dims, preferred_element_type=F32)


def halves(a):
    high = a.astype(BF16)
    return high, (a - high.astype(F32)).astype(BF16)


def two_pass(a, b, dims):
    high, low = halves(a)
    return dot(high, b, dims) + dot(low, b, dims)


def two_pass_right(a, b, dims):
    high, low = halves(b)
    return dot(a, high, dims) + dot(a, low, dims)


def causal(length, lower):
    rows = lax.broadcasted_iota(jnp.int32, (length, length), 0)
    cols = lax.broadcasted_iota(jnp.int32, (length, length), 1)
    return rows >= cols if lower else rows <= cols


def at(position, size=HD):
    if isinstance(position, int):
        return pl.ds(position * size, size)
    return pl.ds(pl.multiple_of(position * size, size), size)


def shape(dims, dtype):
    return jax.ShapeDtypeStruct(dims, dtype)


def call(body, out_shapes, operands, flops, name):
    specs = []
    for operand in operands:
        space = pltpu.SMEM if operand.dtype == jnp.int32 else VMEM
        specs.append(pl.BlockSpec(memory_space=space))
    return pl.pallas_call(
        body,
        out_shape=tuple(out_shapes),
        in_specs=specs,
        out_specs=tuple(pl.BlockSpec(memory_space=VMEM) for _ in out_shapes),
        compiler_params=pltpu.CompilerParams(vmem_limit_bytes=VMEM_LIMIT),
        cost_estimate=pl.CostEstimate(flops=flops // COST, bytes_accessed=0, transcendentals=0),
        name=name,
    )(*operands)


def after(value, *others):
    return lax.optimization_barrier((value, *others))[0]


def state_body(place, k_ref, v_ref, *outs):
    low = place[0]
    for g, rows in enumerate(GROUPS):
        for i, j in enumerate(rows):
            for out, head in ((outs[2 * g], 2 * j + low), (outs[2 * g + 1], 2 * j + 1 - low)):
                out[i] = dot(k_ref[:, at(head)], v_ref[:, at(head)], TN)


def local_body(q_ref, k_ref, v_ref, out_ref):
    mask = causal(q_ref.shape[0], True)
    for h in range(H):
        scores = dot(q_ref[:, at(h)], k_ref[:, at(h)], NT)
        scores = jnp.where(mask, scores, 0.0)
        out_ref[:, at(h)] = two_pass(scores, v_ref[:, at(h)], NN)


def d_normed_body(g_ref, w_ref, out_ref):
    @pl.loop(0, H // 2)
    def _(j):
        out_ref[:, at(j, PAIR)] = dot(g_ref[...], w_ref[at(j, PAIR), :], NT)


def norm_body(
    rows, place, q_ref, att_ref, dn_ref, own_ref, other_ref, nb_ref, nb32_ref, da_ref, keep_ref, send_ref
):
    low = place[0]
    for i, j in enumerate(rows):
        for prior, out, part in ((own_ref, keep_ref, low), (other_ref, send_ref, 1 - low)):
            here, there = at(2 * j + part), at(2 * i + part)
            q = q_ref[:, here]
            attended = att_ref[:, here] + two_pass_right(q, prior[i], NN)
            inverse = lax.rsqrt(jnp.mean(attended * attended, axis=-1, keepdims=True) + EPSILON)
            normed = attended * inverse
            rounded = normed.astype(BF16)
            nb_ref[:, there] = rounded
            nb32_ref[:, there] = rounded.astype(F32)
            d_normed = dn_ref[:, here]
            mean = jnp.mean(d_normed * normed, axis=-1, keepdims=True)
            d_att = (inverse * (d_normed - normed * mean)).astype(BF16)
            da_ref[:, there] = d_att
            out[i] = dot(q, d_att, TN)


def grads_body(
    rows, place, q_ref, k_ref, v_ref, da_ref, own_ref, other_ref, qg_ref, kl_ref, vl_ref
):
    low = place[0]
    lower = causal(q_ref.shape[0], True)
    upper = causal(q_ref.shape[0], False)
    for i, j in enumerate(rows):
        for prior, part in ((own_ref, low), (other_ref, 1 - low)):
            here, there = at(2 * j + part), at(2 * i + part)
            q, k, v, d_att = q_ref[:, here], k_ref[:, here], v_ref[:, here], da_ref[:, there]
            cross = jnp.where(lower, dot(d_att, v, NT), 0.0)
            part_sum = two_pass(cross, k, NN) + two_pass_right(d_att, prior[i], NT)
            qg_ref[:, there] = part_sum.astype(BF16)
            cross = jnp.where(upper, dot(v, d_att, NT), 0.0)
            kl_ref[:, there] = two_pass(cross, q, NN)
            scores = jnp.where(upper, dot(k, q, NT), 0.0)
            vl_ref[:, there] = two_pass(scores, d_att, NN)


def final_body(place, k_ref, v_ref, *refs):
    low = place[0]
    kg_ref, vg_ref = refs[-2:]
    for g, rows in enumerate(GROUPS):
        kl_ref, vl_ref, own_ref, other_ref = refs[4 * g : 4 * g + 4]
        for i, j in enumerate(rows):
            for later, part in ((own_ref, low), (other_ref, 1 - low)):
                here, there = at(2 * j + part), at(2 * i + part)
                high, rest = halves(later[i])
                v, k = v_ref[:, here], k_ref[:, here]
                k_sum = kl_ref[:, there] + (dot(v, high, NT) + dot(v, rest, NT))
                kg_ref[:, here] = k_sum.astype(BF16)
                v_sum = vl_ref[:, there] + (dot(k, high, NN) + dot(k, rest, NN))
                vg_ref[:, here] = v_sum.astype(BF16)


def weight_body(place, nb_ref, g_ref, nbo_ref, go_ref, keep0, keep1, send0, send1):
    low, core = place[0], place[1]
    width = go_ref.shape[1] // 2
    mine = nb_ref[...]
    theirs = nbo_ref[...].astype(BF16)
    for c, keep, send in ((0, keep0, send0), (1, keep1, send1)):
        ours = g_ref[:, at(core * 2 + c, width)]
        other = go_ref[:, c * width : (c + 1) * width].astype(BF16)
        product = dot(mine, ours, TN) + dot(theirs, other, TN)
        for i in range(2):
            first = product[2 * i * HD : (2 * i + 1) * HD]
            second = product[(2 * i + 1) * HD : (2 * i + 2) * HD]
            keep[i] = jnp.where(low == 0, first, second)
            send[i] = jnp.where(low == 0, second, first)


def output_body(far_ref, near_ref, w_ref, out_ref):
    size = 2 * PAIR

    @pl.loop(0, out_ref.shape[1] // size)
    def _(c):
        total = dot(near_ref[...], w_ref[PAIR : 3 * PAIR, at(c, size)], NN)
        total += dot(far_ref[:, :PAIR], w_ref[:PAIR, at(c, size)], NN)
        total += dot(far_ref[:, PAIR:], w_ref[3 * PAIR :, at(c, size)], NN)
        out_ref[:, at(c, size)] = total.astype(BF16)


def exclusive(states, count, low, reverse, pins):
    swap = [(s, s ^ 1) for s in range(count)]
    sign = -2 if reverse else 2
    pairs = count // 2
    first = low == (1 if reverse else 0)

    def links(step):
        return [(s, s + sign * step) for s in range(count) if 0 <= s + sign * step < count]

    received = [lax.ppermute(send, "seq", swap) for _, send in states]
    total = [keep + got for (keep, _), got in zip(states, received)]
    outside = [None for _ in states]
    step = 1
    while step < pairs:
        pinned = pins.pop(0) if pins else ()
        for i in range(len(states)):
            total[i] = after(total[i], *pinned)
            got = lax.ppermute(total[i], "seq", links(step))
            outside[i] = got if step == 1 else outside[i] + got
            total[i] = total[i] + got
        step *= 2
    pinned = pins.pop(0) if pins else ()
    results = []
    for (keep, _), got, sums in zip(states, received, outside):
        mine = jnp.where(first, sums, sums + got)
        theirs = after(jnp.where(first, sums + keep, sums), *pinned)
        results.append((mine, lax.ppermute(theirs, "seq", swap)))
    return results


def per_device(queries, keys, values, out_weight, out_grad):
    count = lax.axis_size("seq")
    cores = lax.axis_size("dp")
    spot = lax.axis_index("seq")
    core = lax.axis_index("dp")
    low, level = spot % 2, spot // 2
    q, k, v, g = queries[0], keys[0], values[0], out_grad[0]
    length, features = q.shape
    width = g.shape[1]
    place = jnp.stack([low, core]).astype(jnp.int32)
    part = features // 2
    state = shape((2, HD, HD), F32)
    unit = 2 * H * length * HD

    flat = call(state_body, (state,) * 4, (place, k, v), unit * HD, "state")
    states = [(flat[0], flat[1]), (flat[2], flat[3])]

    fast = count == 8 and cores == 2
    half = width // 2
    swap = [(0, 1), (1, 0)]
    away = g
    if fast:
        away = lax.dynamic_slice_in_dim(g, (1 - core) * half, half, axis=1).astype(F32)
        go = lax.ppermute(away, "dp", swap)
    (att,) = call(local_body, (shape((length, features), F32),), (q, k, v), 3 * unit * length, "local")
    (d_normed,) = call(
        d_normed_body,
        (shape((length, features), F32),),
        (g, out_weight),
        2 * length * features * width,
        "d_normed",
    )
    priors = exclusive(states, count, low, False, [(away,), (att,), (d_normed,)])

    normed, d_atts, grad_states = [], [], []
    for rows, (own, other) in zip(GROUPS, priors):
        nb, nb32, da, keep, send = call(
            functools.partial(norm_body, rows),
            (
                shape((length, part), BF16),
                shape((length, part), F32),
                shape((length, part), BF16),
                state,
                state,
            ),
            (place, q, att, d_normed, own, other),
            2 * unit * HD,
            "norm",
        )
        normed.append((nb, nb32))
        d_atts.append(da)
        grad_states.append((keep, send))

    scale = 1.0 / math.sqrt(length * count * cores)
    if fast:
        block = shape((2, HD, half // 2), F32)
        chunks = []
        for nb, nb32 in normed:
            nbo = lax.ppermute(nb32, "dp", swap)
            out = call(
                weight_body, (block,) * 4, (place, nb, g, nbo, go), 2 * length * features * half, "weight"
            )
            chunks.append([(out[0], out[2]), (out[1], out[3])])
        ready = (chunks[1][0][1],)
        pins = [(chunks[0][0][1],), ready]
        weight_grad = scatter(chunks, level) * scale
    else:
        far, near = normed[0][0], normed[1][0]
        nb = jnp.concatenate([far[:, :PAIR], near, far[:, PAIR:]], axis=1)
        product = lax.dot_general(nb, g, TN, preferred_element_type=F32)
        product = lax.psum_scatter(product, "dp", scatter_dimension=1, tiled=True)
        weight_grad = lax.psum_scatter(product, "seq", scatter_dimension=0, tiled=True) * scale
        ready, pins = (), []

    laters = exclusive(grad_states, count, low, True, pins)

    pieces = []
    for rows, da, (own, other) in zip(GROUPS, d_atts, priors):
        pieces.append(
            call(
                functools.partial(grads_body, rows),
                (shape((length, part), BF16), shape((length, part), F32), shape((length, part), F32)),
                (place, q, k, v, after(da, *ready), own, other),
                5 * unit * length,
                "grads",
            )
        )
    (output,) = call(
        output_body,
        (shape((length, width), BF16),),
        (after(normed[0][0], *ready), normed[1][0], out_weight),
        2 * length * features * width,
        "output",
    )
    far, near = pieces[0][0], pieces[1][0]
    query_grad = jnp.concatenate([far[:, :PAIR], near, far[:, PAIR:]], axis=1)
    operands = [place, k, v]
    for piece, later in zip(pieces, laters):
        operands += [piece[1], piece[2], later[0], later[1]]
    key_grad, value_grad = call(
        final_body, (shape((length, features), BF16),) * 2, tuple(operands), 4 * unit * HD, "final"
    )
    return output[None], query_grad[None], key_grad[None], value_grad[None], weight_grad


def scatter(chunks, level):
    swap = [(s, s ^ 1) for s in range(8)]

    def on(links):
        return [(2 * a + i, 2 * b + i) for a, b in links for i in range(2)]

    inward = on([(0, 1), (3, 2)])
    middle = on([(1, 2), (2, 1)])
    outward = on([(2, 3), (1, 0)])
    lower = level < 2

    def paired(chunk, *pinned):
        keep, send = chunk
        base = keep + lax.ppermute(after(send, *pinned), "seq", swap)
        return jnp.where(lower, base[1], base[0]), jnp.where(lower, base[0], base[1])

    far0 = paired(chunks[0][0])
    far1 = paired(chunks[0][1])
    near0 = paired(chunks[1][0], far0[0])
    near1 = paired(chunks[1][1], far1[0])
    parts = []
    for far, near in ((far0, near0), (far1, near1)):
        up, down = far
        got = lax.ppermute(up, "seq", inward)
        got = lax.ppermute(up + got, "seq", middle)
        got = lax.ppermute(down + got, "seq", outward)
        outer_sum = down + got
        up, down = near
        got = lax.ppermute(up, "seq", inward)
        direct = lax.ppermute(down, "seq", inward)
        got = lax.ppermute(up + got, "seq", middle)
        inner_sum = (down + direct) + got
        outer = (level == 0) | (level == 3)
        parts.append(jnp.where(outer, outer_sum, inner_sum))
    return jnp.concatenate(parts, axis=1)


def solution(mesh):
    rows = P(("parts", "dp"), "seq", None)
    return jax.shard_map(
        per_device,
        mesh=mesh,
        in_specs=(rows, rows, rows, P(), rows),
        out_specs=(rows, rows, rows, rows, P(("parts", "seq"), "dp")),
        check_vma=False,
    )
```

```python
import functools
import math

import jax
import jax.numpy as jnp
from jax import lax
from jax.experimental import pallas as pl
from jax.experimental.pallas import tpu as pltpu
from jax.sharding import PartitionSpec as P

H = 8
HD = 128
PAIR = 2 * HD
PAIRS = H // 2
FAR = (0, 3)
NEAR = (1, 2)
WIDTHS = ((4, 4), (5, 3))
EPSILON = 1e-06
F32 = jnp.float32
BF16 = jnp.bfloat16
VMEM = pltpu.VMEM
VMEM_LIMIT = 16 << 20
COST = 16

NN = (((1,), (0,)), ((), ()))
NT = (((1,), (1,)), ((), ()))
TN = (((0,), (0,)), ((), ()))


def dot(a, b, dims):
    return lax.dot_general(a, b, dims, preferred_element_type=F32)


def halves(a):
    high = a.astype(BF16)
    return high, (a - high.astype(F32)).astype(BF16)


def two_pass(a, b, dims):
    high, low = halves(a)
    return dot(high, b, dims) + dot(low, b, dims)


def two_pass_right(a, b, dims):
    high, low = halves(b)
    return dot(a, high, dims) + dot(a, low, dims)


def causal(length, lower):
    rows = lax.broadcasted_iota(jnp.int32, (length, length), 0)
    cols = lax.broadcasted_iota(jnp.int32, (length, length), 1)
    return rows >= cols if lower else rows <= cols


def at(position, size=HD):
    if isinstance(position, int):
        return pl.ds(position * size, size)
    return pl.ds(pl.multiple_of(position * size, size), size)


def shape(dims, dtype):
    return jax.ShapeDtypeStruct(dims, dtype)


def call(body, out_shapes, operands, flops, name):
    specs = []
    for operand in operands:
        space = pltpu.SMEM if operand.dtype == jnp.int32 else VMEM
        specs.append(pl.BlockSpec(memory_space=space))
    return pl.pallas_call(
        body,
        out_shape=tuple(out_shapes),
        in_specs=specs,
        out_specs=tuple(pl.BlockSpec(memory_space=VMEM) for _ in out_shapes),
        compiler_params=pltpu.CompilerParams(vmem_limit_bytes=VMEM_LIMIT),
        cost_estimate=pl.CostEstimate(flops=flops // COST, bytes_accessed=0, transcendentals=0),
        name=name,
    )(*operands)


def after(value, *others):
    return lax.optimization_barrier((value, *others))[0]


def state_body(place, k_ref, v_ref, keep_ref, send_ref):
    low = place[0]
    for j in range(PAIRS):
        for out, head in ((send_ref, 2 * j + 1 - low), (keep_ref, 2 * j + low)):
            out[j] = dot(k_ref[:, at(head)], v_ref[:, at(head)], TN)


def away_body(place, g_ref, out_ref):
    half = out_ref.shape[1]
    out_ref[...] = g_ref[:, at(1 - place[1], half)].astype(F32)


def local_body(q_ref, k_ref, v_ref, out_ref):
    mask = causal(q_ref.shape[0], True)
    for h in range(H):
        scores = dot(q_ref[:, at(h)], k_ref[:, at(h)], NT)
        scores = jnp.where(mask, scores, 0.0)
        out_ref[:, at(h)] = two_pass(scores, v_ref[:, at(h)], NN)


def d_normed_body(g_ref, w_ref, out_ref):
    @pl.loop(0, PAIRS)
    def _(j):
        out_ref[:, at(j, PAIR)] = dot(g_ref[...], w_ref[at(j, PAIR), :], NT)


def norm_body(rows, place, q_ref, att_ref, dn_ref, own_ref, other_ref, *refs):
    low = place[0]
    nb_ref, nb32_ref, da_ref, keep_ref, send_ref = refs[-5:]
    whole = keep_ref.shape[0] == PAIRS
    if whole:
        for i, j in enumerate(FAR):
            keep_ref[j] = refs[0][i]
            send_ref[j] = refs[1][i]
    for i, j in enumerate(rows):
        for prior, out, part in ((own_ref, keep_ref, low), (other_ref, send_ref, 1 - low)):
            here, there = at(2 * j + part), at(2 * i + part)
            q = q_ref[:, here]
            attended = att_ref[:, here] + two_pass_right(q, prior[j], NN)
            inverse = lax.rsqrt(jnp.mean(attended * attended, axis=-1, keepdims=True) + EPSILON)
            normed = attended * inverse
            rounded = normed.astype(BF16)
            nb_ref[:, there] = rounded
            nb32_ref[:, there] = rounded.astype(F32)
            d_normed = dn_ref[:, here]
            mean = jnp.mean(d_normed * normed, axis=-1, keepdims=True)
            d_att = (inverse * (d_normed - normed * mean)).astype(BF16)
            da_ref[:, there] = d_att
            out[j if whole else i] = dot(q, d_att, TN)


def grads_body(
    place, q_ref, k_ref, v_ref, far_ref, near_ref, own_ref, other_ref, qg_ref, kl_ref, vl_ref
):
    low = place[0]
    lower = causal(q_ref.shape[0], True)
    upper = causal(q_ref.shape[0], False)
    for da_ref, rows in ((far_ref, FAR), (near_ref, NEAR)):
        for i, j in enumerate(rows):
            for prior, part in ((own_ref, low), (other_ref, 1 - low)):
                here, there = at(2 * j + part), at(2 * i + part)
                q, k, v, d_att = q_ref[:, here], k_ref[:, here], v_ref[:, here], da_ref[:, there]
                cross = jnp.where(lower, dot(d_att, v, NT), 0.0)
                part_sum = two_pass(cross, k, NN) + two_pass_right(d_att, prior[j], NT)
                qg_ref[:, here] = part_sum.astype(BF16)
                cross = jnp.where(upper, dot(v, d_att, NT), 0.0)
                kl_ref[:, here] = two_pass(cross, q, NN)
                scores = jnp.where(upper, dot(k, q, NT), 0.0)
                vl_ref[:, here] = two_pass(scores, d_att, NN)


def final_body(place, k_ref, v_ref, kl_ref, vl_ref, own_ref, other_ref, kg_ref, vg_ref):
    low = place[0]
    for j in range(PAIRS):
        for later, part in ((own_ref, low), (other_ref, 1 - low)):
            here = at(2 * j + part)
            high, rest = halves(later[j])
            v, k = v_ref[:, here], k_ref[:, here]
            kg_ref[:, here] = (kl_ref[:, here] + (dot(v, high, NT) + dot(v, rest, NT))).astype(BF16)
            vg_ref[:, here] = (vl_ref[:, here] + (dot(k, high, NN) + dot(k, rest, NN))).astype(BF16)


def weight_body(place, nb_ref, g_ref, nbo_ref, go_ref, *outs):
    low, core = place[0], place[1]
    half = go_ref.shape[1]
    mine = nb_ref[...]
    theirs = nbo_ref[...].astype(BF16)
    start = 0
    for keep, send in zip(outs[::2], outs[1::2]):
        width = keep.shape[2]
        ours = g_ref[:, pl.ds(pl.multiple_of(core * half + start, HD), width)]
        other = go_ref[:, start : start + width].astype(BF16)
        start += width
        product = dot(mine, ours, TN) + dot(theirs, other, TN)
        for i in range(2):
            first = product[2 * i * HD : (2 * i + 1) * HD]
            second = product[(2 * i + 1) * HD : (2 * i + 2) * HD]
            keep[i] = jnp.where(low == 0, first, second)
            send[i] = jnp.where(low == 0, second, first)


def output_body(far_ref, near_ref, w_ref, out_ref):
    size = 2 * PAIR

    @pl.loop(0, out_ref.shape[1] // size)
    def _(c):
        total = dot(near_ref[...], w_ref[PAIR : 3 * PAIR, at(c, size)], NN)
        total += dot(far_ref[:, :PAIR], w_ref[:PAIR, at(c, size)], NN)
        total += dot(far_ref[:, PAIR:], w_ref[3 * PAIR :, at(c, size)], NN)
        out_ref[:, at(c, size)] = total.astype(BF16)


def exclusive(keep, send, count, even, reverse, pins):
    swap = [(s, s ^ 1) for s in range(count)]
    sign = -2 if reverse else 2
    pairs = count // 2

    def first(here, there):
        return jnp.where(even, there, here) if reverse else jnp.where(even, here, there)

    def links(step):
        return [(s, s + sign * step) for s in range(count) if 0 <= s + sign * step < count]

    received = lax.ppermute(send, "seq", swap)
    total = keep + received
    outside = None
    step = 1
    while step < pairs:
        pinned = pins.pop(0) if pins else ()
        total = after(total, *pinned)
        got = lax.ppermute(total, "seq", links(step))
        outside = got if step == 1 else outside + got
        total = total + got
        step *= 2
    pinned = pins.pop(0) if pins else ()
    mine = first(outside, outside + received)
    theirs = after(first(outside + keep, outside), *pinned)
    return mine, lax.ppermute(theirs, "seq", swap)


def per_device(queries, keys, values, out_weight, out_grad):
    count = lax.axis_size("seq")
    cores = lax.axis_size("dp")
    spot = lax.axis_index("seq")
    core = lax.axis_index("dp")
    low, level = spot & 1, spot >> 1
    place = jnp.stack([low, core]).astype(jnp.int32)
    place, even, lower, outer = lax.optimization_barrier(
        (place, low == 0, level < 2, (level == 0) | (level == 3))
    )
    q, k, v, g = queries[0], keys[0], values[0], out_grad[0]
    length, features = q.shape
    width = g.shape[1]
    part = features // 2
    half = width // 2
    state = shape((PAIRS, HD, HD), F32)
    rows32 = shape((length, features), F32)
    rows16 = shape((length, features), BF16)
    unit = 2 * H * length * HD
    fast = count == 8 and cores == 2
    swap = [(0, 1), (1, 0)]

    keep, send = call(state_body, (state, state), (place, k, v), unit * HD, "state")
    away = g
    if fast:
        (away,) = call(away_body, (shape((length, half), F32),), (place, g), unit, "away")
        go = lax.ppermute(away, "dp", swap)
    (att,) = call(local_body, (rows32,), (q, k, v), 3 * unit * length, "local")
    (d_normed,) = call(d_normed_body, (rows32,), (g, out_weight), unit * width, "d_normed")
    own, other = exclusive(keep, send, count, even, False, [(away, att), (d_normed,)])

    pieces = (shape((length, part), BF16), shape((length, part), F32), shape((length, part), BF16))
    some = shape((2, HD, HD), F32)
    far, far32, far_att, *some_states = call(
        functools.partial(norm_body, FAR),
        pieces + (some, some),
        (place, q, att, d_normed, own, other),
        unit * HD,
        "norm_far",
    )
    near, near32, near_att, keep, send = call(
        functools.partial(norm_body, NEAR),
        pieces + (state, state),
        (place, q, att, d_normed, own, other, *some_states),
        unit * HD * 64,
        "norm_near",
    )

    scale = 1.0 / math.sqrt(length * count * cores)
    if fast:
        chunks = []
        for nb, nb32, widths in ((far, far32, WIDTHS[0]), (near, near32, WIDTHS[1])):
            nbo = lax.ppermute(nb32, "dp", swap)
            blocks = []
            for w in widths:
                block = shape((2, HD, w * half // sum(widths)), F32)
                blocks += [block, block]
            if chunks:
                nb = after(nb, chunks[0][1][1])
            out = call(weight_body, tuple(blocks), (place, nb, g, nbo, go), unit * half, "weight")
            chunks.append([(out[0], out[1]), (out[2], out[3])])
        ready = (chunks[1][0][1],)
        early = chunks[0][0][1]
        weight_grad, landed = scatter(chunks, lower, outer)
        weight_grad = weight_grad * scale
    else:
        nb = jnp.concatenate([far[:, :PAIR], near, far[:, PAIR:]], axis=1)
        product = lax.dot_general(nb, g, TN, preferred_element_type=F32)
        product = lax.psum_scatter(product, "dp", scatter_dimension=1, tiled=True)
        weight_grad = lax.psum_scatter(product, "seq", scatter_dimension=0, tiled=True) * scale
        ready, early, landed = (), near, near

    query_grad, key_local, value_local = call(
        grads_body,
        (rows16, rows32, rows32),
        (place, q, k, v, after(far_att, landed), near_att, own, other),
        9 * unit * length,
        "grads",
    )
    (output,) = call(
        output_body,
        (shape((length, width), BF16),),
        (after(far, *ready), near, out_weight),
        unit * width,
        "output",
    )
    pins = [(early,), (output,), (key_local,)]
    own_later, other_later = exclusive(keep, send, count, even, True, pins)

    key_grad, value_grad = call(
        final_body,
        (rows16, rows16),
        (place, k, v, key_local, value_local, own_later, other_later),
        4 * unit * HD,
        "final",
    )
    return output[None], query_grad[None], key_grad[None], value_grad[None], weight_grad


def scatter(chunks, lower, outer):
    swap = [(s, s ^ 1) for s in range(8)]

    def on(links):
        return [(2 * a + i, 2 * b + i) for a, b in links for i in range(2)]

    inward = on([(0, 1), (3, 2)])
    middle = on([(1, 2), (2, 1)])
    outward = on([(2, 3), (1, 0)])

    def paired(chunk, *pinned):
        keep, send = chunk
        base = keep + lax.ppermute(after(send, *pinned), "seq", swap)
        return jnp.where(lower, base[1], base[0]), jnp.where(lower, base[0], base[1])

    far, near, pins = [], [], []
    for chunk in chunks[0]:
        up, down = paired(chunk)
        pins.append(up)
        got = lax.ppermute(up, "seq", inward)
        got = lax.ppermute(up + got, "seq", middle)
        got = lax.ppermute(down + got, "seq", outward)
        far.append(down + got)
    for chunk, pin in zip(chunks[1], ((), pins[:1])):
        up, down = paired(chunk, *pin)
        got = lax.ppermute(up, "seq", inward)
        direct = lax.ppermute(down, "seq", inward)
        got = lax.ppermute(up + got, "seq", middle)
        near.append((down + direct) + got)
    total = jnp.where(outer, jnp.concatenate(far, axis=1), jnp.concatenate(near, axis=1))
    return total, pins[0]


def solution(mesh):
    rows = P(("parts", "dp"), "seq", None)
    return jax.shard_map(
        per_device,
        mesh=mesh,
        in_specs=(rows, rows, rows, P(), rows),
        out_specs=(rows, rows, rows, rows, P(("parts", "seq"), "dp")),
        check_vma=False,
    )
```

```python
import functools
import math

import jax
import jax.numpy as jnp
from jax import lax
from jax.experimental import pallas as pl
from jax.experimental.pallas import tpu as pltpu
from jax.sharding import PartitionSpec as P

H = 8
HD = 128
PAIR = 2 * HD
PAIRS = H // 2
FAR = (0, 3)
NEAR = (1, 2)
WIDTHS = ((4, 4), (5, 3))
EPSILON = 1e-06
F32 = jnp.float32
BF16 = jnp.bfloat16
VMEM = pltpu.VMEM
VMEM_LIMIT = 16 << 20
COST = 16

NN = (((1,), (0,)), ((), ()))
NT = (((1,), (1,)), ((), ()))
TN = (((0,), (0,)), ((), ()))


def dot(a, b, dims):
    return lax.dot_general(a, b, dims, preferred_element_type=F32)


def halves(a):
    high = a.astype(BF16)
    return high, (a - high.astype(F32)).astype(BF16)


def two_pass(a, b, dims):
    high, low = halves(a)
    return dot(high, b, dims) + dot(low, b, dims)


def two_pass_right(a, b, dims):
    high, low = halves(b)
    return dot(a, high, dims) + dot(a, low, dims)


def causal(length, lower):
    rows = lax.broadcasted_iota(jnp.int32, (length, length), 0)
    cols = lax.broadcasted_iota(jnp.int32, (length, length), 1)
    return rows >= cols if lower else rows <= cols


def at(position, size=HD):
    if isinstance(position, int):
        return pl.ds(position * size, size)
    return pl.ds(pl.multiple_of(position * size, size), size)


def shape(dims, dtype):
    return jax.ShapeDtypeStruct(dims, dtype)


def call(body, out_shapes, operands, flops, name):
    specs = []
    for operand in operands:
        space = pltpu.SMEM if operand.dtype == jnp.int32 else VMEM
        specs.append(pl.BlockSpec(memory_space=space))
    return pl.pallas_call(
        body,
        out_shape=tuple(out_shapes),
        in_specs=specs,
        out_specs=tuple(pl.BlockSpec(memory_space=VMEM) for _ in out_shapes),
        compiler_params=pltpu.CompilerParams(vmem_limit_bytes=VMEM_LIMIT),
        cost_estimate=pl.CostEstimate(flops=flops // COST, bytes_accessed=0, transcendentals=0),
        name=name,
    )(*operands)


def after(value, *others):
    return lax.optimization_barrier((value, *others))[0]


def state_body(place, k_ref, v_ref, *outs):
    low = place[0]
    for rows, keep_ref, send_ref in ((FAR, outs[0], outs[1]), (NEAR, outs[2], outs[3])):
        for i, j in enumerate(rows):
            for out, head in ((send_ref, 2 * j + 1 - low), (keep_ref, 2 * j + low)):
                out[i] = dot(k_ref[:, at(head)], v_ref[:, at(head)], TN)


def away_body(place, g_ref, out_ref):
    half = out_ref.shape[1]
    out_ref[...] = g_ref[:, at(1 - place[1], half)].astype(F32)


def local_body(q_ref, k_ref, v_ref, out_ref):
    mask = causal(q_ref.shape[0], True)
    for h in range(H):
        scores = dot(q_ref[:, at(h)], k_ref[:, at(h)], NT)
        scores = jnp.where(mask, scores, 0.0)
        out_ref[:, at(h)] = two_pass(scores, v_ref[:, at(h)], NN)


def d_normed_body(g_ref, w_ref, out_ref):
    @pl.loop(0, PAIRS)
    def _(j):
        out_ref[:, at(j, PAIR)] = dot(g_ref[...], w_ref[at(j, PAIR), :], NT)


def norm_body(rows, place, q_ref, att_ref, dn_ref, own_ref, other_ref, *refs):
    low = place[0]
    nb_ref, nb32_ref, da_ref, keep_ref, send_ref = refs[-5:]
    whole = keep_ref.shape[0] == PAIRS
    if whole:
        for i, j in enumerate(FAR):
            keep_ref[j] = refs[0][i]
            send_ref[j] = refs[1][i]
    for i, j in enumerate(rows):
        for prior, out, part in ((own_ref, keep_ref, low), (other_ref, send_ref, 1 - low)):
            here, there = at(2 * j + part), at(2 * i + part)
            q = q_ref[:, here]
            attended = att_ref[:, here] + two_pass_right(q, prior[i], NN)
            inverse = lax.rsqrt(jnp.mean(attended * attended, axis=-1, keepdims=True) + EPSILON)
            normed = attended * inverse
            rounded = normed.astype(BF16)
            nb_ref[:, there] = rounded
            nb32_ref[:, there] = rounded.astype(F32)
            d_normed = dn_ref[:, here]
            mean = jnp.mean(d_normed * normed, axis=-1, keepdims=True)
            d_att = (inverse * (d_normed - normed * mean)).astype(BF16)
            da_ref[:, there] = d_att
            out[j if whole else i] = dot(q, d_att, TN)


def grads_body(place, q_ref, k_ref, v_ref, *refs):
    low = place[0]
    qg_ref, kl_ref, vl_ref = refs[-3:]
    lower = causal(q_ref.shape[0], True)
    upper = causal(q_ref.shape[0], False)
    for rows, (da_ref, own_ref, other_ref) in ((FAR, refs[:3]), (NEAR, refs[3:6])):
        for i, j in enumerate(rows):
            for prior, part in ((own_ref, low), (other_ref, 1 - low)):
                here, there = at(2 * j + part), at(2 * i + part)
                q, k, v, d_att = q_ref[:, here], k_ref[:, here], v_ref[:, here], da_ref[:, there]
                cross = jnp.where(lower, dot(d_att, v, NT), 0.0)
                part_sum = two_pass(cross, k, NN) + two_pass_right(d_att, prior[i], NT)
                qg_ref[:, here] = part_sum.astype(BF16)
                cross = jnp.where(upper, dot(v, d_att, NT), 0.0)
                kl_ref[:, here] = two_pass(cross, q, NN)
                scores = jnp.where(upper, dot(k, q, NT), 0.0)
                vl_ref[:, here] = two_pass(scores, d_att, NN)


def final_body(place, k_ref, v_ref, kl_ref, vl_ref, own_ref, other_ref, kg_ref, vg_ref):
    low = place[0]
    for j in range(PAIRS):
        for later, part in ((own_ref, low), (other_ref, 1 - low)):
            here = at(2 * j + part)
            high, rest = halves(later[j])
            v, k = v_ref[:, here], k_ref[:, here]
            kg_ref[:, here] = (kl_ref[:, here] + (dot(v, high, NT) + dot(v, rest, NT))).astype(BF16)
            vg_ref[:, here] = (vl_ref[:, here] + (dot(k, high, NN) + dot(k, rest, NN))).astype(BF16)


def weight_body(place, nb_ref, g_ref, nbo_ref, go_ref, *outs):
    low, core = place[0], place[1]
    half = go_ref.shape[1]
    mine = nb_ref[...]
    theirs = nbo_ref[...].astype(BF16)
    start = 0
    for keep, send in zip(outs[::2], outs[1::2]):
        width = keep.shape[2]
        ours = g_ref[:, pl.ds(pl.multiple_of(core * half + start, HD), width)]
        other = go_ref[:, start : start + width].astype(BF16)
        start += width
        product = dot(mine, ours, TN) + dot(theirs, other, TN)
        for i in range(2):
            first = product[2 * i * HD : (2 * i + 1) * HD]
            second = product[(2 * i + 1) * HD : (2 * i + 2) * HD]
            keep[i] = jnp.where(low == 0, first, second)
            send[i] = jnp.where(low == 0, second, first)


def output_body(far_ref, near_ref, w_ref, out_ref):
    size = 2 * PAIR

    @pl.loop(0, out_ref.shape[1] // size)
    def _(c):
        total = dot(near_ref[...], w_ref[PAIR : 3 * PAIR, at(c, size)], NN)
        total += dot(far_ref[:, :PAIR], w_ref[:PAIR, at(c, size)], NN)
        total += dot(far_ref[:, PAIR:], w_ref[3 * PAIR :, at(c, size)], NN)
        out_ref[:, at(c, size)] = total.astype(BF16)


def exclusive(states, count, even, reverse, pins):
    swap = [(s, s ^ 1) for s in range(count)]
    sign = -2 if reverse else 2
    pairs = count // 2

    def first(here, there):
        return jnp.where(even, there, here) if reverse else jnp.where(even, here, there)

    def links(step):
        return [(s, s + sign * step) for s in range(count) if 0 <= s + sign * step < count]

    received = [got for _, got in states]
    totals = [keep + got for keep, got in states]
    sums = [None for _ in states]
    trail = ()
    step = 1
    while step < pairs:
        pinned = (*trail, *(pins.pop(0) if pins else ()))
        for i, total in enumerate(totals):
            total = after(total, *pinned)
            pinned = (total,)
            trail = (total,) if i else ()
            got = lax.ppermute(total, "seq", links(step))
            sums[i] = got if step == 1 else sums[i] + got
            totals[i] = total + got
        step *= 2
    pinned = (*trail, *(pins.pop(0) if pins else ()))
    results = []
    for (keep, _), got, before in zip(states, received, sums):
        mine = first(before, before + got)
        theirs = after(first(before + keep, before), *pinned)
        pinned = ()
        results.append((mine, lax.ppermute(theirs, "seq", swap)))
    return results


def per_device(queries, keys, values, out_weight, out_grad):
    count = lax.axis_size("seq")
    cores = lax.axis_size("dp")
    spot = lax.axis_index("seq")
    core = lax.axis_index("dp")
    low, level = spot & 1, spot >> 1
    place = jnp.stack([low, core]).astype(jnp.int32)
    place, even, lower, outer, odd = lax.optimization_barrier(
        (place, low == 0, level < 2, (level == 0) | (level == 3), (level & 1) == 1)
    )
    q, k, v, g = queries[0], keys[0], values[0], out_grad[0]
    length, features = q.shape
    width = g.shape[1]
    part = features // 2
    half = width // 2
    state = shape((PAIRS, HD, HD), F32)
    some = shape((2, HD, HD), F32)
    rows32 = shape((length, features), F32)
    rows16 = shape((length, features), BF16)
    unit = 2 * H * length * HD
    fast = count == 8 and cores == 2
    swap = [(0, 1), (1, 0)]

    def trade(send):
        return lax.ppermute(send, "seq", [(s, s ^ 1) for s in range(count)])

    states = call(state_body, (some,) * 4, (place, k, v), unit * HD, "state")
    away = g
    if fast:
        (away,) = call(away_body, (shape((length, half), F32),), (place, after(g, states[0])), unit, "away")
        go = lax.ppermute(away, "dp", swap)
    (att,) = call(local_body, (rows32,), (q, k, v), 3 * unit * length, "local")
    (d_normed,) = call(d_normed_body, (rows32,), (g, out_weight), unit * width, "d_normed")
    far_prior, near_prior = exclusive(
        [(states[0], trade(states[1])), (states[2], trade(states[3]))], count, even, False, [(away,), (att,), (d_normed,)]
    )

    pieces = (shape((length, part), BF16), shape((length, part), F32), shape((length, part), BF16))
    far, far32, far_att, *some_states = call(
        functools.partial(norm_body, FAR),
        pieces + (some, some),
        (place, q, att, d_normed, after(far_prior[0], near_prior[0]), far_prior[1]),
        unit * HD,
        "norm_far",
    )

    def product(nb, nbo, widths):
        blocks = []
        for w in widths:
            block = shape((2, HD, w * half // sum(widths)), F32)
            blocks += [block, block]
        out = call(weight_body, tuple(blocks), (place, nb, g, nbo, go), unit * half, "weight")
        return list(zip(out[::2], out[1::2]))

    near_own, near_other = near_prior
    if fast:
        chunks = product(far, lax.ppermute(far32, "dp", swap), WIDTHS[0])
        near_own = after(near_own, chunks[0][1])
        landed = chunks[0][0] + trade(after(chunks[0][1], near_other))
    near, near32, near_att, keep, send = call(
        functools.partial(norm_body, NEAR),
        pieces + (state, state),
        (place, q, att, d_normed, near_own, near_other, *some_states),
        unit * HD * 64,
        "norm_near",
    )

    scale = 1.0 / math.sqrt(length * count * cores)
    received = trade(send)
    if fast:
        others = [(kept, trade(after(sent, landed))) for kept, sent in chunks[1:]]
        lines = [toward(landed, lower, odd)]
        nbo = lax.ppermute(after(near32, landed, received), "dp", swap)
        chunks = product(after(near, lines[0][0]), nbo, WIDTHS[1])
        ready = chunks[0][1]
        near_bases = [kept + trade(sent) for kept, sent in chunks]
        lines += [toward(kept + after(got, ready), lower, odd) for kept, got in others]
        weight_grad = scatter(lines, near_bases, lower, outer) * scale
    else:
        nb = jnp.concatenate([far[:, :PAIR], near, far[:, PAIR:]], axis=1)
        weight = lax.dot_general(nb, g, TN, preferred_element_type=F32)
        weight = lax.psum_scatter(weight, "dp", scatter_dimension=1, tiled=True)
        weight_grad = lax.psum_scatter(weight, "seq", scatter_dimension=0, tiled=True) * scale
        ready = near

    query_grad, key_local, value_local = call(
        grads_body,
        (rows16, rows32, rows32),
        (place, q, k, v, after(far_att, ready), *far_prior, near_att, *near_prior),
        9 * unit * length,
        "grads",
    )
    (output,) = call(
        output_body,
        (shape((length, width), BF16),),
        (after(far, ready), near, out_weight),
        unit * width,
        "output",
    )
    ((own_later, other_later),) = exclusive(
        [(keep, received)], count, even, True, [(), (output,), (key_local,)]
    )

    key_grad, value_grad = call(
        final_body,
        (rows16, rows16),
        (place, k, v, key_local, value_local, own_later, other_later),
        4 * unit * HD,
        "final",
    )
    return output[None], query_grad[None], key_grad[None], value_grad[None], weight_grad


def along(links):
    return [(2 * a + i, 2 * b + i) for a, b in links for i in range(2)]


def toward(base, lower, odd):
    out = jnp.where(odd, base[0], base[1])
    got = lax.ppermute(out, "seq", along([(0, 1), (1, 0), (2, 3), (3, 2)]))
    return jnp.where(lower, base[1], base[0]) + got, jnp.where(lower, base[0], base[1]) + got


def scatter(lines, near_bases, lower, outer):
    far, near = [], []
    for half, rest in lines:
        pin = half
        far.append(rest + lax.ppermute(half, "seq", along([(1, 3), (2, 0)])))
    for base in near_bases:
        base = after(base, pin)
        got = lax.ppermute(base, "seq", along([(0, 1), (3, 2)]))
        pin = jnp.where(lower, base[1] + got[1], base[0] + got[0])
        final = lax.ppermute(pin, "seq", along([(1, 2), (2, 1)]))
        near.append(jnp.where(lower, base[0] + got[0], base[1] + got[1]) + final)
    return jnp.where(outer, jnp.concatenate(far, axis=1), jnp.concatenate(near, axis=1))


def solution(mesh):
    rows = P(("parts", "dp"), "seq", None)
    return jax.shard_map(
        per_device,
        mesh=mesh,
        in_specs=(rows, rows, rows, P(), rows),
        out_specs=(rows, rows, rows, rows, P(("parts", "seq"), "dp")),
        check_vma=False,
    )
```

```python
import functools
import math

import jax
import jax.numpy as jnp
from jax import lax
from jax.experimental import pallas as pl
from jax.experimental.pallas import tpu as pltpu
from jax.sharding import PartitionSpec as P

H = 8
HD = 128
PAIR = 2 * HD
PAIRS = H // 2
FAR = (0, 3)
NEAR = (1, 2)
WIDTHS = ((4, 4), (5, 3))
EPSILON = 1e-06
F32 = jnp.float32
BF16 = jnp.bfloat16
VMEM = pltpu.VMEM
VMEM_LIMIT = 16 << 20
COST = 16

NN = (((1,), (0,)), ((), ()))
NT = (((1,), (1,)), ((), ()))
TN = (((0,), (0,)), ((), ()))


def dot(a, b, dims):
    return lax.dot_general(a, b, dims, preferred_element_type=F32)


def halves(a):
    high = a.astype(BF16)
    return high, (a - high.astype(F32)).astype(BF16)


def two_pass(a, b, dims):
    high, low = halves(a)
    return dot(high, b, dims) + dot(low, b, dims)


def two_pass_right(a, b, dims):
    high, low = halves(b)
    return dot(a, high, dims) + dot(a, low, dims)


def causal(length, lower):
    rows = lax.broadcasted_iota(jnp.int32, (length, length), 0)
    cols = lax.broadcasted_iota(jnp.int32, (length, length), 1)
    return rows >= cols if lower else rows <= cols


def at(position, size=HD):
    if isinstance(position, int):
        return pl.ds(position * size, size)
    return pl.ds(pl.multiple_of(position * size, size), size)


def shape(dims, dtype):
    return jax.ShapeDtypeStruct(dims, dtype)


def call(body, out_shapes, operands, flops, name):
    specs = []
    for operand in operands:
        space = pltpu.SMEM if operand.dtype == jnp.int32 else VMEM
        specs.append(pl.BlockSpec(memory_space=space))
    return pl.pallas_call(
        body,
        out_shape=tuple(out_shapes),
        in_specs=specs,
        out_specs=tuple(pl.BlockSpec(memory_space=VMEM) for _ in out_shapes),
        compiler_params=pltpu.CompilerParams(vmem_limit_bytes=VMEM_LIMIT),
        cost_estimate=pl.CostEstimate(flops=flops // COST, bytes_accessed=0, transcendentals=0),
        name=name,
    )(*operands)


def after(value, *others):
    return lax.optimization_barrier((value, *others))[0]


def state_body(place, k_ref, v_ref, *outs):
    low = place[0]
    for rows, keep_ref, send_ref in ((FAR, outs[0], outs[1]), (NEAR, outs[2], outs[3])):
        for i, j in enumerate(rows):
            for out, head in ((send_ref, 2 * j + 1 - low), (keep_ref, 2 * j + low)):
                out[i] = dot(k_ref[:, at(head)], v_ref[:, at(head)], TN)


def away_body(place, g_ref, out_ref):
    half = out_ref.shape[1]
    out_ref[...] = g_ref[:, at(1 - place[1], half)].astype(F32)


def local_body(q_ref, k_ref, v_ref, out_ref):
    mask = causal(q_ref.shape[0], True)
    for h in range(H):
        scores = dot(q_ref[:, at(h)], k_ref[:, at(h)], NT)
        scores = jnp.where(mask, scores, 0.0)
        out_ref[:, at(h)] = two_pass(scores, v_ref[:, at(h)], NN)


def d_normed_body(g_ref, w_ref, out_ref):
    @pl.loop(0, PAIRS)
    def _(j):
        out_ref[:, at(j, PAIR)] = dot(g_ref[...], w_ref[at(j, PAIR), :], NT)


def norm_body(rows, place, q_ref, att_ref, dn_ref, own_ref, other_ref, *refs):
    low = place[0]
    nb_ref, nb32_ref, da_ref, keep_ref, send_ref = refs[-5:]
    whole = keep_ref.shape[0] == PAIRS
    if whole:
        for i, j in enumerate(FAR):
            keep_ref[j] = refs[0][i]
            send_ref[j] = refs[1][i]
    for i, j in enumerate(rows):
        for prior, out, part in ((own_ref, keep_ref, low), (other_ref, send_ref, 1 - low)):
            here, there = at(2 * j + part), at(2 * i + part)
            q = q_ref[:, here]
            attended = att_ref[:, here] + two_pass_right(q, prior[i], NN)
            inverse = lax.rsqrt(jnp.mean(attended * attended, axis=-1, keepdims=True) + EPSILON)
            normed = attended * inverse
            rounded = normed.astype(BF16)
            nb_ref[:, there] = rounded
            nb32_ref[:, there] = rounded.astype(F32)
            d_normed = dn_ref[:, here]
            mean = jnp.mean(d_normed * normed, axis=-1, keepdims=True)
            d_att = (inverse * (d_normed - normed * mean)).astype(BF16)
            da_ref[:, there] = d_att
            out[j if whole else i] = dot(q, d_att, TN)


def grads_body(place, q_ref, k_ref, v_ref, *refs):
    low = place[0]
    qg_ref, kl_ref, vl_ref = refs[-3:]
    lower = causal(q_ref.shape[0], True)
    upper = causal(q_ref.shape[0], False)
    for rows, (da_ref, own_ref, other_ref) in ((FAR, refs[:3]), (NEAR, refs[3:6])):
        for i, j in enumerate(rows):
            for prior, part in ((own_ref, low), (other_ref, 1 - low)):
                here, there = at(2 * j + part), at(2 * i + part)
                q, k, v, d_att = q_ref[:, here], k_ref[:, here], v_ref[:, here], da_ref[:, there]
                cross = jnp.where(lower, dot(d_att, v, NT), 0.0)
                part_sum = two_pass(cross, k, NN) + two_pass_right(d_att, prior[i], NT)
                qg_ref[:, here] = part_sum.astype(BF16)
                cross = jnp.where(upper, dot(v, d_att, NT), 0.0)
                kl_ref[:, here] = two_pass(cross, q, NN)
                scores = jnp.where(upper, dot(k, q, NT), 0.0)
                vl_ref[:, here] = two_pass(scores, d_att, NN)


def final_body(place, k_ref, v_ref, kl_ref, vl_ref, own_ref, other_ref, kg_ref, vg_ref):
    low = place[0]
    for j in range(PAIRS):
        for later, part in ((own_ref, low), (other_ref, 1 - low)):
            here = at(2 * j + part)
            high, rest = halves(later[j])
            v, k = v_ref[:, here], k_ref[:, here]
            kg_ref[:, here] = (kl_ref[:, here] + (dot(v, high, NT) + dot(v, rest, NT))).astype(BF16)
            vg_ref[:, here] = (vl_ref[:, here] + (dot(k, high, NN) + dot(k, rest, NN))).astype(BF16)


def weight_body(place, nb_ref, g_ref, nbo_ref, go_ref, *outs):
    low, core = place[0], place[1]
    half = go_ref.shape[1]
    mine = nb_ref[...]
    theirs = nbo_ref[...].astype(BF16)
    start = 0
    for keep, send in zip(outs[::2], outs[1::2]):
        width = keep.shape[2]
        ours = g_ref[:, pl.ds(pl.multiple_of(core * half + start, HD), width)]
        other = go_ref[:, start : start + width].astype(BF16)
        start += width
        product = dot(mine, ours, TN) + dot(theirs, other, TN)
        for i in range(2):
            first = product[2 * i * HD : (2 * i + 1) * HD]
            second = product[(2 * i + 1) * HD : (2 * i + 2) * HD]
            keep[i] = jnp.where(low == 0, first, second)
            send[i] = jnp.where(low == 0, second, first)


def output_body(far_ref, near_ref, w_ref, out_ref):
    size = 2 * PAIR

    @pl.loop(0, out_ref.shape[1] // size)
    def _(c):
        total = dot(near_ref[...], w_ref[PAIR : 3 * PAIR, at(c, size)], NN)
        total += dot(far_ref[:, :PAIR], w_ref[:PAIR, at(c, size)], NN)
        total += dot(far_ref[:, PAIR:], w_ref[3 * PAIR :, at(c, size)], NN)
        out_ref[:, at(c, size)] = total.astype(BF16)


def exclusive(states, count, even, reverse, pins):
    swap = [(s, s ^ 1) for s in range(count)]
    sign = -2 if reverse else 2
    pairs = count // 2

    def first(here, there):
        return jnp.where(even, there, here) if reverse else jnp.where(even, here, there)

    def links(step):
        return [(s, s + sign * step) for s in range(count) if 0 <= s + sign * step < count]

    received = [got for _, got in states]
    totals = [keep + got for keep, got in states]
    sums = [None for _ in states]
    trail = ()
    step = 1
    while step < pairs:
        pinned = (*trail, *(pins.pop(0) if pins else ()))
        for i, total in enumerate(totals):
            total = after(total, *pinned)
            pinned = (total,)
            trail = (total,) if i else ()
            got = lax.ppermute(total, "seq", links(step))
            sums[i] = got if step == 1 else sums[i] + got
            totals[i] = total + got
        step *= 2
    pinned = (*trail, *(pins.pop(0) if pins else ()))
    results = []
    for (keep, _), got, before in zip(states, received, sums):
        mine = first(before, before + got)
        theirs = after(first(before + keep, before), *pinned)
        pinned = ()
        results.append((mine, lax.ppermute(theirs, "seq", swap)))
    return results


def per_device(queries, keys, values, out_weight, out_grad):
    count = lax.axis_size("seq")
    cores = lax.axis_size("dp")
    spot = lax.axis_index("seq")
    core = lax.axis_index("dp")
    low, level = spot & 1, spot >> 1
    place = jnp.stack([low, core]).astype(jnp.int32)
    place, even, lower, outer, odd = lax.optimization_barrier(
        (place, low == 0, level < 2, (level == 0) | (level == 3), (level & 1) == 1)
    )
    q, k, v, g = queries[0], keys[0], values[0], out_grad[0]
    length, features = q.shape
    width = g.shape[1]
    part = features // 2
    half = width // 2
    state = shape((PAIRS, HD, HD), F32)
    some = shape((2, HD, HD), F32)
    rows32 = shape((length, features), F32)
    rows16 = shape((length, features), BF16)
    unit = 2 * H * length * HD
    fast = count == 8 and cores == 2
    swap = [(0, 1), (1, 0)]

    def trade(send):
        return lax.ppermute(send, "seq", [(s, s ^ 1) for s in range(count)])

    states = call(state_body, (some,) * 4, (place, k, v), unit * HD, "state")
    away = g
    if fast:
        (away,) = call(away_body, (shape((length, half), F32),), (place, after(g, states[0])), unit, "away")
        go = lax.ppermute(away, "dp", swap)
    (att,) = call(local_body, (rows32,), (q, k, v), 3 * unit * length, "local")
    (d_normed,) = call(d_normed_body, (rows32,), (g, out_weight), unit * width, "d_normed")
    far_prior, near_prior = exclusive(
        [(states[0], trade(states[1])), (states[2], trade(states[3]))], count, even, False, [(away,), (att,), (d_normed,)]
    )

    pieces = (shape((length, part), BF16), shape((length, part), F32), shape((length, part), BF16))
    far, far32, far_att, *some_states = call(
        functools.partial(norm_body, FAR),
        pieces + (some, some),
        (place, q, att, d_normed, after(far_prior[0], near_prior[0]), far_prior[1]),
        unit * HD,
        "norm_far",
    )

    def product(nb, nbo, widths):
        blocks = []
        for w in widths:
            block = shape((2, HD, w * half // sum(widths)), F32)
            blocks += [block, block]
        out = call(weight_body, tuple(blocks), (place, nb, g, nbo, go), unit * half, "weight")
        return list(zip(out[::2], out[1::2]))

    near_own, near_other = near_prior
    if fast:
        chunks = product(far, lax.ppermute(far32, "dp", swap), WIDTHS[0])
        near_own = after(near_own, chunks[0][1])
        first_got = trade(after(chunks[0][1], near_other))
    near, near32, near_att, keep, send = call(
        functools.partial(norm_body, NEAR),
        pieces + (state, state),
        (place, q, att, d_normed, near_own, near_other, *some_states),
        unit * HD * 64,
        "norm_near",
    )

    query_grad, key_local, value_local = call(
        grads_body,
        (rows16, rows32, rows32),
        (place, q, k, v, far_att, *far_prior, near_att, *near_prior),
        9 * unit * length,
        "grads",
    )
    received = trade(send)
    if fast:
        landed = chunks[0][0] + after(first_got, key_local)
        others = [(kept, trade(after(sent, landed))) for kept, sent in chunks[1:]]
        lines = [toward(landed, lower, odd)]
        nbo = lax.ppermute(after(near32, landed), "dp", swap)
    (output,) = call(
        output_body,
        (shape((length, width), BF16),),
        (after(far, key_local), near, out_weight),
        unit * width,
        "output",
    )
    scale = 1.0 / math.sqrt(length * count * cores)
    if fast:
        chunks = product(after(near, output), nbo, WIDTHS[1])
        ready = chunks[0][1]
        near_bases = [kept + trade(sent) for kept, sent in chunks]
        kept, got = others[0]
        base = after(kept + after(got, ready), lines[0][0])
        lines.append(toward(base, lower, odd))
        weight_grad = scatter(lines, near_bases, base, lower, outer) * scale
        pins = [(lines[0][0],), (ready,)]
    else:
        nb = jnp.concatenate([far[:, :PAIR], near, far[:, PAIR:]], axis=1)
        weight = lax.dot_general(nb, g, TN, preferred_element_type=F32)
        weight = lax.psum_scatter(weight, "dp", scatter_dimension=1, tiled=True)
        weight_grad = lax.psum_scatter(weight, "seq", scatter_dimension=0, tiled=True) * scale
        pins = []
    ((own_later, other_later),) = exclusive([(keep, received)], count, even, True, pins)
    key_grad, value_grad = call(
        final_body,
        (rows16, rows16),
        (place, k, v, key_local, value_local, own_later, other_later),
        4 * unit * HD,
        "final",
    )
    return output[None], query_grad[None], key_grad[None], value_grad[None], weight_grad


def along(links):
    return [(2 * a + i, 2 * b + i) for a, b in links for i in range(2)]


def toward(base, lower, odd):
    out = jnp.where(odd, base[0], base[1])
    got = lax.ppermute(out, "seq", along([(0, 1), (1, 0), (2, 3), (3, 2)]))
    return jnp.where(lower, base[1], base[0]) + got, jnp.where(lower, base[0], base[1]) + got


def scatter(lines, near_bases, landed, lower, outer):
    far = [rest + lax.ppermute(half, "seq", along([(1, 3), (2, 0)])) for half, rest in lines]
    near = []
    pins = [(landed,), (lines[1][0],)]
    for i, base in enumerate(near_bases):
        base = after(base, *pins[i])
        got = lax.ppermute(base, "seq", along([(0, 1), (3, 2)]))
        across = jnp.where(lower, base[1] + got[1], base[0] + got[0])
        pins[-1] = (*pins[-1], across)
        across = after(across, *near_bases[i + 1 :])
        final = lax.ppermute(across, "seq", along([(1, 2), (2, 1)]))
        near.append(jnp.where(lower, base[0] + got[0], base[1] + got[1]) + final)
    return jnp.where(outer, jnp.concatenate(far, axis=1), jnp.concatenate(near, axis=1))


def solution(mesh):
    rows = P(("parts", "dp"), "seq", None)
    return jax.shard_map(
        per_device,
        mesh=mesh,
        in_specs=(rows, rows, rows, P(), rows),
        out_specs=(rows, rows, rows, rows, P(("parts", "seq"), "dp")),
        check_vma=False,
    )
```

```python
import functools
import math

import jax
import jax.numpy as jnp
from jax import lax
from jax.experimental import pallas as pl
from jax.experimental.pallas import tpu as pltpu
from jax.sharding import PartitionSpec as P

H = 8
HD = 128
PAIR = 2 * HD
PAIRS = H // 2
FAR = (0, 3)
NEAR = (1, 2)
WIDTHS = ((4, 4), (5, 3))
EPSILON = 1e-06
F32 = jnp.float32
BF16 = jnp.bfloat16
VMEM = pltpu.VMEM
VMEM_LIMIT = 16 << 20
COST = 16

NN = (((1,), (0,)), ((), ()))
NT = (((1,), (1,)), ((), ()))
TN = (((0,), (0,)), ((), ()))


def dot(a, b, dims):
    return lax.dot_general(a, b, dims, preferred_element_type=F32)


def halves(a):
    high = a.astype(BF16)
    return high, (a - high.astype(F32)).astype(BF16)


def two_pass(a, b, dims):
    high, low = halves(a)
    return dot(high, b, dims) + dot(low, b, dims)


def two_pass_right(a, b, dims):
    high, low = halves(b)
    return dot(a, high, dims) + dot(a, low, dims)


def causal(length, lower):
    rows = lax.broadcasted_iota(jnp.int32, (length, length), 0)
    cols = lax.broadcasted_iota(jnp.int32, (length, length), 1)
    return rows >= cols if lower else rows <= cols


def at(position, size=HD):
    if isinstance(position, int):
        return pl.ds(position * size, size)
    return pl.ds(pl.multiple_of(position * size, size), size)


def shape(dims, dtype):
    return jax.ShapeDtypeStruct(dims, dtype)


def call(body, out_shapes, operands, flops, name):
    specs = []
    for operand in operands:
        space = pltpu.SMEM if operand.dtype == jnp.int32 else VMEM
        specs.append(pl.BlockSpec(memory_space=space))
    return pl.pallas_call(
        body,
        out_shape=tuple(out_shapes),
        in_specs=specs,
        out_specs=tuple(pl.BlockSpec(memory_space=VMEM) for _ in out_shapes),
        compiler_params=pltpu.CompilerParams(vmem_limit_bytes=VMEM_LIMIT),
        cost_estimate=pl.CostEstimate(flops=flops // COST, bytes_accessed=0, transcendentals=0),
        name=name,
    )(*operands)


def after(value, *others):
    return lax.optimization_barrier((value, *others))[0]


def state_body(place, k_ref, v_ref, *outs):
    low = place[0]
    for rows, keep_ref, send_ref in ((FAR, outs[0], outs[1]), (NEAR, outs[2], outs[3])):
        for i, j in enumerate(rows):
            for out, head in ((send_ref, 2 * j + 1 - low), (keep_ref, 2 * j + low)):
                out[i] = dot(k_ref[:, at(head)], v_ref[:, at(head)], TN)


def away_body(place, g_ref, out_ref):
    half = out_ref.shape[1]
    out_ref[...] = g_ref[:, at(1 - place[1], half)].astype(F32)


def local_body(q_ref, k_ref, v_ref, out_ref):
    mask = causal(q_ref.shape[0], True)
    for h in range(H):
        scores = dot(q_ref[:, at(h)], k_ref[:, at(h)], NT)
        scores = jnp.where(mask, scores, 0.0)
        out_ref[:, at(h)] = two_pass(scores, v_ref[:, at(h)], NN)


def d_normed_body(g_ref, w_ref, out_ref):
    @pl.loop(0, PAIRS)
    def _(j):
        out_ref[:, at(j, PAIR)] = dot(g_ref[...], w_ref[at(j, PAIR), :], NT)


def norm_body(rows, place, q_ref, att_ref, dn_ref, own_ref, other_ref, *refs):
    low = place[0]
    nb_ref, nb32_ref, da_ref, keep_ref, send_ref = refs[-5:]
    whole = keep_ref.shape[0] == PAIRS
    if whole:
        for i, j in enumerate(FAR):
            keep_ref[j] = refs[0][i]
            send_ref[j] = refs[1][i]
    for i, j in enumerate(rows):
        for prior, out, part in ((own_ref, keep_ref, low), (other_ref, send_ref, 1 - low)):
            here, there = at(2 * j + part), at(2 * i + part)
            q = q_ref[:, here]
            attended = att_ref[:, here] + two_pass_right(q, prior[i], NN)
            inverse = lax.rsqrt(jnp.mean(attended * attended, axis=-1, keepdims=True) + EPSILON)
            normed = attended * inverse
            rounded = normed.astype(BF16)
            nb_ref[:, there] = rounded
            nb32_ref[:, there] = rounded.astype(F32)
            d_normed = dn_ref[:, here]
            mean = jnp.mean(d_normed * normed, axis=-1, keepdims=True)
            d_att = (inverse * (d_normed - normed * mean)).astype(BF16)
            da_ref[:, there] = d_att
            out[j if whole else i] = dot(q, d_att, TN)


def grads_body(place, q_ref, k_ref, v_ref, *refs):
    low = place[0]
    qg_ref, kl_ref, vl_ref = refs[-3:]
    lower = causal(q_ref.shape[0], True)
    upper = causal(q_ref.shape[0], False)
    for rows, (da_ref, own_ref, other_ref) in ((FAR, refs[:3]), (NEAR, refs[3:6])):
        for i, j in enumerate(rows):
            for prior, part in ((own_ref, low), (other_ref, 1 - low)):
                here, there = at(2 * j + part), at(2 * i + part)
                q, k, v, d_att = q_ref[:, here], k_ref[:, here], v_ref[:, here], da_ref[:, there]
                cross = jnp.where(lower, dot(d_att, v, NT), 0.0)
                part_sum = two_pass(cross, k, NN) + two_pass_right(d_att, prior[i], NT)
                qg_ref[:, here] = part_sum.astype(BF16)
                cross = jnp.where(upper, dot(v, d_att, NT), 0.0)
                kl_ref[:, here] = two_pass(cross, q, NN)
                scores = jnp.where(upper, dot(k, q, NT), 0.0)
                vl_ref[:, here] = two_pass(scores, d_att, NN)


def final_body(place, k_ref, v_ref, kl_ref, vl_ref, own_ref, other_ref, kg_ref, vg_ref):
    low = place[0]
    for j in range(PAIRS):
        for later, part in ((own_ref, low), (other_ref, 1 - low)):
            here = at(2 * j + part)
            high, rest = halves(later[j])
            v, k = v_ref[:, here], k_ref[:, here]
            kg_ref[:, here] = (kl_ref[:, here] + (dot(v, high, NT) + dot(v, rest, NT))).astype(BF16)
            vg_ref[:, here] = (vl_ref[:, here] + (dot(k, high, NN) + dot(k, rest, NN))).astype(BF16)


def weight_body(place, nb_ref, g_ref, nbo_ref, go_ref, *outs):
    low, core = place[0], place[1]
    half = go_ref.shape[1]
    mine = nb_ref[...]
    theirs = nbo_ref[...].astype(BF16)
    start = 0
    for keep, send in zip(outs[::2], outs[1::2]):
        width = keep.shape[2]
        ours = g_ref[:, pl.ds(pl.multiple_of(core * half + start, HD), width)]
        other = go_ref[:, start : start + width].astype(BF16)
        start += width
        product = dot(mine, ours, TN) + dot(theirs, other, TN)
        for i in range(2):
            first = product[2 * i * HD : (2 * i + 1) * HD]
            second = product[(2 * i + 1) * HD : (2 * i + 2) * HD]
            keep[i] = jnp.where(low == 0, first, second)
            send[i] = jnp.where(low == 0, second, first)


def output_body(far_ref, near_ref, w_ref, out_ref):
    size = 2 * PAIR

    @pl.loop(0, out_ref.shape[1] // size)
    def _(c):
        total = dot(near_ref[...], w_ref[PAIR : 3 * PAIR, at(c, size)], NN)
        total += dot(far_ref[:, :PAIR], w_ref[:PAIR, at(c, size)], NN)
        total += dot(far_ref[:, PAIR:], w_ref[3 * PAIR :, at(c, size)], NN)
        out_ref[:, at(c, size)] = total.astype(BF16)


def exclusive(states, count, even, reverse, pins, marks):
    swap = [(s, s ^ 1) for s in range(count)]
    sign = -2 if reverse else 2
    pairs = count // 2

    def first(here, there):
        return jnp.where(even, there, here) if reverse else jnp.where(even, here, there)

    def links(step):
        return [(s, s + sign * step) for s in range(count) if 0 <= s + sign * step < count]

    received = [got for _, got in states]
    totals = [keep + got for keep, got in states]
    sums = [None for _ in states]
    trail = ()
    step = 1
    while step < pairs:
        pinned = (*trail, *(pins.pop(0) if pins else ()))
        for i, total in enumerate(totals):
            total = after(total, *pinned)
            pinned = (total,)
            trail = (total,) if i else ()
            marks.append(total)
            got = lax.ppermute(total, "seq", links(step))
            sums[i] = got if step == 1 else sums[i] + got
            totals[i] = total + got
        step *= 2
    pinned = (*trail, *(pins.pop(0) if pins else ()))
    results = []
    for (keep, _), got, before in zip(states, received, sums):
        mine = first(before, before + got)
        theirs = after(first(before + keep, before), *pinned)
        pinned = ()
        results.append((mine, lax.ppermute(theirs, "seq", swap)))
    return results


def per_device(queries, keys, values, out_weight, out_grad):
    count = lax.axis_size("seq")
    cores = lax.axis_size("dp")
    spot = lax.axis_index("seq")
    core = lax.axis_index("dp")
    low, level = spot & 1, spot >> 1
    place = jnp.stack([low, core]).astype(jnp.int32)
    place, even, lower, outer, odd = lax.optimization_barrier(
        (place, low == 0, level < 2, (level == 0) | (level == 3), (level & 1) == 1)
    )
    q, k, v, g = queries[0], keys[0], values[0], out_grad[0]
    length, features = q.shape
    width = g.shape[1]
    part = features // 2
    half = width // 2
    state = shape((PAIRS, HD, HD), F32)
    some = shape((2, HD, HD), F32)
    rows32 = shape((length, features), F32)
    rows16 = shape((length, features), BF16)
    unit = 2 * H * length * HD
    fast = count == 8 and cores == 2
    swap = [(0, 1), (1, 0)]

    def trade(send):
        return lax.ppermute(send, "seq", [(s, s ^ 1) for s in range(count)])

    states = call(state_body, (some,) * 4, (place, k, v), unit * HD, "state")
    away = g
    if fast:
        (away,) = call(away_body, (shape((length, half), F32),), (place, after(g, states[0])), unit, "away")
        go = lax.ppermute(away, "dp", swap)
    (att,) = call(local_body, (rows32,), (q, k, v), 3 * unit * length, "local")
    (d_normed,) = call(d_normed_body, (rows32,), (g, out_weight), unit * width, "d_normed")
    far_prior, near_prior = exclusive(
        [(states[0], trade(states[1])), (states[2], trade(states[3]))], count, even, False, [(away,), (att,), (d_normed,)], []
    )

    pieces = (shape((length, part), BF16), shape((length, part), F32), shape((length, part), BF16))
    far, far32, far_att, *some_states = call(
        functools.partial(norm_body, FAR),
        pieces + (some, some),
        (place, q, att, d_normed, after(far_prior[0], near_prior[0]), far_prior[1]),
        unit * HD,
        "norm_far",
    )

    def product(nb, nbo, widths):
        blocks = []
        for w in widths:
            block = shape((2, HD, w * half // sum(widths)), F32)
            blocks += [block, block]
        out = call(weight_body, tuple(blocks), (place, nb, g, nbo, go), unit * half, "weight")
        return list(zip(out[::2], out[1::2]))

    near_own, near_other = near_prior
    if fast:
        chunks = product(far, lax.ppermute(far32, "dp", swap), WIDTHS[0])
        near_own = after(near_own, chunks[0][1])
        first_got = trade(after(chunks[0][1], near_other))
    near, near32, near_att, keep, send = call(
        functools.partial(norm_body, NEAR),
        pieces + (state, state),
        (place, q, att, d_normed, near_own, near_other, *some_states),
        unit * HD * 64,
        "norm_near",
    )

    query_grad, key_local, value_local = call(
        grads_body,
        (rows16, rows32, rows32),
        (place, q, k, v, far_att, *far_prior, near_att, *near_prior),
        9 * unit * length,
        "grads",
    )
    received = trade(send)
    if fast:
        landed = chunks[0][0] + after(first_got, key_local)
        others = [(kept, trade(after(sent, landed))) for kept, sent in chunks[1:]]
        lines = [toward(landed, lower, odd)]
        nbo = lax.ppermute(after(near32, landed), "dp", swap)
    scale = 1.0 / math.sqrt(length * count * cores)
    if fast:
        chunks = product(near, nbo, WIDTHS[1])
        ready = chunks[0][1]
        kept, got = others[0]
        base = after(kept + after(got, ready), lines[0][0])
        lines.append(toward(base, lower, odd))
        near_gots = [trade(sent) for _, sent in chunks]
        hops = [(lines[0][0],), (ready, base), near_gots[1:]]
    else:
        nb = jnp.concatenate([far[:, :PAIR], near, far[:, PAIR:]], axis=1)
        weight = lax.dot_general(nb, g, TN, preferred_element_type=F32)
        weight = lax.psum_scatter(weight, "dp", scatter_dimension=1, tiled=True)
        weight_grad = lax.psum_scatter(weight, "seq", scatter_dimension=0, tiled=True) * scale
        hops, ready = [], far
    (output,) = call(
        output_body,
        (shape((length, width), BF16),),
        (after(far, ready), near, out_weight),
        unit * width,
        "output",
    )
    hops[:1] = [(*hops[0], output)] if fast else []
    marks = []
    ((own_later, other_later),) = exclusive([(keep, received)], count, even, True, hops, marks)
    if fast:
        (first_keep, _), (last_keep, _) = chunks
        near_bases = [first_keep + after(near_gots[0], *marks[1:]), last_keep + near_gots[1]]
        weight_grad = scatter(lines, near_bases, base, lower, outer) * scale
    key_grad, value_grad = call(
        final_body,
        (rows16, rows16),
        (place, k, v, key_local, value_local, own_later, other_later),
        4 * unit * HD,
        "final",
    )
    return output[None], query_grad[None], key_grad[None], value_grad[None], weight_grad


def along(links):
    return [(2 * a + i, 2 * b + i) for a, b in links for i in range(2)]


def toward(base, lower, odd):
    out = jnp.where(odd, base[0], base[1])
    got = lax.ppermute(out, "seq", along([(0, 1), (1, 0), (2, 3), (3, 2)]))
    return jnp.where(lower, base[1], base[0]) + got, jnp.where(lower, base[0], base[1]) + got


def scatter(lines, near_bases, landed, lower, outer):
    far = []
    for (half, rest), pin in zip(lines, ((), near_bases[1:])):
        far.append(rest + lax.ppermute(after(half, *pin), "seq", along([(1, 3), (2, 0)])))
    near = []
    pins = [(landed,), (lines[1][0],)]
    for i, base in enumerate(near_bases):
        base = after(base, *pins[i])
        got = lax.ppermute(base, "seq", along([(0, 1), (3, 2)]))
        across = jnp.where(lower, base[1] + got[1], base[0] + got[0])
        pins[-1] = (*pins[-1], across)
        across = after(across, *near_bases[i + 1 :])
        final = lax.ppermute(across, "seq", along([(1, 2), (2, 1)]))
        near.append(jnp.where(lower, base[0] + got[0], base[1] + got[1]) + final)
    return jnp.where(outer, jnp.concatenate(far, axis=1), jnp.concatenate(near, axis=1))


def solution(mesh):
    rows = P(("parts", "dp"), "seq", None)
    return jax.shard_map(
        per_device,
        mesh=mesh,
        in_specs=(rows, rows, rows, P(), rows),
        out_specs=(rows, rows, rows, rows, P(("parts", "seq"), "dp")),
        check_vma=False,
    )
```

```python
import functools
import math

import jax
import jax.numpy as jnp
from jax import lax
from jax.experimental import pallas as pl
from jax.experimental.pallas import tpu as pltpu
from jax.sharding import PartitionSpec as P

H = 8
HD = 128
PAIR = 2 * HD
PAIRS = H // 2
FAR = (0, 3)
NEAR = (1, 2)
WIDTHS = ((4, 4), (5, 3))
EPSILON = 1e-06
F32 = jnp.float32
BF16 = jnp.bfloat16
VMEM = pltpu.VMEM
VMEM_LIMIT = 16 << 20
COST = 16

NN = (((1,), (0,)), ((), ()))
NT = (((1,), (1,)), ((), ()))
TN = (((0,), (0,)), ((), ()))


def dot(a, b, dims):
    return lax.dot_general(a, b, dims, preferred_element_type=F32)


def halves(a):
    high = a.astype(BF16)
    return high, (a - high.astype(F32)).astype(BF16)


def two_pass(a, b, dims):
    high, low = halves(a)
    return dot(high, b, dims) + dot(low, b, dims)


def two_pass_right(a, b, dims):
    high, low = halves(b)
    return dot(a, high, dims) + dot(a, low, dims)


def causal(length, lower):
    rows = lax.broadcasted_iota(jnp.int32, (length, length), 0)
    cols = lax.broadcasted_iota(jnp.int32, (length, length), 1)
    return rows >= cols if lower else rows <= cols


def at(position, size=HD):
    if isinstance(position, int):
        return pl.ds(position * size, size)
    return pl.ds(pl.multiple_of(position * size, size), size)


def shape(dims, dtype):
    return jax.ShapeDtypeStruct(dims, dtype)


def call(body, out_shapes, operands, flops, name):
    specs = []
    for operand in operands:
        space = pltpu.SMEM if operand.dtype == jnp.int32 else VMEM
        specs.append(pl.BlockSpec(memory_space=space))
    return pl.pallas_call(
        body,
        out_shape=tuple(out_shapes),
        in_specs=specs,
        out_specs=tuple(pl.BlockSpec(memory_space=VMEM) for _ in out_shapes),
        compiler_params=pltpu.CompilerParams(vmem_limit_bytes=VMEM_LIMIT),
        cost_estimate=pl.CostEstimate(flops=flops // COST, bytes_accessed=0, transcendentals=0),
        name=name,
    )(*operands)


def after(value, *others):
    return lax.optimization_barrier((value, *others))[0]


def state_body(place, k_ref, v_ref, *outs):
    low = place[0]
    for rows, keep_ref, send_ref in ((FAR, outs[0], outs[1]), (NEAR, outs[2], outs[3])):
        for i, j in enumerate(rows):
            for out, head in ((send_ref, 2 * j + 1 - low), (keep_ref, 2 * j + low)):
                out[i] = dot(k_ref[:, at(head)], v_ref[:, at(head)], TN)


def away_body(place, g_ref, out_ref):
    half = out_ref.shape[1]
    out_ref[...] = g_ref[:, at(1 - place[1], half)].astype(F32)


def local_body(q_ref, k_ref, v_ref, out_ref):
    mask = causal(q_ref.shape[0], True)
    for h in range(H):
        scores = dot(q_ref[:, at(h)], k_ref[:, at(h)], NT)
        scores = jnp.where(mask, scores, 0.0)
        out_ref[:, at(h)] = two_pass(scores, v_ref[:, at(h)], NN)


def d_normed_body(g_ref, w_ref, out_ref):
    @pl.loop(0, PAIRS)
    def _(j):
        out_ref[:, at(j, PAIR)] = dot(g_ref[...], w_ref[at(j, PAIR), :], NT)


def norm_body(rows, place, q_ref, att_ref, dn_ref, own_ref, other_ref, *refs):
    low = place[0]
    nb_ref, nb32_ref, da_ref, keep_ref, send_ref = refs[-5:]
    whole = keep_ref.shape[0] == PAIRS
    if whole:
        for i, j in enumerate(FAR):
            keep_ref[j] = refs[0][i]
            send_ref[j] = refs[1][i]
    for i, j in enumerate(rows):
        for prior, out, part in ((own_ref, keep_ref, low), (other_ref, send_ref, 1 - low)):
            here, there = at(2 * j + part), at(2 * i + part)
            q = q_ref[:, here]
            attended = att_ref[:, here] + two_pass_right(q, prior[i], NN)
            inverse = lax.rsqrt(jnp.mean(attended * attended, axis=-1, keepdims=True) + EPSILON)
            normed = attended * inverse
            rounded = normed.astype(BF16)
            nb_ref[:, there] = rounded
            nb32_ref[:, there] = rounded.astype(F32)
            d_normed = dn_ref[:, here]
            mean = jnp.mean(d_normed * normed, axis=-1, keepdims=True)
            d_att = (inverse * (d_normed - normed * mean)).astype(BF16)
            da_ref[:, there] = d_att
            out[j if whole else i] = dot(q, d_att, TN)


def grads_body(place, q_ref, k_ref, v_ref, *refs):
    low = place[0]
    qg_ref, kl_ref, vl_ref = refs[-3:]
    lower = causal(q_ref.shape[0], True)
    upper = causal(q_ref.shape[0], False)
    for rows, (da_ref, own_ref, other_ref) in ((FAR, refs[:3]), (NEAR, refs[3:6])):
        for i, j in enumerate(rows):
            for prior, part in ((own_ref, low), (other_ref, 1 - low)):
                here, there = at(2 * j + part), at(2 * i + part)
                q, k, v, d_att = q_ref[:, here], k_ref[:, here], v_ref[:, here], da_ref[:, there]
                cross = jnp.where(lower, dot(d_att, v, NT), 0.0)
                part_sum = two_pass(cross, k, NN) + two_pass_right(d_att, prior[i], NT)
                qg_ref[:, here] = part_sum.astype(BF16)
                cross = jnp.where(upper, dot(v, d_att, NT), 0.0)
                kl_ref[:, here] = two_pass(cross, q, NN)
                scores = jnp.where(upper, dot(k, q, NT), 0.0)
                vl_ref[:, here] = two_pass(scores, d_att, NN)


def final_body(place, k_ref, v_ref, kl_ref, vl_ref, own_ref, other_ref, kg_ref, vg_ref):
    low = place[0]
    for j in range(PAIRS):
        for later, part in ((own_ref, low), (other_ref, 1 - low)):
            here = at(2 * j + part)
            high, rest = halves(later[j])
            v, k = v_ref[:, here], k_ref[:, here]
            kg_ref[:, here] = (kl_ref[:, here] + (dot(v, high, NT) + dot(v, rest, NT))).astype(BF16)
            vg_ref[:, here] = (vl_ref[:, here] + (dot(k, high, NN) + dot(k, rest, NN))).astype(BF16)


def weight_body(place, nb_ref, g_ref, nbo_ref, go_ref, *outs):
    low, core = place[0], place[1]
    half = go_ref.shape[1]
    mine = nb_ref[...]
    theirs = nbo_ref[...].astype(BF16)
    start = 0
    for keep, send in zip(outs[::2], outs[1::2]):
        width = keep.shape[2]
        ours = g_ref[:, pl.ds(pl.multiple_of(core * half + start, HD), width)]
        other = go_ref[:, start : start + width].astype(BF16)
        start += width
        product = dot(mine, ours, TN) + dot(theirs, other, TN)
        for i in range(2):
            first = product[2 * i * HD : (2 * i + 1) * HD]
            second = product[(2 * i + 1) * HD : (2 * i + 2) * HD]
            keep[i] = jnp.where(low == 0, first, second)
            send[i] = jnp.where(low == 0, second, first)


def output_body(far_ref, near_ref, w_ref, out_ref):
    size = 2 * PAIR

    @pl.loop(0, out_ref.shape[1] // size)
    def _(c):
        total = dot(near_ref[...], w_ref[PAIR : 3 * PAIR, at(c, size)], NN)
        total += dot(far_ref[:, :PAIR], w_ref[:PAIR, at(c, size)], NN)
        total += dot(far_ref[:, PAIR:], w_ref[3 * PAIR :, at(c, size)], NN)
        out_ref[:, at(c, size)] = total.astype(BF16)


def exclusive(states, count, even, reverse, pins):
    swap = [(s, s ^ 1) for s in range(count)]
    sign = -2 if reverse else 2
    pairs = count // 2

    def first(here, there):
        return jnp.where(even, there, here) if reverse else jnp.where(even, here, there)

    def links(step):
        return [(s, s + sign * step) for s in range(count) if 0 <= s + sign * step < count]

    received = [got for _, got in states]
    totals = [keep + got for keep, got in states]
    sums = [None for _ in states]
    trail = ()
    step = 1
    while step < pairs:
        pinned = (*trail, *(pins.pop(0) if pins else ()))
        for i, total in enumerate(totals):
            total = after(total, *pinned)
            pinned = (total,)
            trail = (total,) if i else ()
            got = lax.ppermute(total, "seq", links(step))
            sums[i] = got if step == 1 else sums[i] + got
            totals[i] = total + got
        step *= 2
    pinned = (*trail, *(pins.pop(0) if pins else ()))
    results = []
    for (keep, _), got, before in zip(states, received, sums):
        mine = first(before, before + got)
        theirs = after(first(before + keep, before), *pinned)
        pinned = ()
        results.append((mine, lax.ppermute(theirs, "seq", swap)))
    return results


def per_device(queries, keys, values, out_weight, out_grad):
    count = lax.axis_size("seq")
    cores = lax.axis_size("dp")
    spot = lax.axis_index("seq")
    core = lax.axis_index("dp")
    low, level = spot & 1, spot >> 1
    place = jnp.stack([low, core]).astype(jnp.int32)
    place, even, lower, outer, odd = lax.optimization_barrier(
        (place, low == 0, level < 2, (level == 0) | (level == 3), (level & 1) == 1)
    )
    q, k, v, g = queries[0], keys[0], values[0], out_grad[0]
    length, features = q.shape
    width = g.shape[1]
    part = features // 2
    half = width // 2
    state = shape((PAIRS, HD, HD), F32)
    some = shape((2, HD, HD), F32)
    rows32 = shape((length, features), F32)
    rows16 = shape((length, features), BF16)
    unit = 2 * H * length * HD
    fast = count == 8 and cores == 2
    swap = [(0, 1), (1, 0)]

    def trade(send):
        return lax.ppermute(send, "seq", [(s, s ^ 1) for s in range(count)])

    states = call(state_body, (some,) * 4, (place, k, v), unit * HD, "state")
    away = g
    if fast:
        (away,) = call(away_body, (shape((length, half), F32),), (place, after(g, states[0])), unit, "away")
        go = lax.ppermute(away, "dp", swap)
    (att,) = call(local_body, (rows32,), (q, k, v), 3 * unit * length, "local")
    (d_normed,) = call(d_normed_body, (rows32,), (g, out_weight), unit * width, "d_normed")
    far_prior, near_prior = exclusive(
        [(states[0], trade(states[1])), (states[2], trade(states[3]))], count, even, False, [(away,), (att,), (d_normed,)]
    )

    pieces = (shape((length, part), BF16), shape((length, part), F32), shape((length, part), BF16))
    far, far32, far_att, *some_states = call(
        functools.partial(norm_body, FAR),
        pieces + (some, some),
        (place, q, att, d_normed, after(far_prior[0], near_prior[0]), far_prior[1]),
        unit * HD,
        "norm_far",
    )

    def product(nb, nbo, widths):
        blocks = []
        for w in widths:
            block = shape((2, HD, w * half // sum(widths)), F32)
            blocks += [block, block]
        out = call(weight_body, tuple(blocks), (place, nb, g, nbo, go), unit * half, "weight")
        return list(zip(out[::2], out[1::2]))

    near_own, near_other = near_prior
    if fast:
        chunks = product(far, lax.ppermute(far32, "dp", swap), WIDTHS[0])
        near_own = after(near_own, chunks[0][1])
        far0_got = trade(after(chunks[0][1], near_other))
    near, near32, near_att, keep, send = call(
        functools.partial(norm_body, NEAR),
        pieces + (state, state),
        (place, q, att, d_normed, near_own, near_other, *some_states),
        unit * HD * 64,
        "norm_near",
    )

    received = trade(send)
    ready = ()
    if fast:
        nbo = lax.ppermute(near32, "dp", swap)
        (near0_keep, near0_send), (near1_keep, near1_send) = product(near, nbo, WIDTHS[1])
        ready = (near0_send,)
    query_grad, key_local, value_local = call(
        grads_body,
        (rows16, rows32, rows32),
        (place, q, k, v, after(far_att, *ready), *far_prior, near_att, *near_prior),
        9 * unit * length,
        "grads",
    )

    def finish(own, other):
        return call(
            final_body,
            (rows16, rows16),
            (place, k, v, key_local, value_local, own, other),
            4 * unit * HD,
            "final",
        )

    def project(rows):
        return call(
            output_body,
            (shape((length, width), BF16),),
            (rows, near, out_weight),
            unit * width,
            "output",
        )[0]

    scale = 1.0 / math.sqrt(length * count * cores)
    if not fast:
        nb = jnp.concatenate([far[:, :PAIR], near, far[:, PAIR:]], axis=1)
        weight = lax.dot_general(nb, g, TN, preferred_element_type=F32)
        weight = lax.psum_scatter(weight, "dp", scatter_dimension=1, tiled=True)
        weight_grad = lax.psum_scatter(weight, "seq", scatter_dimension=0, tiled=True) * scale
        output = project(far)
        ((own, other),) = exclusive([(keep, received)], count, even, True, [])
        key_grad, value_grad = finish(own, other)
        return output[None], query_grad[None], key_grad[None], value_grad[None], weight_grad

    (far0_keep, _), (far1_keep, far1_send) = chunks
    far0 = far0_keep + after(far0_got, key_local)
    far0_in = hop(jnp.where(odd, far0[0], far0[1]), NEXT)
    far1_got = trade(after(far1_send, far0))
    near0_got, near1_got = trade(near0_send), trade(near1_send)

    total = keep + after(received, far0)
    back1 = hop(total, BACK)
    output = project(after(far, total))
    far0_in = after(far0_in, output)
    far0_half = jnp.where(lower, far0[1], far0[0]) + far0_in
    far0_end = hop(far0_half, OUTWARD)
    back1 = after(back1, far0_half)
    total = total + back1
    back2 = hop(total, BACK2)
    near0 = near0_keep + after(near0_got, total)
    near0_in = hop(near0, INWARD)
    far1 = far1_keep + after(far1_got, near0)
    far1_out = jnp.where(odd, far1[0], far1[1])
    far1_in = hop(far1_out, NEXT)
    near0_in = after(near0_in, far1_out)
    near0_half = jnp.where(lower, near0[1] + near0_in[1], near0[0] + near0_in[0])
    near0_end = hop(near0_half, ACROSS)
    outside = back1 + after(back2, near0_half)
    theirs = jnp.where(even, outside, outside + keep)
    other = trade(theirs)
    own = jnp.where(even, outside + received, outside)
    near1 = near1_keep + after(near1_got, theirs)
    near1_in = hop(near1, INWARD)
    far1_in = after(far1_in, near1)
    far1_half = jnp.where(lower, far1[1], far1[0]) + far1_in
    far1_end = hop(far1_half, OUTWARD)
    key_grad, value_grad = finish(own, after(other, far1_half))
    near1_in = after(near1_in, key_grad, near0_end)
    near1_half = jnp.where(lower, near1[1] + near1_in[1], near1[0] + near1_in[0])
    near1_end = hop(near1_half, ACROSS)

    far_parts = [
        (jnp.where(lower, base[0], base[1]) + got) + end
        for base, got, end in ((far0, far0_in, far0_end), (far1, far1_in, far1_end))
    ]
    near_parts = [
        jnp.where(lower, base[0] + got[0], base[1] + got[1]) + end
        for base, got, end in ((near0, near0_in, near0_end), (near1, near1_in, near1_end))
    ]
    weight_grad = jnp.where(
        outer, jnp.concatenate(far_parts, axis=1), jnp.concatenate(near_parts, axis=1)
    )
    return output[None], query_grad[None], key_grad[None], value_grad[None], weight_grad * scale


NEXT = ((0, 1), (1, 0), (2, 3), (3, 2))
OUTWARD = ((1, 3), (2, 0))
INWARD = ((0, 1), (3, 2))
ACROSS = ((1, 2), (2, 1))
BACK = ((1, 0), (2, 1), (3, 2))
BACK2 = ((2, 0), (3, 1))


def hop(block, links):
    return lax.ppermute(block, "seq", [(2 * a + i, 2 * b + i) for a, b in links for i in range(2)])


def solution(mesh):
    rows = P(("parts", "dp"), "seq", None)
    return jax.shard_map(
        per_device,
        mesh=mesh,
        in_specs=(rows, rows, rows, P(), rows),
        out_specs=(rows, rows, rows, rows, P(("parts", "seq"), "dp")),
        check_vma=False,
    )
```

```python
import functools
import math

import jax
import jax.numpy as jnp
from jax import lax
from jax.experimental import pallas as pl
from jax.experimental.pallas import tpu as pltpu
from jax.sharding import PartitionSpec as P

H = 8
HD = 128
PAIR = 2 * HD
PAIRS = H // 2
FAR = (0, 3)
NEAR = (1, 2)
WIDTHS = ((4, 4), (5, 3))
EPSILON = 1e-06
F32 = jnp.float32
BF16 = jnp.bfloat16
VMEM = pltpu.VMEM
VMEM_LIMIT = 16 << 20
COST = 16

NN = (((1,), (0,)), ((), ()))
NT = (((1,), (1,)), ((), ()))
TN = (((0,), (0,)), ((), ()))


def dot(a, b, dims):
    return lax.dot_general(a, b, dims, preferred_element_type=F32)


def halves(a):
    high = a.astype(BF16)
    return high, (a - high.astype(F32)).astype(BF16)


def two_pass(a, b, dims):
    high, low = halves(a)
    return dot(high, b, dims) + dot(low, b, dims)


def two_pass_right(a, b, dims):
    high, low = halves(b)
    return dot(a, high, dims) + dot(a, low, dims)


def causal(length, lower):
    rows = lax.broadcasted_iota(jnp.int32, (length, length), 0)
    cols = lax.broadcasted_iota(jnp.int32, (length, length), 1)
    return rows >= cols if lower else rows <= cols


def at(position, size=HD):
    if isinstance(position, int):
        return pl.ds(position * size, size)
    return pl.ds(pl.multiple_of(position * size, size), size)


def shape(dims, dtype):
    return jax.ShapeDtypeStruct(dims, dtype)


def call(body, out_shapes, operands, flops, name):
    specs = []
    for operand in operands:
        space = pltpu.SMEM if operand.dtype == jnp.int32 else VMEM
        specs.append(pl.BlockSpec(memory_space=space))
    return pl.pallas_call(
        body,
        out_shape=tuple(out_shapes),
        in_specs=specs,
        out_specs=tuple(pl.BlockSpec(memory_space=VMEM) for _ in out_shapes),
        compiler_params=pltpu.CompilerParams(vmem_limit_bytes=VMEM_LIMIT),
        cost_estimate=pl.CostEstimate(flops=flops // COST, bytes_accessed=0, transcendentals=0),
        name=name,
    )(*operands)


def after(value, *others):
    return lax.optimization_barrier((value, *others))[0]


def state_body(place, k_ref, v_ref, *outs):
    low = place[0]
    for rows, keep_ref, send_ref in ((FAR, outs[0], outs[1]), (NEAR, outs[2], outs[3])):
        for i, j in enumerate(rows):
            for out, head in ((send_ref, 2 * j + 1 - low), (keep_ref, 2 * j + low)):
                out[i] = dot(k_ref[:, at(head)], v_ref[:, at(head)], TN)


def away_body(place, g_ref, out_ref):
    half = out_ref.shape[1]
    out_ref[...] = g_ref[:, at(1 - place[1], half)].astype(F32)


def local_body(q_ref, k_ref, v_ref, out_ref):
    mask = causal(q_ref.shape[0], True)
    for h in range(H):
        scores = dot(q_ref[:, at(h)], k_ref[:, at(h)], NT)
        scores = jnp.where(mask, scores, 0.0)
        out_ref[:, at(h)] = two_pass(scores, v_ref[:, at(h)], NN)


def d_normed_body(g_ref, w_ref, out_ref):
    @pl.loop(0, PAIRS)
    def _(j):
        out_ref[:, at(j, PAIR)] = dot(g_ref[...], w_ref[at(j, PAIR), :], NT)


def norm_body(rows, place, q_ref, att_ref, dn_ref, own_ref, other_ref, *refs):
    low = place[0]
    nb_ref, nb32_ref, da_ref, keep_ref, send_ref = refs[-5:]
    whole = keep_ref.shape[0] == PAIRS
    if whole:
        for i, j in enumerate(FAR):
            keep_ref[j] = refs[0][i]
            send_ref[j] = refs[1][i]
    for i, j in enumerate(rows):
        for prior, out, part in ((own_ref, keep_ref, low), (other_ref, send_ref, 1 - low)):
            here, there = at(2 * j + part), at(2 * i + part)
            q = q_ref[:, here]
            attended = att_ref[:, here] + two_pass_right(q, prior[i], NN)
            inverse = lax.rsqrt(jnp.mean(attended * attended, axis=-1, keepdims=True) + EPSILON)
            normed = attended * inverse
            rounded = normed.astype(BF16)
            nb_ref[:, there] = rounded
            nb32_ref[:, there] = rounded.astype(F32)
            d_normed = dn_ref[:, here]
            mean = jnp.mean(d_normed * normed, axis=-1, keepdims=True)
            d_att = (inverse * (d_normed - normed * mean)).astype(BF16)
            da_ref[:, there] = d_att
            out[j if whole else i] = dot(q, d_att, TN)


def grads_body(place, q_ref, k_ref, v_ref, *refs):
    low = place[0]
    qg_ref, kl_ref, vl_ref = refs[-3:]
    lower = causal(q_ref.shape[0], True)
    upper = causal(q_ref.shape[0], False)
    for rows, (da_ref, own_ref, other_ref) in ((FAR, refs[:3]), (NEAR, refs[3:6])):
        for i, j in enumerate(rows):
            for prior, part in ((own_ref, low), (other_ref, 1 - low)):
                here, there = at(2 * j + part), at(2 * i + part)
                q, k, v, d_att = q_ref[:, here], k_ref[:, here], v_ref[:, here], da_ref[:, there]
                cross = jnp.where(lower, dot(d_att, v, NT), 0.0)
                part_sum = two_pass(cross, k, NN) + two_pass_right(d_att, prior[i], NT)
                qg_ref[:, here] = part_sum.astype(BF16)
                cross = jnp.where(upper, dot(v, d_att, NT), 0.0)
                kl_ref[:, here] = two_pass(cross, q, NN)
                scores = jnp.where(upper, dot(k, q, NT), 0.0)
                vl_ref[:, here] = two_pass(scores, d_att, NN)


def final_body(place, k_ref, v_ref, kl_ref, vl_ref, own_ref, other_ref, kg_ref, vg_ref):
    low = place[0]
    for j in range(PAIRS):
        for later, part in ((own_ref, low), (other_ref, 1 - low)):
            here = at(2 * j + part)
            high, rest = halves(later[j])
            v, k = v_ref[:, here], k_ref[:, here]
            kg_ref[:, here] = (kl_ref[:, here] + (dot(v, high, NT) + dot(v, rest, NT))).astype(BF16)
            vg_ref[:, here] = (vl_ref[:, here] + (dot(k, high, NN) + dot(k, rest, NN))).astype(BF16)


def weight_body(place, nb_ref, g_ref, nbo_ref, go_ref, *outs):
    low, core = place[0], place[1]
    half = go_ref.shape[1]
    mine = nb_ref[...]
    theirs = nbo_ref[...].astype(BF16)
    start = 0
    for keep, send in zip(outs[::2], outs[1::2]):
        width = keep.shape[2]
        ours = g_ref[:, pl.ds(pl.multiple_of(core * half + start, HD), width)]
        other = go_ref[:, start : start + width].astype(BF16)
        start += width
        product = dot(mine, ours, TN) + dot(theirs, other, TN)
        for i in range(2):
            first = product[2 * i * HD : (2 * i + 1) * HD]
            second = product[(2 * i + 1) * HD : (2 * i + 2) * HD]
            keep[i] = jnp.where(low == 0, first, second)
            send[i] = jnp.where(low == 0, second, first)


def output_body(far_ref, near_ref, w_ref, out_ref):
    size = 2 * PAIR

    @pl.loop(0, out_ref.shape[1] // size)
    def _(c):
        total = dot(near_ref[...], w_ref[PAIR : 3 * PAIR, at(c, size)], NN)
        total += dot(far_ref[:, :PAIR], w_ref[:PAIR, at(c, size)], NN)
        total += dot(far_ref[:, PAIR:], w_ref[3 * PAIR :, at(c, size)], NN)
        out_ref[:, at(c, size)] = total.astype(BF16)


def exclusive(states, count, even, reverse, pins):
    swap = [(s, s ^ 1) for s in range(count)]
    sign = -2 if reverse else 2
    pairs = count // 2

    def first(here, there):
        return jnp.where(even, there, here) if reverse else jnp.where(even, here, there)

    def links(step):
        return [(s, s + sign * step) for s in range(count) if 0 <= s + sign * step < count]

    received = [got for _, got in states]
    totals = [keep + got for keep, got in states]
    sums = [None for _ in states]
    trail = ()
    step = 1
    while step < pairs:
        pinned = (*trail, *(pins.pop(0) if pins else ()))
        for i, total in enumerate(totals):
            total = after(total, *pinned)
            pinned = (total,)
            trail = (total,) if i else ()
            got = lax.ppermute(total, "seq", links(step))
            sums[i] = got if step == 1 else sums[i] + got
            totals[i] = total + got
        step *= 2
    pinned = (*trail, *(pins.pop(0) if pins else ()))
    results = []
    for (keep, _), got, before in zip(states, received, sums):
        mine = first(before, before + got)
        theirs = after(first(before + keep, before), *pinned)
        pinned = ()
        results.append((mine, lax.ppermute(theirs, "seq", swap)))
    return results


def per_device(queries, keys, values, out_weight, out_grad):
    count = lax.axis_size("seq")
    cores = lax.axis_size("dp")
    spot = lax.axis_index("seq")
    core = lax.axis_index("dp")
    low, level = spot & 1, spot >> 1
    place = jnp.stack([low, core]).astype(jnp.int32)
    place, even, lower, outer, odd = lax.optimization_barrier(
        (place, low == 0, level < 2, (level == 0) | (level == 3), (level & 1) == 1)
    )
    q, k, v, g = queries[0], keys[0], values[0], out_grad[0]
    length, features = q.shape
    width = g.shape[1]
    part = features // 2
    half = width // 2
    state = shape((PAIRS, HD, HD), F32)
    some = shape((2, HD, HD), F32)
    rows32 = shape((length, features), F32)
    rows16 = shape((length, features), BF16)
    unit = 2 * H * length * HD
    fast = count == 8 and cores == 2
    swap = [(0, 1), (1, 0)]

    def trade(send):
        return lax.ppermute(send, "seq", [(s, s ^ 1) for s in range(count)])

    states = call(state_body, (some,) * 4, (place, k, v), unit * HD, "state")
    away = g
    if fast:
        (away,) = call(away_body, (shape((length, half), F32),), (place, after(g, states[0])), unit, "away")
        go = lax.ppermute(away, "dp", swap)
    (att,) = call(local_body, (rows32,), (q, k, v), 3 * unit * length, "local")
    (d_normed,) = call(d_normed_body, (rows32,), (g, out_weight), unit * width, "d_normed")
    far_prior, near_prior = exclusive(
        [(states[0], trade(states[1])), (states[2], trade(states[3]))], count, even, False, [(away,), (att,), (d_normed,)]
    )

    pieces = (shape((length, part), BF16), shape((length, part), F32), shape((length, part), BF16))
    far, far32, far_att, *some_states = call(
        functools.partial(norm_body, FAR),
        pieces + (some, some),
        (place, q, att, d_normed, after(far_prior[0], near_prior[0]), far_prior[1]),
        unit * HD,
        "norm_far",
    )

    def product(nb, nbo, widths):
        blocks = []
        for w in widths:
            block = shape((2, HD, w * half // sum(widths)), F32)
            blocks += [block, block]
        out = call(weight_body, tuple(blocks), (place, nb, g, nbo, go), unit * half, "weight")
        return list(zip(out[::2], out[1::2]))

    near_own, near_other = near_prior
    if fast:
        chunks = product(far, lax.ppermute(far32, "dp", swap), WIDTHS[0])
        near_own = after(near_own, chunks[0][1])
    near, near32, near_att, keep, send = call(
        functools.partial(norm_body, NEAR),
        pieces + (state, state),
        (place, q, att, d_normed, near_own, near_other, *some_states),
        unit * HD * 64,
        "norm_near",
    )

    received = trade(send)
    total = keep + received
    if fast:
        nbo = lax.ppermute(near32, "dp", swap)
        (near0_keep, near0_send), (near1_keep, near1_send) = product(after(near, received), nbo, WIDTHS[1])
        near0_got = trade(near0_send)
        far0_got = trade(after(chunks[0][1], received))
        back1 = hop(total, BACK)
    def gradients(far_att):
        return call(
            grads_body,
            (rows16, rows32, rows32),
            (place, q, k, v, far_att, *far_prior, near_att, *near_prior),
            9 * unit * length,
            "grads",
        )

    def finish(own, other):
        return call(
            final_body,
            (rows16, rows16),
            (place, k, v, key_local, value_local, own, other),
            4 * unit * HD,
            "final",
        )

    def project(rows):
        return call(
            output_body,
            (shape((length, width), BF16),),
            (rows, near, out_weight),
            unit * width,
            "output",
        )[0]

    scale = 1.0 / math.sqrt(length * count * cores)
    if not fast:
        nb = jnp.concatenate([far[:, :PAIR], near, far[:, PAIR:]], axis=1)
        weight = lax.dot_general(nb, g, TN, preferred_element_type=F32)
        weight = lax.psum_scatter(weight, "dp", scatter_dimension=1, tiled=True)
        weight_grad = lax.psum_scatter(weight, "seq", scatter_dimension=0, tiled=True) * scale
        output = project(far)
        query_grad, key_local, value_local = gradients(far_att)
        ((own, other),) = exclusive([(keep, received)], count, even, True, [])
        key_grad, value_grad = finish(own, other)
        return output[None], query_grad[None], key_grad[None], value_grad[None], weight_grad

    (far0_keep, _), (far1_keep, far1_send) = chunks
    near1_got = trade(near1_send)
    output = project(after(far, near0_send))
    back1 = after(back1, output)
    total = total + back1
    back2 = hop(total, BACK2)
    far0 = far0_keep + after(far0_got, total)
    far0_out = jnp.where(odd, far0[0], far0[1])
    far0_in = hop(far0_out, NEXT)
    far1_got = trade(after(far1_send, far0))
    query_grad, key_local, value_local = gradients(after(far_att, far0_out))
    far0_in = after(far0_in, key_local)
    far0_half = jnp.where(lower, far0[1], far0[0]) + far0_in
    far0_end = hop(far0_half, OUTWARD)
    near0 = near0_keep + after(near0_got, far0_half)
    near0_in = hop(near0, INWARD)
    outside = back1 + after(back2, near0)
    theirs = jnp.where(even, outside, outside + keep)
    other = trade(theirs)
    own = jnp.where(even, outside + received, outside)
    far1 = far1_keep + after(far1_got, theirs)
    far1_out = jnp.where(odd, far1[0], far1[1])
    far1_in = hop(far1_out, NEXT)
    near0_in = after(near0_in, far1_out, far0_end)
    near0_half = jnp.where(lower, near0[1] + near0_in[1], near0[0] + near0_in[0])
    near0_end = hop(near0_half, ACROSS)
    near1 = near1_keep + after(near1_got, near0_half)
    near1_in = hop(near1, INWARD)
    far1_in = after(far1_in, near1)
    far1_half = jnp.where(lower, far1[1], far1[0]) + far1_in
    far1_end = hop(far1_half, OUTWARD)
    key_grad, value_grad = finish(own, after(other, far1_half))
    near1_in = after(near1_in, key_grad, near0_end)
    near1_half = jnp.where(lower, near1[1] + near1_in[1], near1[0] + near1_in[0])
    near1_end = hop(near1_half, ACROSS)

    far_parts = [
        (jnp.where(lower, base[0], base[1]) + got) + end
        for base, got, end in ((far0, far0_in, far0_end), (far1, far1_in, far1_end))
    ]
    near_parts = [
        jnp.where(lower, base[0] + got[0], base[1] + got[1]) + end
        for base, got, end in ((near0, near0_in, near0_end), (near1, near1_in, near1_end))
    ]
    weight_grad = jnp.where(
        outer, jnp.concatenate(far_parts, axis=1), jnp.concatenate(near_parts, axis=1)
    )
    return output[None], query_grad[None], key_grad[None], value_grad[None], weight_grad * scale


NEXT = ((0, 1), (1, 0), (2, 3), (3, 2))
OUTWARD = ((1, 3), (2, 0))
INWARD = ((0, 1), (3, 2))
ACROSS = ((1, 2), (2, 1))
BACK = ((1, 0), (2, 1), (3, 2))
BACK2 = ((2, 0), (3, 1))


def hop(block, links):
    return lax.ppermute(block, "seq", [(2 * a + i, 2 * b + i) for a, b in links for i in range(2)])


def solution(mesh):
    rows = P(("parts", "dp"), "seq", None)
    return jax.shard_map(
        per_device,
        mesh=mesh,
        in_specs=(rows, rows, rows, P(), rows),
        out_specs=(rows, rows, rows, rows, P(("parts", "seq"), "dp")),
        check_vma=False,
    )
```

```python
import functools
import math

import jax
import jax.numpy as jnp
from jax import lax
from jax.experimental import pallas as pl
from jax.experimental.pallas import tpu as pltpu
from jax.sharding import PartitionSpec as P

H = 8
HD = 128
PAIR = 2 * HD
PAIRS = H // 2
FAR = (0, 3)
NEAR = (1, 2)
WIDTHS = ((4, 4), (5, 3))
EPSILON = 1e-06
F32 = jnp.float32
BF16 = jnp.bfloat16
VMEM = pltpu.VMEM
VMEM_LIMIT = 16 << 20
COST = 16

NN = (((1,), (0,)), ((), ()))
NT = (((1,), (1,)), ((), ()))
TN = (((0,), (0,)), ((), ()))


def dot(a, b, dims):
    return lax.dot_general(a, b, dims, preferred_element_type=F32)


def halves(a):
    high = a.astype(BF16)
    return high, (a - high.astype(F32)).astype(BF16)


def two_pass(a, b, dims):
    high, low = halves(a)
    return dot(high, b, dims) + dot(low, b, dims)


def two_pass_right(a, b, dims):
    high, low = halves(b)
    return dot(a, high, dims) + dot(a, low, dims)


def causal(length, lower):
    rows = lax.broadcasted_iota(jnp.int32, (length, length), 0)
    cols = lax.broadcasted_iota(jnp.int32, (length, length), 1)
    return rows >= cols if lower else rows <= cols


def at(position, size=HD):
    if isinstance(position, int):
        return pl.ds(position * size, size)
    return pl.ds(pl.multiple_of(position * size, size), size)


def shape(dims, dtype):
    return jax.ShapeDtypeStruct(dims, dtype)


def call(body, out_shapes, operands, flops, name):
    specs = []
    for operand in operands:
        space = pltpu.SMEM if operand.dtype == jnp.int32 else VMEM
        specs.append(pl.BlockSpec(memory_space=space))
    return pl.pallas_call(
        body,
        out_shape=tuple(out_shapes),
        in_specs=specs,
        out_specs=tuple(pl.BlockSpec(memory_space=VMEM) for _ in out_shapes),
        compiler_params=pltpu.CompilerParams(vmem_limit_bytes=VMEM_LIMIT),
        cost_estimate=pl.CostEstimate(flops=flops // COST, bytes_accessed=0, transcendentals=0),
        name=name,
    )(*operands)


def after(value, *others):
    return lax.optimization_barrier((value, *others))[0]


def state_body(place, k_ref, v_ref, *outs):
    low = place[0]
    for rows, keep_ref, send_ref in ((FAR, outs[0], outs[1]), (NEAR, outs[2], outs[3])):
        for i, j in enumerate(rows):
            for out, head in ((send_ref, 2 * j + 1 - low), (keep_ref, 2 * j + low)):
                out[i] = dot(k_ref[:, at(head)], v_ref[:, at(head)], TN)


def away_body(place, g_ref, out_ref):
    half = out_ref.shape[1]
    out_ref[...] = g_ref[:, at(1 - place[1], half)].astype(F32)


def local_body(q_ref, k_ref, v_ref, out_ref):
    mask = causal(q_ref.shape[0], True)
    for h in range(H):
        scores = dot(q_ref[:, at(h)], k_ref[:, at(h)], NT)
        scores = jnp.where(mask, scores, 0.0)
        out_ref[:, at(h)] = two_pass(scores, v_ref[:, at(h)], NN)


def d_normed_body(g_ref, w_ref, out_ref):
    @pl.loop(0, PAIRS)
    def _(j):
        out_ref[:, at(j, PAIR)] = dot(g_ref[...], w_ref[at(j, PAIR), :], NT)


def norm_body(rows, place, q_ref, att_ref, dn_ref, own_ref, other_ref, *refs):
    low = place[0]
    nb_ref, nb32_ref, da_ref, keep_ref, send_ref = refs[-5:]
    whole = keep_ref.shape[0] == PAIRS
    if whole:
        for i, j in enumerate(FAR):
            keep_ref[j] = refs[0][i]
            send_ref[j] = refs[1][i]
    for i, j in enumerate(rows):
        for prior, out, part in ((own_ref, keep_ref, low), (other_ref, send_ref, 1 - low)):
            here, there = at(2 * j + part), at(2 * i + part)
            q = q_ref[:, here]
            attended = att_ref[:, here] + two_pass_right(q, prior[i], NN)
            inverse = lax.rsqrt(jnp.mean(attended * attended, axis=-1, keepdims=True) + EPSILON)
            normed = attended * inverse
            rounded = normed.astype(BF16)
            nb_ref[:, there] = rounded
            nb32_ref[:, there] = rounded.astype(F32)
            d_normed = dn_ref[:, here]
            mean = jnp.mean(d_normed * normed, axis=-1, keepdims=True)
            d_att = (inverse * (d_normed - normed * mean)).astype(BF16)
            da_ref[:, there] = d_att
            out[j if whole else i] = dot(q, d_att, TN)


def grads_body(place, q_ref, k_ref, v_ref, *refs):
    low = place[0]
    qg_ref, kl_ref, vl_ref = refs[-3:]
    lower = causal(q_ref.shape[0], True)
    upper = causal(q_ref.shape[0], False)
    for rows, (da_ref, own_ref, other_ref) in ((FAR, refs[:3]), (NEAR, refs[3:6])):
        for i, j in enumerate(rows):
            for prior, part in ((own_ref, low), (other_ref, 1 - low)):
                here, there = at(2 * j + part), at(2 * i + part)
                q, k, v, d_att = q_ref[:, here], k_ref[:, here], v_ref[:, here], da_ref[:, there]
                cross = jnp.where(lower, dot(d_att, v, NT), 0.0)
                part_sum = two_pass(cross, k, NN) + two_pass_right(d_att, prior[i], NT)
                qg_ref[:, here] = part_sum.astype(BF16)
                cross = jnp.where(upper, dot(v, d_att, NT), 0.0)
                kl_ref[:, here] = two_pass(cross, q, NN)
                scores = jnp.where(upper, dot(k, q, NT), 0.0)
                vl_ref[:, here] = two_pass(scores, d_att, NN)


def final_body(place, k_ref, v_ref, kl_ref, vl_ref, own_ref, other_ref, kg_ref, vg_ref):
    low = place[0]
    for j in range(PAIRS):
        for later, part in ((own_ref, low), (other_ref, 1 - low)):
            here = at(2 * j + part)
            high, rest = halves(later[j])
            v, k = v_ref[:, here], k_ref[:, here]
            kg_ref[:, here] = (kl_ref[:, here] + (dot(v, high, NT) + dot(v, rest, NT))).astype(BF16)
            vg_ref[:, here] = (vl_ref[:, here] + (dot(k, high, NN) + dot(k, rest, NN))).astype(BF16)


def weight_body(place, nb_ref, g_ref, nbo_ref, go_ref, *outs):
    low, core = place[0], place[1]
    half = go_ref.shape[1]
    mine = nb_ref[...]
    theirs = nbo_ref[...].astype(BF16)
    start = 0
    for keep, send in zip(outs[::2], outs[1::2]):
        width = keep.shape[2]
        ours = g_ref[:, pl.ds(pl.multiple_of(core * half + start, HD), width)]
        other = go_ref[:, start : start + width].astype(BF16)
        start += width
        product = dot(mine, ours, TN) + dot(theirs, other, TN)
        for i in range(2):
            first = product[2 * i * HD : (2 * i + 1) * HD]
            second = product[(2 * i + 1) * HD : (2 * i + 2) * HD]
            keep[i] = jnp.where(low == 0, first, second)
            send[i] = jnp.where(low == 0, second, first)


def output_body(far_ref, near_ref, w_ref, out_ref):
    size = 2 * PAIR

    @pl.loop(0, out_ref.shape[1] // size)
    def _(c):
        total = dot(near_ref[...], w_ref[PAIR : 3 * PAIR, at(c, size)], NN)
        total += dot(far_ref[:, :PAIR], w_ref[:PAIR, at(c, size)], NN)
        total += dot(far_ref[:, PAIR:], w_ref[3 * PAIR :, at(c, size)], NN)
        out_ref[:, at(c, size)] = total.astype(BF16)


def exclusive(states, count, even, reverse, pins):
    swap = [(s, s ^ 1) for s in range(count)]
    sign = -2 if reverse else 2
    pairs = count // 2

    def first(here, there):
        return jnp.where(even, there, here) if reverse else jnp.where(even, here, there)

    def links(step):
        return [(s, s + sign * step) for s in range(count) if 0 <= s + sign * step < count]

    received = [got for _, got in states]
    totals = [keep + got for keep, got in states]
    sums = [None for _ in states]
    trail = ()
    step = 1
    while step < pairs:
        pinned = (*trail, *(pins.pop(0) if pins else ()))
        for i, total in enumerate(totals):
            total = after(total, *pinned)
            pinned = (total,)
            trail = (total,) if i else ()
            got = lax.ppermute(total, "seq", links(step))
            sums[i] = got if step == 1 else sums[i] + got
            totals[i] = total + got
        step *= 2
    pinned = (*trail, *(pins.pop(0) if pins else ()))
    results = []
    for (keep, _), got, before in zip(states, received, sums):
        mine = first(before, before + got)
        theirs = after(first(before + keep, before), *pinned)
        pinned = ()
        results.append((mine, lax.ppermute(theirs, "seq", swap)))
    return results


def per_device(queries, keys, values, out_weight, out_grad):
    count = lax.axis_size("seq")
    cores = lax.axis_size("dp")
    spot = lax.axis_index("seq")
    core = lax.axis_index("dp")
    low, level = spot & 1, spot >> 1
    place = jnp.stack([low, core]).astype(jnp.int32)
    place, even, lower, outer, odd = lax.optimization_barrier(
        (place, low == 0, level < 2, (level == 0) | (level == 3), (level & 1) == 1)
    )
    q, k, v, g = queries[0], keys[0], values[0], out_grad[0]
    length, features = q.shape
    width = g.shape[1]
    part = features // 2
    half = width // 2
    state = shape((PAIRS, HD, HD), F32)
    some = shape((2, HD, HD), F32)
    rows32 = shape((length, features), F32)
    rows16 = shape((length, features), BF16)
    unit = 2 * H * length * HD
    fast = count == 8 and cores == 2
    swap = [(0, 1), (1, 0)]

    def trade(send):
        return lax.ppermute(send, "seq", [(s, s ^ 1) for s in range(count)])

    states = call(state_body, (some,) * 4, (place, k, v), unit * HD, "state")
    away = g
    if fast:
        (away,) = call(away_body, (shape((length, half), F32),), (place, after(g, states[0])), unit, "away")
        go = lax.ppermute(away, "dp", swap)
    (att,) = call(local_body, (rows32,), (q, k, v), 3 * unit * length, "local")
    (d_normed,) = call(d_normed_body, (rows32,), (g, out_weight), unit * width, "d_normed")
    far_prior, near_prior = exclusive(
        [(states[0], trade(states[1])), (states[2], trade(states[3]))], count, even, False, [(away,), (att,), (d_normed,)]
    )

    pieces = (shape((length, part), BF16), shape((length, part), F32), shape((length, part), BF16))
    far, far32, far_att, *some_states = call(
        functools.partial(norm_body, FAR),
        pieces + (some, some),
        (place, q, att, d_normed, after(far_prior[0], near_prior[0]), far_prior[1]),
        unit * HD,
        "norm_far",
    )

    def product(nb, nbo, widths):
        blocks = []
        for w in widths:
            block = shape((2, HD, w * half // sum(widths)), F32)
            blocks += [block, block]
        out = call(weight_body, tuple(blocks), (place, nb, g, nbo, go), unit * half, "weight")
        return list(zip(out[::2], out[1::2]))

    near_own, near_other = near_prior
    if fast:
        chunks = product(far, lax.ppermute(far32, "dp", swap), WIDTHS[0])
        near_own = after(near_own, chunks[0][1])
    near, near32, near_att, keep, send = call(
        functools.partial(norm_body, NEAR),
        pieces + (state, state),
        (place, q, att, d_normed, near_own, near_other, *some_states),
        unit * HD * 64,
        "norm_near",
    )

    received = trade(send)
    total = keep + received
    if fast:
        nbo = lax.ppermute(near32, "dp", swap)
        (near0_keep, near0_send), (near1_keep, near1_send) = product(after(near, received), nbo, WIDTHS[1])
        near0_got = trade(near0_send)
        far0_got = trade(after(chunks[0][1], near_other))
        back1 = hop(total, BACK)
    def gradients(far_att):
        return call(
            grads_body,
            (rows16, rows32, rows32),
            (place, q, k, v, far_att, *far_prior, near_att, *near_prior),
            9 * unit * length,
            "grads",
        )

    def finish(own, other):
        return call(
            final_body,
            (rows16, rows16),
            (place, k, v, key_local, value_local, own, other),
            4 * unit * HD,
            "final",
        )

    def project(rows):
        return call(
            output_body,
            (shape((length, width), BF16),),
            (rows, near, out_weight),
            unit * width,
            "output",
        )[0]

    scale = 1.0 / math.sqrt(length * count * cores)
    if not fast:
        nb = jnp.concatenate([far[:, :PAIR], near, far[:, PAIR:]], axis=1)
        weight = lax.dot_general(nb, g, TN, preferred_element_type=F32)
        weight = lax.psum_scatter(weight, "dp", scatter_dimension=1, tiled=True)
        weight_grad = lax.psum_scatter(weight, "seq", scatter_dimension=0, tiled=True) * scale
        output = project(far)
        query_grad, key_local, value_local = gradients(far_att)
        ((own, other),) = exclusive([(keep, received)], count, even, True, [])
        key_grad, value_grad = finish(own, other)
        return output[None], query_grad[None], key_grad[None], value_grad[None], weight_grad

    (far0_keep, _), (far1_keep, far1_send) = chunks
    near1_got = trade(near1_send)
    output = project(after(far, near0_send))
    back1 = after(back1, output)
    total = total + back1
    back2 = hop(total, BACK2)
    far0 = far0_keep + after(far0_got, total)
    far0_out = jnp.where(odd, far0[0], far0[1])
    far0_in = hop(far0_out, NEXT)
    far1_got = trade(after(far1_send, far0))
    query_grad, key_local, value_local = gradients(after(far_att, far0_out))
    far0_in = after(far0_in, key_local)
    far0_half = jnp.where(lower, far0[1], far0[0]) + far0_in
    far0_end = hop(far0_half, OUTWARD)
    near0 = near0_keep + after(near0_got, far0_half)
    near0_in = hop(near0, INWARD)
    outside = back1 + after(back2, near0)
    theirs = jnp.where(even, outside, outside + keep)
    other = trade(theirs)
    own = jnp.where(even, outside + received, outside)
    far1 = far1_keep + after(far1_got, theirs)
    far1_out = jnp.where(odd, far1[0], far1[1])
    far1_in = hop(far1_out, NEXT)
    near0_in = after(near0_in, far1_out, far0_end)
    near0_half = jnp.where(lower, near0[1] + near0_in[1], near0[0] + near0_in[0])
    near0_end = hop(near0_half, ACROSS)
    near1 = near1_keep + after(near1_got, near0_half)
    near1_in = hop(near1, INWARD)
    far1_in = after(far1_in, near1)
    far1_half = jnp.where(lower, far1[1], far1[0]) + far1_in
    far1_end = hop(far1_half, OUTWARD)
    near1_in = after(near1_in, far1_half)
    near1_half = jnp.where(lower, near1[1] + near1_in[1], near1[0] + near1_in[0])
    near1_end = hop(near1_half, ACROSS)
    key_grad, value_grad = finish(own, after(other, near1_half))
    near0_end, far1_end = after(near0_end, near1_half), after(far1_end, near1_half)

    far_parts = [
        (jnp.where(lower, base[0], base[1]) + got) + end
        for base, got, end in ((far0, far0_in, far0_end), (far1, far1_in, far1_end))
    ]
    near_parts = [
        jnp.where(lower, base[0] + got[0], base[1] + got[1]) + end
        for base, got, end in ((near0, near0_in, near0_end), (near1, near1_in, near1_end))
    ]
    weight_grad = jnp.where(
        outer, jnp.concatenate(far_parts, axis=1), jnp.concatenate(near_parts, axis=1)
    )
    return output[None], query_grad[None], key_grad[None], value_grad[None], weight_grad * scale


NEXT = ((0, 1), (1, 0), (2, 3), (3, 2))
OUTWARD = ((1, 3), (2, 0))
INWARD = ((0, 1), (3, 2))
ACROSS = ((1, 2), (2, 1))
BACK = ((1, 0), (2, 1), (3, 2))
BACK2 = ((2, 0), (3, 1))


def hop(block, links):
    return lax.ppermute(block, "seq", [(2 * a + i, 2 * b + i) for a, b in links for i in range(2)])


def solution(mesh):
    rows = P(("parts", "dp"), "seq", None)
    return jax.shard_map(
        per_device,
        mesh=mesh,
        in_specs=(rows, rows, rows, P(), rows),
        out_specs=(rows, rows, rows, rows, P(("parts", "seq"), "dp")),
        check_vma=False,
    )
```

```python
import functools
import math

import jax
import jax.numpy as jnp
from jax import lax
from jax.experimental import pallas as pl
from jax.experimental.pallas import tpu as pltpu
from jax.sharding import PartitionSpec as P

H = 8
HD = 128
PAIR = 2 * HD
PAIRS = H // 2
FAR = (0, 3)
NEAR = (1, 2)
WIDTHS = ((4, 4), (5, 3))
EPSILON = 1e-06
F32 = jnp.float32
BF16 = jnp.bfloat16
VMEM = pltpu.VMEM
VMEM_LIMIT = 16 << 20
COST = 16

NN = (((1,), (0,)), ((), ()))
NT = (((1,), (1,)), ((), ()))
TN = (((0,), (0,)), ((), ()))


def dot(a, b, dims):
    return lax.dot_general(a, b, dims, preferred_element_type=F32)


def halves(a):
    high = a.astype(BF16)
    return high, (a - high.astype(F32)).astype(BF16)


def two_pass(a, b, dims):
    high, low = halves(a)
    return dot(high, b, dims) + dot(low, b, dims)


def two_pass_right(a, b, dims):
    high, low = halves(b)
    return dot(a, high, dims) + dot(a, low, dims)


def causal(length, lower):
    rows = lax.broadcasted_iota(jnp.int32, (length, length), 0)
    cols = lax.broadcasted_iota(jnp.int32, (length, length), 1)
    return rows >= cols if lower else rows <= cols


def at(position, size=HD):
    if isinstance(position, int):
        return pl.ds(position * size, size)
    return pl.ds(pl.multiple_of(position * size, size), size)


def shape(dims, dtype):
    return jax.ShapeDtypeStruct(dims, dtype)


def call(body, out_shapes, operands, flops, name):
    specs = []
    for operand in operands:
        space = pltpu.SMEM if operand.dtype == jnp.int32 else VMEM
        specs.append(pl.BlockSpec(memory_space=space))
    return pl.pallas_call(
        body,
        out_shape=tuple(out_shapes),
        in_specs=specs,
        out_specs=tuple(pl.BlockSpec(memory_space=VMEM) for _ in out_shapes),
        compiler_params=pltpu.CompilerParams(vmem_limit_bytes=VMEM_LIMIT),
        cost_estimate=pl.CostEstimate(flops=flops // COST, bytes_accessed=0, transcendentals=0),
        name=name,
    )(*operands)


def after(value, *others):
    return lax.optimization_barrier((value, *others))[0]


def state_body(place, k_ref, v_ref, *outs):
    low = place[0]
    for rows, keep_ref, send_ref in ((FAR, outs[0], outs[1]), (NEAR, outs[2], outs[3])):
        for i, j in enumerate(rows):
            for out, head in ((send_ref, 2 * j + 1 - low), (keep_ref, 2 * j + low)):
                out[i] = dot(k_ref[:, at(head)], v_ref[:, at(head)], TN)


def away_body(place, g_ref, out_ref):
    half = out_ref.shape[1]
    out_ref[...] = g_ref[:, at(1 - place[1], half)].astype(F32)


def local_body(q_ref, k_ref, v_ref, out_ref):
    mask = causal(q_ref.shape[0], True)
    for h in range(H):
        scores = dot(q_ref[:, at(h)], k_ref[:, at(h)], NT)
        scores = jnp.where(mask, scores, 0.0)
        out_ref[:, at(h)] = two_pass(scores, v_ref[:, at(h)], NN)


def d_normed_body(g_ref, w_ref, out_ref):
    @pl.loop(0, PAIRS)
    def _(j):
        out_ref[:, at(j, PAIR)] = dot(g_ref[...], w_ref[at(j, PAIR), :], NT)


def norm_body(rows, place, q_ref, att_ref, dn_ref, own_ref, other_ref, *refs):
    low = place[0]
    nb_ref, nb32_ref, da_ref, keep_ref, send_ref = refs[-5:]
    whole = keep_ref.shape[0] == PAIRS
    if whole:
        for i, j in enumerate(FAR):
            keep_ref[j] = refs[0][i]
            send_ref[j] = refs[1][i]
    for i, j in enumerate(rows):
        for prior, out, part in ((own_ref, keep_ref, low), (other_ref, send_ref, 1 - low)):
            here, there = at(2 * j + part), at(2 * i + part)
            q = q_ref[:, here]
            attended = att_ref[:, here] + two_pass_right(q, prior[i], NN)
            inverse = lax.rsqrt(jnp.mean(attended * attended, axis=-1, keepdims=True) + EPSILON)
            normed = attended * inverse
            rounded = normed.astype(BF16)
            nb_ref[:, there] = rounded
            nb32_ref[:, there] = rounded.astype(F32)
            d_normed = dn_ref[:, here]
            mean = jnp.mean(d_normed * normed, axis=-1, keepdims=True)
            d_att = (inverse * (d_normed - normed * mean)).astype(BF16)
            da_ref[:, there] = d_att
            out[j if whole else i] = dot(q, d_att, TN)


def grads_body(rows, place, q_ref, k_ref, v_ref, da_ref, own_ref, other_ref, qg_ref, kl_ref, vl_ref):
    low = place[0]
    lower = causal(q_ref.shape[0], True)
    upper = causal(q_ref.shape[0], False)
    for i, j in enumerate(rows):
        for prior, part in ((own_ref, low), (other_ref, 1 - low)):
            here, there = at(2 * j + part), at(2 * i + part)
            q, k, v, d_att = q_ref[:, here], k_ref[:, here], v_ref[:, here], da_ref[:, there]
            cross = jnp.where(lower, dot(d_att, v, NT), 0.0)
            part_sum = two_pass(cross, k, NN) + two_pass_right(d_att, prior[i], NT)
            qg_ref[:, there] = part_sum.astype(BF16)
            cross = jnp.where(upper, dot(v, d_att, NT), 0.0)
            kl_ref[:, there] = two_pass(cross, q, NN)
            scores = jnp.where(upper, dot(k, q, NT), 0.0)
            vl_ref[:, there] = two_pass(scores, d_att, NN)


def final_body(place, k_ref, v_ref, *refs):
    low = place[0]
    own_ref, other_ref, qg_ref, kg_ref, vg_ref = refs[-5:]
    for rows, (part_ref, kl_ref, vl_ref) in ((FAR, refs[:3]), (NEAR, refs[3:6])):
        for i, j in enumerate(rows):
            qg_ref[:, at(j, PAIR)] = part_ref[:, at(i, PAIR)]
            for later, part in ((own_ref, low), (other_ref, 1 - low)):
                here, there = at(2 * j + part), at(2 * i + part)
                high, rest = halves(later[j])
                v, k = v_ref[:, here], k_ref[:, here]
                k_sum = kl_ref[:, there] + (dot(v, high, NT) + dot(v, rest, NT))
                kg_ref[:, here] = k_sum.astype(BF16)
                v_sum = vl_ref[:, there] + (dot(k, high, NN) + dot(k, rest, NN))
                vg_ref[:, here] = v_sum.astype(BF16)


def weight_body(place, nb_ref, g_ref, nbo_ref, go_ref, *outs):
    low, core = place[0], place[1]
    half = go_ref.shape[1]
    mine = nb_ref[...]
    theirs = nbo_ref[...].astype(BF16)
    start = 0
    for keep, send in zip(outs[::2], outs[1::2]):
        width = keep.shape[2]
        ours = g_ref[:, pl.ds(pl.multiple_of(core * half + start, HD), width)]
        other = go_ref[:, start : start + width].astype(BF16)
        start += width
        product = dot(mine, ours, TN) + dot(theirs, other, TN)
        for i in range(2):
            first = product[2 * i * HD : (2 * i + 1) * HD]
            second = product[(2 * i + 1) * HD : (2 * i + 2) * HD]
            keep[i] = jnp.where(low == 0, first, second)
            send[i] = jnp.where(low == 0, second, first)


def output_body(far_ref, near_ref, w_ref, out_ref):
    size = 2 * PAIR

    @pl.loop(0, out_ref.shape[1] // size)
    def _(c):
        total = dot(near_ref[...], w_ref[PAIR : 3 * PAIR, at(c, size)], NN)
        total += dot(far_ref[:, :PAIR], w_ref[:PAIR, at(c, size)], NN)
        total += dot(far_ref[:, PAIR:], w_ref[3 * PAIR :, at(c, size)], NN)
        out_ref[:, at(c, size)] = total.astype(BF16)


def exclusive(states, count, even, reverse, pins):
    swap = [(s, s ^ 1) for s in range(count)]
    sign = -2 if reverse else 2
    pairs = count // 2

    def first(here, there):
        return jnp.where(even, there, here) if reverse else jnp.where(even, here, there)

    def links(step):
        return [(s, s + sign * step) for s in range(count) if 0 <= s + sign * step < count]

    received = [got for _, got in states]
    totals = [keep + got for keep, got in states]
    sums = [None for _ in states]
    trail = ()
    step = 1
    while step < pairs:
        pinned = (*trail, *(pins.pop(0) if pins else ()))
        for i, total in enumerate(totals):
            total = after(total, *pinned)
            pinned = (total,)
            trail = (total,) if i else ()
            got = lax.ppermute(total, "seq", links(step))
            sums[i] = got if step == 1 else sums[i] + got
            totals[i] = total + got
        step *= 2
    pinned = (*trail, *(pins.pop(0) if pins else ()))
    results = []
    for (keep, _), got, before in zip(states, received, sums):
        mine = first(before, before + got)
        theirs = after(first(before + keep, before), *pinned)
        pinned = ()
        results.append((mine, lax.ppermute(theirs, "seq", swap)))
    return results


def per_device(queries, keys, values, out_weight, out_grad):
    count = lax.axis_size("seq")
    cores = lax.axis_size("dp")
    spot = lax.axis_index("seq")
    core = lax.axis_index("dp")
    low, level = spot & 1, spot >> 1
    place = jnp.stack([low, core]).astype(jnp.int32)
    place, even, lower, outer, odd = lax.optimization_barrier(
        (place, low == 0, level < 2, (level == 0) | (level == 3), (level & 1) == 1)
    )
    q, k, v, g = queries[0], keys[0], values[0], out_grad[0]
    length, features = q.shape
    width = g.shape[1]
    part = features // 2
    half = width // 2
    state = shape((PAIRS, HD, HD), F32)
    some = shape((2, HD, HD), F32)
    rows32 = shape((length, features), F32)
    rows16 = shape((length, features), BF16)
    unit = 2 * H * length * HD
    fast = count == 8 and cores == 2
    swap = [(0, 1), (1, 0)]

    def trade(send):
        return lax.ppermute(send, "seq", [(s, s ^ 1) for s in range(count)])

    states = call(state_body, (some,) * 4, (place, k, v), unit * HD, "state")
    away = g
    if fast:
        (away,) = call(away_body, (shape((length, half), F32),), (place, after(g, states[0])), unit, "away")
        go = lax.ppermute(away, "dp", swap)
    (att,) = call(local_body, (rows32,), (q, k, v), 3 * unit * length, "local")
    (d_normed,) = call(d_normed_body, (rows32,), (g, out_weight), unit * width, "d_normed")
    far_prior, near_prior = exclusive(
        [(states[0], trade(states[1])), (states[2], trade(states[3]))], count, even, False, [(away,), (att,), (d_normed,)]
    )

    pieces = (shape((length, part), BF16), shape((length, part), F32), shape((length, part), BF16))
    far, far32, far_att, *some_states = call(
        functools.partial(norm_body, FAR),
        pieces + (some, some),
        (place, q, att, d_normed, after(far_prior[0], near_prior[0]), far_prior[1]),
        unit * HD,
        "norm_far",
    )

    def product(nb, nbo, widths):
        blocks = []
        for w in widths:
            block = shape((2, HD, w * half // sum(widths)), F32)
            blocks += [block, block]
        out = call(weight_body, tuple(blocks), (place, nb, g, nbo, go), unit * half, "weight")
        return list(zip(out[::2], out[1::2]))

    near_own, near_other = near_prior
    if fast:
        chunks = product(far, lax.ppermute(far32, "dp", swap), WIDTHS[0])
        near_own = after(near_own, chunks[0][1])
    near, near32, near_att, keep, send = call(
        functools.partial(norm_body, NEAR),
        pieces + (state, state),
        (place, q, att, d_normed, near_own, near_other, *some_states),
        unit * HD * 64,
        "norm_near",
    )

    received = trade(send)
    def gradients(rows, d_att, prior):
        return call(
            functools.partial(grads_body, rows),
            (pieces[0], pieces[1], pieces[1]),
            (place, q, k, v, d_att, *prior),
            5 * unit * length,
            "grads",
        )

    def finish(own, other):
        return call(
            final_body,
            (rows16, rows16, rows16),
            (place, k, v, *far_grads, *near_grads, own, other),
            4 * unit * HD,
            "final",
        )

    def project(rows):
        return call(
            output_body,
            (shape((length, width), BF16),),
            (rows, near, out_weight),
            unit * width,
            "output",
        )[0]

    scale = 1.0 / math.sqrt(length * count * cores)
    if not fast:
        nb = jnp.concatenate([far[:, :PAIR], near, far[:, PAIR:]], axis=1)
        weight = lax.dot_general(nb, g, TN, preferred_element_type=F32)
        weight = lax.psum_scatter(weight, "dp", scatter_dimension=1, tiled=True)
        weight_grad = lax.psum_scatter(weight, "seq", scatter_dimension=0, tiled=True) * scale
        output = project(far)
        far_grads = gradients(FAR, far_att, far_prior)
        near_grads = gradients(NEAR, near_att, near_prior)
        ((own, other),) = exclusive([(keep, received)], count, even, True, [])
        query_grad, key_grad, value_grad = finish(own, other)
        return output[None], query_grad[None], key_grad[None], value_grad[None], weight_grad

    (far0_keep, far0_send), (far1_keep, far1_send) = chunks
    nbo = lax.ppermute(near32, "dp", swap)
    far0_got = trade(after(far0_send, near_other))
    far_grads = gradients(FAR, after(far_att, send), far_prior)
    received = after(received, far_grads[1])
    (near0_keep, near0_send), (near1_keep, near1_send) = product(after(near, received), nbo, WIDTHS[1])
    near0_got = trade(near0_send)
    total = keep + received
    back1 = hop(total, BACK)
    near1_got = trade(near1_send)
    back1 = after(back1, near0_send)
    total = total + back1
    back2 = hop(total, BACK2)
    far0 = far0_keep + after(far0_got, total)
    far0_out = jnp.where(odd, far0[0], far0[1])
    far0_in = hop(far0_out, NEXT)
    far1_got = trade(after(far1_send, far0))
    near_grads = gradients(NEAR, after(near_att, far0_out), near_prior)
    far0_in = after(far0_in, near_grads[1])
    far0_half = jnp.where(lower, far0[1], far0[0]) + far0_in
    far0_end = hop(far0_half, OUTWARD)
    near0 = near0_keep + after(near0_got, far0_half)
    near0_in = hop(near0, INWARD)
    outside = back1 + after(back2, near0)
    theirs = jnp.where(even, outside, outside + keep)
    other = trade(theirs)
    own = jnp.where(even, outside + received, outside)
    output = project(after(far, theirs))
    far1 = far1_keep + after(far1_got, output)
    far1_out = jnp.where(odd, far1[0], far1[1])
    far1_in = hop(far1_out, NEXT)
    near0_in = after(near0_in, far1_out, far0_end)
    near0_half = jnp.where(lower, near0[1] + near0_in[1], near0[0] + near0_in[0])
    near0_end = hop(near0_half, ACROSS)
    near1 = near1_keep + after(near1_got, near0_half)
    near1_in = hop(near1, INWARD)
    far1_in = after(far1_in, near1)
    far1_half = jnp.where(lower, far1[1], far1[0]) + far1_in
    far1_end = hop(far1_half, OUTWARD)
    near1_in = after(near1_in, far1_half)
    near1_half = jnp.where(lower, near1[1] + near1_in[1], near1[0] + near1_in[0])
    near1_end = hop(near1_half, ACROSS)
    query_grad, key_grad, value_grad = finish(own, after(other, near1_half))
    near0_end, far1_end = after(near0_end, near1_half), after(far1_end, near1_half)

    far_parts = [
        (jnp.where(lower, base[0], base[1]) + got) + end
        for base, got, end in ((far0, far0_in, far0_end), (far1, far1_in, far1_end))
    ]
    near_parts = [
        jnp.where(lower, base[0] + got[0], base[1] + got[1]) + end
        for base, got, end in ((near0, near0_in, near0_end), (near1, near1_in, near1_end))
    ]
    weight_grad = jnp.where(
        outer, jnp.concatenate(far_parts, axis=1), jnp.concatenate(near_parts, axis=1)
    )
    return output[None], query_grad[None], key_grad[None], value_grad[None], weight_grad * scale


NEXT = ((0, 1), (1, 0), (2, 3), (3, 2))
OUTWARD = ((1, 3), (2, 0))
INWARD = ((0, 1), (3, 2))
ACROSS = ((1, 2), (2, 1))
BACK = ((1, 0), (2, 1), (3, 2))
BACK2 = ((2, 0), (3, 1))


def hop(block, links):
    return lax.ppermute(block, "seq", [(2 * a + i, 2 * b + i) for a, b in links for i in range(2)])


def solution(mesh):
    rows = P(("parts", "dp"), "seq", None)
    return jax.shard_map(
        per_device,
        mesh=mesh,
        in_specs=(rows, rows, rows, P(), rows),
        out_specs=(rows, rows, rows, rows, P(("parts", "seq"), "dp")),
        check_vma=False,
    )
```

```python
import functools
import math

import jax
import jax.numpy as jnp
from jax import lax
from jax.experimental import pallas as pl
from jax.experimental.pallas import tpu as pltpu
from jax.sharding import PartitionSpec as P

H = 8
HD = 128
PAIR = 2 * HD
PAIRS = H // 2
FAR = (0, 3)
NEAR = (1, 2)
WIDTHS = ((4, 4), (5, 3))
EPSILON = 1e-06
F32 = jnp.float32
BF16 = jnp.bfloat16
VMEM = pltpu.VMEM
VMEM_LIMIT = 16 << 20
COST = 16

NN = (((1,), (0,)), ((), ()))
NT = (((1,), (1,)), ((), ()))
TN = (((0,), (0,)), ((), ()))


def dot(a, b, dims):
    return lax.dot_general(a, b, dims, preferred_element_type=F32)


def halves(a):
    high = a.astype(BF16)
    return high, (a - high.astype(F32)).astype(BF16)


def two_pass(a, b, dims):
    high, low = halves(a)
    return dot(high, b, dims) + dot(low, b, dims)


def two_pass_right(a, b, dims):
    high, low = halves(b)
    return dot(a, high, dims) + dot(a, low, dims)


def causal(length, lower):
    rows = lax.broadcasted_iota(jnp.int32, (length, length), 0)
    cols = lax.broadcasted_iota(jnp.int32, (length, length), 1)
    return rows >= cols if lower else rows <= cols


def at(position, size=HD):
    if isinstance(position, int):
        return pl.ds(position * size, size)
    return pl.ds(pl.multiple_of(position * size, size), size)


def shape(dims, dtype):
    return jax.ShapeDtypeStruct(dims, dtype)


def call(body, out_shapes, operands, flops, name):
    specs = []
    for operand in operands:
        space = pltpu.SMEM if operand.dtype == jnp.int32 else VMEM
        specs.append(pl.BlockSpec(memory_space=space))
    return pl.pallas_call(
        body,
        out_shape=tuple(out_shapes),
        in_specs=specs,
        out_specs=tuple(pl.BlockSpec(memory_space=VMEM) for _ in out_shapes),
        compiler_params=pltpu.CompilerParams(vmem_limit_bytes=VMEM_LIMIT),
        cost_estimate=pl.CostEstimate(flops=flops // COST, bytes_accessed=0, transcendentals=0),
        name=name,
    )(*operands)


def after(value, *others):
    return lax.optimization_barrier((value, *others))[0]


def state_body(place, k_ref, v_ref, *outs):
    low = place[0]
    for rows, keep_ref, send_ref in ((FAR, outs[0], outs[1]), (NEAR, outs[2], outs[3])):
        for i, j in enumerate(rows):
            for out, head in ((send_ref, 2 * j + 1 - low), (keep_ref, 2 * j + low)):
                out[i] = dot(k_ref[:, at(head)], v_ref[:, at(head)], TN)


def away_body(place, g_ref, out_ref):
    half = out_ref.shape[1]
    out_ref[...] = g_ref[:, at(1 - place[1], half)].astype(F32)


def local_body(q_ref, k_ref, v_ref, out_ref):
    mask = causal(q_ref.shape[0], True)
    for h in range(H):
        scores = dot(q_ref[:, at(h)], k_ref[:, at(h)], NT)
        scores = jnp.where(mask, scores, 0.0)
        out_ref[:, at(h)] = two_pass(scores, v_ref[:, at(h)], NN)


def d_normed_body(g_ref, w_ref, out_ref):
    @pl.loop(0, PAIRS)
    def _(j):
        out_ref[:, at(j, PAIR)] = dot(g_ref[...], w_ref[at(j, PAIR), :], NT)


def norm_body(rows, place, q_ref, att_ref, dn_ref, own_ref, other_ref, *refs):
    low = place[0]
    nb_ref, nb32_ref, da_ref, keep_ref, send_ref = refs[-5:]
    whole = keep_ref.shape[0] == PAIRS
    if whole:
        for i, j in enumerate(FAR):
            keep_ref[j] = refs[0][i]
            send_ref[j] = refs[1][i]
    for i, j in enumerate(rows):
        for prior, out, part in ((own_ref, keep_ref, low), (other_ref, send_ref, 1 - low)):
            here, there = at(2 * j + part), at(2 * i + part)
            q = q_ref[:, here]
            attended = att_ref[:, here] + two_pass_right(q, prior[i], NN)
            inverse = lax.rsqrt(jnp.mean(attended * attended, axis=-1, keepdims=True) + EPSILON)
            normed = attended * inverse
            rounded = normed.astype(BF16)
            nb_ref[:, there] = rounded
            nb32_ref[:, there] = rounded.astype(F32)
            d_normed = dn_ref[:, here]
            mean = jnp.mean(d_normed * normed, axis=-1, keepdims=True)
            d_att = (inverse * (d_normed - normed * mean)).astype(BF16)
            da_ref[:, there] = d_att
            out[j if whole else i] = dot(q, d_att, TN)


def grads_body(rows, place, q_ref, k_ref, v_ref, da_ref, own_ref, other_ref, qg_ref, kl_ref, vl_ref):
    low = place[0]
    lower = causal(q_ref.shape[0], True)
    upper = causal(q_ref.shape[0], False)
    for i, j in enumerate(rows):
        for prior, part in ((own_ref, low), (other_ref, 1 - low)):
            here, there = at(2 * j + part), at(2 * i + part)
            q, k, v, d_att = q_ref[:, here], k_ref[:, here], v_ref[:, here], da_ref[:, there]
            cross = jnp.where(lower, dot(d_att, v, NT), 0.0)
            part_sum = two_pass(cross, k, NN) + two_pass_right(d_att, prior[i], NT)
            qg_ref[:, there] = part_sum.astype(BF16)
            cross = jnp.where(upper, dot(v, d_att, NT), 0.0)
            kl_ref[:, there] = two_pass(cross, q, NN)
            scores = jnp.where(upper, dot(k, q, NT), 0.0)
            vl_ref[:, there] = two_pass(scores, d_att, NN)


def final_body(place, k_ref, v_ref, *refs):
    low = place[0]
    own_ref, other_ref, qg_ref, kg_ref, vg_ref = refs[-5:]
    for rows, (part_ref, kl_ref, vl_ref) in ((FAR, refs[:3]), (NEAR, refs[3:6])):
        for i, j in enumerate(rows):
            qg_ref[:, at(j, PAIR)] = part_ref[:, at(i, PAIR)]
            for later, part in ((own_ref, low), (other_ref, 1 - low)):
                here, there = at(2 * j + part), at(2 * i + part)
                high, rest = halves(later[j])
                v, k = v_ref[:, here], k_ref[:, here]
                k_sum = kl_ref[:, there] + (dot(v, high, NT) + dot(v, rest, NT))
                kg_ref[:, here] = k_sum.astype(BF16)
                v_sum = vl_ref[:, there] + (dot(k, high, NN) + dot(k, rest, NN))
                vg_ref[:, here] = v_sum.astype(BF16)


def weight_body(place, nb_ref, g_ref, nbo_ref, go_ref, *outs):
    low, core = place[0], place[1]
    half = go_ref.shape[1]
    mine = nb_ref[...]
    theirs = nbo_ref[...].astype(BF16)
    start = 0
    for keep, send in zip(outs[::2], outs[1::2]):
        width = keep.shape[2]
        ours = g_ref[:, pl.ds(pl.multiple_of(core * half + start, HD), width)]
        other = go_ref[:, start : start + width].astype(BF16)
        start += width
        product = dot(mine, ours, TN) + dot(theirs, other, TN)
        for i in range(2):
            first = product[2 * i * HD : (2 * i + 1) * HD]
            second = product[(2 * i + 1) * HD : (2 * i + 2) * HD]
            keep[i] = jnp.where(low == 0, first, second)
            send[i] = jnp.where(low == 0, second, first)


def output_body(far_ref, near_ref, w_ref, out_ref):
    size = 2 * PAIR

    @pl.loop(0, out_ref.shape[1] // size)
    def _(c):
        total = dot(near_ref[...], w_ref[PAIR : 3 * PAIR, at(c, size)], NN)
        total += dot(far_ref[:, :PAIR], w_ref[:PAIR, at(c, size)], NN)
        total += dot(far_ref[:, PAIR:], w_ref[3 * PAIR :, at(c, size)], NN)
        out_ref[:, at(c, size)] = total.astype(BF16)


def exclusive(states, count, even, reverse, pins):
    swap = [(s, s ^ 1) for s in range(count)]
    sign = -2 if reverse else 2
    pairs = count // 2

    def first(here, there):
        return jnp.where(even, there, here) if reverse else jnp.where(even, here, there)

    def links(step):
        return [(s, s + sign * step) for s in range(count) if 0 <= s + sign * step < count]

    received = [got for _, got in states]
    totals = [keep + got for keep, got in states]
    sums = [None for _ in states]
    trail = ()
    step = 1
    while step < pairs:
        pinned = (*trail, *(pins.pop(0) if pins else ()))
        for i, total in enumerate(totals):
            total = after(total, *pinned)
            pinned = (total,)
            trail = (total,) if i else ()
            got = lax.ppermute(total, "seq", links(step))
            sums[i] = got if step == 1 else sums[i] + got
            totals[i] = total + got
        step *= 2
    pinned = (*trail, *(pins.pop(0) if pins else ()))
    results = []
    for (keep, _), got, before in zip(states, received, sums):
        mine = first(before, before + got)
        theirs = after(first(before + keep, before), *pinned)
        pinned = ()
        results.append((mine, lax.ppermute(theirs, "seq", swap)))
    return results


def per_device(queries, keys, values, out_weight, out_grad):
    count = lax.axis_size("seq")
    cores = lax.axis_size("dp")
    spot = lax.axis_index("seq")
    core = lax.axis_index("dp")
    low, level = spot & 1, spot >> 1
    place = jnp.stack([low, core]).astype(jnp.int32)
    place, even, lower, outer, odd = lax.optimization_barrier(
        (place, low == 0, level < 2, (level == 0) | (level == 3), (level & 1) == 1)
    )
    q, k, v, g = queries[0], keys[0], values[0], out_grad[0]
    length, features = q.shape
    width = g.shape[1]
    part = features // 2
    half = width // 2
    state = shape((PAIRS, HD, HD), F32)
    some = shape((2, HD, HD), F32)
    rows32 = shape((length, features), F32)
    rows16 = shape((length, features), BF16)
    unit = 2 * H * length * HD
    fast = count == 8 and cores == 2
    swap = [(0, 1), (1, 0)]

    def trade(send):
        return lax.ppermute(send, "seq", [(s, s ^ 1) for s in range(count)])

    states = call(state_body, (some,) * 4, (place, k, v), unit * HD, "state")
    away = g
    if fast:
        (away,) = call(away_body, (shape((length, half), F32),), (place, after(g, states[0])), unit, "away")
        go = lax.ppermute(away, "dp", swap)
    (att,) = call(local_body, (rows32,), (q, k, v), 3 * unit * length, "local")
    (d_normed,) = call(d_normed_body, (rows32,), (g, out_weight), unit * width, "d_normed")
    far_prior, near_prior = exclusive(
        [(states[0], trade(states[1])), (states[2], trade(states[3]))], count, even, False, [(away,), (), (att, d_normed)]
    )

    pieces = (shape((length, part), BF16), shape((length, part), F32), shape((length, part), BF16))
    far, far32, far_att, *some_states = call(
        functools.partial(norm_body, FAR),
        pieces + (some, some),
        (place, q, att, d_normed, after(far_prior[0], near_prior[0]), far_prior[1]),
        unit * HD,
        "norm_far",
    )

    def product(nb, nbo, widths):
        blocks = []
        for w in widths:
            block = shape((2, HD, w * half // sum(widths)), F32)
            blocks += [block, block]
        out = call(weight_body, tuple(blocks), (place, nb, g, nbo, go), unit * half, "weight")
        return list(zip(out[::2], out[1::2]))

    near_own, near_other = near_prior
    if fast:
        chunks = product(far, lax.ppermute(far32, "dp", swap), WIDTHS[0])
        near_own = after(near_own, chunks[0][1])
    near, near32, near_att, keep, send = call(
        functools.partial(norm_body, NEAR),
        pieces + (state, state),
        (place, q, att, d_normed, near_own, near_other, *some_states),
        unit * HD * 64,
        "norm_near",
    )

    received = trade(send)
    def gradients(rows, d_att, prior):
        return call(
            functools.partial(grads_body, rows),
            (pieces[0], pieces[1], pieces[1]),
            (place, q, k, v, d_att, *prior),
            5 * unit * length,
            "grads",
        )

    def finish(own, other):
        return call(
            final_body,
            (rows16, rows16, rows16),
            (place, k, v, *far_grads, *near_grads, own, other),
            4 * unit * HD,
            "final",
        )

    def project(rows):
        return call(
            output_body,
            (shape((length, width), BF16),),
            (rows, near, out_weight),
            unit * width,
            "output",
        )[0]

    scale = 1.0 / math.sqrt(length * count * cores)
    if not fast:
        nb = jnp.concatenate([far[:, :PAIR], near, far[:, PAIR:]], axis=1)
        weight = lax.dot_general(nb, g, TN, preferred_element_type=F32)
        weight = lax.psum_scatter(weight, "dp", scatter_dimension=1, tiled=True)
        weight_grad = lax.psum_scatter(weight, "seq", scatter_dimension=0, tiled=True) * scale
        output = project(far)
        far_grads = gradients(FAR, far_att, far_prior)
        near_grads = gradients(NEAR, near_att, near_prior)
        ((own, other),) = exclusive([(keep, received)], count, even, True, [])
        query_grad, key_grad, value_grad = finish(own, other)
        return output[None], query_grad[None], key_grad[None], value_grad[None], weight_grad

    (far0_keep, far0_send), (far1_keep, far1_send) = chunks
    nbo = lax.ppermute(near32, "dp", swap)
    far0_got = trade(after(far0_send, near_other))
    far_grads = gradients(FAR, after(far_att, send), far_prior)
    received = after(received, far_grads[1])
    (near0_keep, near0_send), (near1_keep, near1_send) = product(after(near, received), nbo, WIDTHS[1])
    near0_got = trade(near0_send)
    total = keep + received
    back1 = hop(total, BACK)
    near1_got = trade(near1_send)
    back1 = after(back1, near0_send)
    total = total + back1
    back2 = hop(total, BACK2)
    far0 = far0_keep + after(far0_got, total)
    far0_out = jnp.where(odd, far0[0], far0[1])
    far0_in = hop(far0_out, NEXT)
    far1_got = trade(after(far1_send, far0))
    near_grads = gradients(NEAR, after(near_att, far0_out), near_prior)
    far0_in = after(far0_in, near_grads[1])
    far0_half = jnp.where(lower, far0[1], far0[0]) + far0_in
    far0_end = hop(far0_half, OUTWARD)
    near0 = near0_keep + after(near0_got, far0_half)
    near0_in = hop(near0, INWARD)
    outside = back1 + after(back2, near0)
    theirs = jnp.where(even, outside, outside + keep)
    other = trade(theirs)
    own = jnp.where(even, outside + received, outside)
    output = project(after(far, theirs))
    far1 = far1_keep + after(far1_got, output)
    far1_out = jnp.where(odd, far1[0], far1[1])
    far1_in = hop(far1_out, NEXT)
    near1 = near1_keep + after(near1_got, far1_out)
    near1_in = hop(near1, INWARD)
    near0_in = after(near0_in, near1, far0_end)
    near0_half = jnp.where(lower, near0[1] + near0_in[1], near0[0] + near0_in[0])
    near0_end = hop(near0_half, ACROSS)
    far1_in = after(far1_in, near0_half)
    far1_half = jnp.where(lower, far1[1], far1[0]) + far1_in
    far1_end = hop(far1_half, OUTWARD)
    near1_in = after(near1_in, far1_half, near0_end)
    near1_half = jnp.where(lower, near1[1] + near1_in[1], near1[0] + near1_in[0])
    near1_end = hop(near1_half, ACROSS)
    query_grad, key_grad, value_grad = finish(own, after(other, near1_half))
    far1_end = after(far1_end, near1_half)

    far_parts = [
        (jnp.where(lower, base[0], base[1]) + got) + end
        for base, got, end in ((far0, far0_in, far0_end), (far1, far1_in, far1_end))
    ]
    near_parts = [
        jnp.where(lower, base[0] + got[0], base[1] + got[1]) + end
        for base, got, end in ((near0, near0_in, near0_end), (near1, near1_in, near1_end))
    ]
    weight_grad = jnp.where(
        outer, jnp.concatenate(far_parts, axis=1), jnp.concatenate(near_parts, axis=1)
    )
    return output[None], query_grad[None], key_grad[None], value_grad[None], weight_grad * scale


NEXT = ((0, 1), (1, 0), (2, 3), (3, 2))
OUTWARD = ((1, 3), (2, 0))
INWARD = ((0, 1), (3, 2))
ACROSS = ((1, 2), (2, 1))
BACK = ((1, 0), (2, 1), (3, 2))
BACK2 = ((2, 0), (3, 1))


def hop(block, links):
    return lax.ppermute(block, "seq", [(2 * a + i, 2 * b + i) for a, b in links for i in range(2)])


def solution(mesh):
    rows = P(("parts", "dp"), "seq", None)
    return jax.shard_map(
        per_device,
        mesh=mesh,
        in_specs=(rows, rows, rows, P(), rows),
        out_specs=(rows, rows, rows, rows, P(("parts", "seq"), "dp")),
        check_vma=False,
    )
```

```python
import functools
import math

import jax
import jax.numpy as jnp
from jax import lax
from jax.experimental import pallas as pl
from jax.experimental.pallas import tpu as pltpu
from jax.sharding import PartitionSpec as P

H = 8
HD = 128
PAIR = 2 * HD
PAIRS = H // 2
FAR = (0, 3)
NEAR = (1, 2)
WIDTHS = ((3, 5), (6, 2))
EPSILON = 1e-06
F32 = jnp.float32
BF16 = jnp.bfloat16
VMEM = pltpu.VMEM
VMEM_LIMIT = 16 << 20
COST = 16

NN = (((1,), (0,)), ((), ()))
NT = (((1,), (1,)), ((), ()))
TN = (((0,), (0,)), ((), ()))


def dot(a, b, dims):
    return lax.dot_general(a, b, dims, preferred_element_type=F32)


def halves(a):
    high = a.astype(BF16)
    return high, (a - high.astype(F32)).astype(BF16)


def two_pass(a, b, dims):
    high, low = halves(a)
    return dot(high, b, dims) + dot(low, b, dims)


def two_pass_right(a, b, dims):
    high, low = halves(b)
    return dot(a, high, dims) + dot(a, low, dims)


def causal(length, lower):
    rows = lax.broadcasted_iota(jnp.int32, (length, length), 0)
    cols = lax.broadcasted_iota(jnp.int32, (length, length), 1)
    return rows >= cols if lower else rows <= cols


def at(position, size=HD):
    if isinstance(position, int):
        return pl.ds(position * size, size)
    return pl.ds(pl.multiple_of(position * size, size), size)


def shape(dims, dtype):
    return jax.ShapeDtypeStruct(dims, dtype)


def call(body, out_shapes, operands, flops, name):
    specs = []
    for operand in operands:
        space = pltpu.SMEM if operand.dtype == jnp.int32 else VMEM
        specs.append(pl.BlockSpec(memory_space=space))
    return pl.pallas_call(
        body,
        out_shape=tuple(out_shapes),
        in_specs=specs,
        out_specs=tuple(pl.BlockSpec(memory_space=VMEM) for _ in out_shapes),
        compiler_params=pltpu.CompilerParams(vmem_limit_bytes=VMEM_LIMIT),
        cost_estimate=pl.CostEstimate(flops=flops // COST, bytes_accessed=0, transcendentals=0),
        name=name,
    )(*operands)


def after(value, *others):
    return lax.optimization_barrier((value, *others))[0]


def state_body(place, k_ref, v_ref, *outs):
    low = place[0]
    for rows, keep_ref, send_ref in ((FAR, outs[0], outs[1]), (NEAR, outs[2], outs[3])):
        for i, j in enumerate(rows):
            for out, head in ((send_ref, 2 * j + 1 - low), (keep_ref, 2 * j + low)):
                out[i] = dot(k_ref[:, at(head)], v_ref[:, at(head)], TN)


def away_body(place, g_ref, out_ref):
    half = out_ref.shape[1]
    out_ref[...] = g_ref[:, at(1 - place[1], half)].astype(F32)


def local_body(q_ref, k_ref, v_ref, out_ref):
    mask = causal(q_ref.shape[0], True)
    for h in range(H):
        scores = dot(q_ref[:, at(h)], k_ref[:, at(h)], NT)
        scores = jnp.where(mask, scores, 0.0)
        out_ref[:, at(h)] = two_pass(scores, v_ref[:, at(h)], NN)


def d_normed_body(g_ref, w_ref, out_ref):
    @pl.loop(0, PAIRS)
    def _(j):
        out_ref[:, at(j, PAIR)] = dot(g_ref[...], w_ref[at(j, PAIR), :], NT)


def norm_body(rows, place, q_ref, att_ref, dn_ref, own_ref, other_ref, *refs):
    low = place[0]
    nb_ref, nb32_ref, da_ref, keep_ref, send_ref = refs[-5:]
    whole = keep_ref.shape[0] == PAIRS
    if whole:
        for i, j in enumerate(FAR):
            keep_ref[j] = refs[0][i]
            send_ref[j] = refs[1][i]
    for i, j in enumerate(rows):
        for prior, out, part in ((own_ref, keep_ref, low), (other_ref, send_ref, 1 - low)):
            here, there = at(2 * j + part), at(2 * i + part)
            q = q_ref[:, here]
            attended = att_ref[:, here] + two_pass_right(q, prior[i], NN)
            inverse = lax.rsqrt(jnp.mean(attended * attended, axis=-1, keepdims=True) + EPSILON)
            normed = attended * inverse
            rounded = normed.astype(BF16)
            nb_ref[:, there] = rounded
            nb32_ref[:, there] = rounded.astype(F32)
            d_normed = dn_ref[:, here]
            mean = jnp.mean(d_normed * normed, axis=-1, keepdims=True)
            d_att = (inverse * (d_normed - normed * mean)).astype(BF16)
            da_ref[:, there] = d_att
            out[j if whole else i] = dot(q, d_att, TN)


def grads_body(rows, place, q_ref, k_ref, v_ref, da_ref, own_ref, other_ref, qg_ref, kl_ref, vl_ref):
    low = place[0]
    lower = causal(q_ref.shape[0], True)
    upper = causal(q_ref.shape[0], False)
    for i, j in enumerate(rows):
        for prior, part in ((own_ref, low), (other_ref, 1 - low)):
            here, there = at(2 * j + part), at(2 * i + part)
            q, k, v, d_att = q_ref[:, here], k_ref[:, here], v_ref[:, here], da_ref[:, there]
            cross = jnp.where(lower, dot(d_att, v, NT), 0.0)
            part_sum = two_pass(cross, k, NN) + two_pass_right(d_att, prior[i], NT)
            qg_ref[:, there] = part_sum.astype(BF16)
            cross = jnp.where(upper, dot(v, d_att, NT), 0.0)
            kl_ref[:, there] = two_pass(cross, q, NN)
            scores = jnp.where(upper, dot(k, q, NT), 0.0)
            vl_ref[:, there] = two_pass(scores, d_att, NN)


def final_body(place, k_ref, v_ref, *refs):
    low = place[0]
    own_ref, other_ref, qg_ref, kg_ref, vg_ref = refs[-5:]
    for rows, (part_ref, kl_ref, vl_ref) in ((FAR, refs[:3]), (NEAR, refs[3:6])):
        for i, j in enumerate(rows):
            qg_ref[:, at(j, PAIR)] = part_ref[:, at(i, PAIR)]
            for later, part in ((own_ref, low), (other_ref, 1 - low)):
                here, there = at(2 * j + part), at(2 * i + part)
                high, rest = halves(later[j])
                v, k = v_ref[:, here], k_ref[:, here]
                k_sum = kl_ref[:, there] + (dot(v, high, NT) + dot(v, rest, NT))
                kg_ref[:, here] = k_sum.astype(BF16)
                v_sum = vl_ref[:, there] + (dot(k, high, NN) + dot(k, rest, NN))
                vg_ref[:, here] = v_sum.astype(BF16)


def weight_body(place, nb_ref, g_ref, nbo_ref, go_ref, *outs):
    low, core = place[0], place[1]
    half = go_ref.shape[1]
    mine = nb_ref[...]
    theirs = nbo_ref[...].astype(BF16)
    start = 0
    for keep, send in zip(outs[::2], outs[1::2]):
        width = keep.shape[2]
        ours = g_ref[:, pl.ds(pl.multiple_of(core * half + start, HD), width)]
        other = go_ref[:, start : start + width].astype(BF16)
        start += width
        product = dot(mine, ours, TN) + dot(theirs, other, TN)
        for i in range(2):
            first = product[2 * i * HD : (2 * i + 1) * HD]
            second = product[(2 * i + 1) * HD : (2 * i + 2) * HD]
            keep[i] = jnp.where(low == 0, first, second)
            send[i] = jnp.where(low == 0, second, first)


def output_body(far_ref, near_ref, w_ref, out_ref):
    size = 2 * PAIR

    @pl.loop(0, out_ref.shape[1] // size)
    def _(c):
        total = dot(near_ref[...], w_ref[PAIR : 3 * PAIR, at(c, size)], NN)
        total += dot(far_ref[:, :PAIR], w_ref[:PAIR, at(c, size)], NN)
        total += dot(far_ref[:, PAIR:], w_ref[3 * PAIR :, at(c, size)], NN)
        out_ref[:, at(c, size)] = total.astype(BF16)


def exclusive(states, count, even, reverse, pins):
    swap = [(s, s ^ 1) for s in range(count)]
    sign = -2 if reverse else 2
    pairs = count // 2

    def first(here, there):
        return jnp.where(even, there, here) if reverse else jnp.where(even, here, there)

    def links(step):
        return [(s, s + sign * step) for s in range(count) if 0 <= s + sign * step < count]

    received = [got for _, got in states]
    totals = [keep + got for keep, got in states]
    sums = [None for _ in states]
    trail = ()
    step = 1
    while step < pairs:
        pinned = (*trail, *(pins.pop(0) if pins else ()))
        for i, total in enumerate(totals):
            total = after(total, *pinned)
            pinned = (total,)
            trail = (total,) if i else ()
            got = lax.ppermute(total, "seq", links(step))
            sums[i] = got if step == 1 else sums[i] + got
            totals[i] = total + got
        step *= 2
    pinned = (*trail, *(pins.pop(0) if pins else ()))
    results = []
    for (keep, _), got, before in zip(states, received, sums):
        mine = first(before, before + got)
        theirs = after(first(before + keep, before), *pinned)
        pinned = ()
        results.append((mine, lax.ppermute(theirs, "seq", swap)))
    return results


def per_device(queries, keys, values, out_weight, out_grad):
    count = lax.axis_size("seq")
    cores = lax.axis_size("dp")
    spot = lax.axis_index("seq")
    core = lax.axis_index("dp")
    low, level = spot & 1, spot >> 1
    place = jnp.stack([low, core]).astype(jnp.int32)
    place, even, lower, outer, odd = lax.optimization_barrier(
        (place, low == 0, level < 2, (level == 0) | (level == 3), (level & 1) == 1)
    )
    q, k, v, g = queries[0], keys[0], values[0], out_grad[0]
    length, features = q.shape
    width = g.shape[1]
    part = features // 2
    half = width // 2
    state = shape((PAIRS, HD, HD), F32)
    some = shape((2, HD, HD), F32)
    rows32 = shape((length, features), F32)
    rows16 = shape((length, features), BF16)
    unit = 2 * H * length * HD
    fast = count == 8 and cores == 2
    swap = [(0, 1), (1, 0)]

    def trade(send):
        return lax.ppermute(send, "seq", [(s, s ^ 1) for s in range(count)])

    states = call(state_body, (some,) * 4, (place, k, v), unit * HD, "state")
    away = g
    if fast:
        (away,) = call(away_body, (shape((length, half), F32),), (place, after(g, states[0])), unit, "away")
        go = lax.ppermute(away, "dp", swap)
    (att,) = call(local_body, (rows32,), (q, k, v), 3 * unit * length, "local")
    (d_normed,) = call(d_normed_body, (rows32,), (g, out_weight), unit * width, "d_normed")
    far_prior, near_prior = exclusive(
        [(states[0], trade(states[1])), (states[2], trade(states[3]))], count, even, False, [(away,), (att,), (d_normed,)]
    )

    pieces = (shape((length, part), BF16), shape((length, part), F32), shape((length, part), BF16))
    far, far32, far_att, *some_states = call(
        functools.partial(norm_body, FAR),
        pieces + (some, some),
        (place, q, att, d_normed, after(far_prior[0], near_prior[0]), far_prior[1]),
        unit * HD,
        "norm_far",
    )

    def product(nb, nbo, widths):
        blocks = []
        for w in widths:
            block = shape((2, HD, w * half // sum(widths)), F32)
            blocks += [block, block]
        out = call(weight_body, tuple(blocks), (place, nb, g, nbo, go), unit * half, "weight")
        return list(zip(out[::2], out[1::2]))

    near_own, near_other = near_prior
    if fast:
        chunks = product(far, lax.ppermute(far32, "dp", swap), WIDTHS[0])
        near_own = after(near_own, chunks[0][1])
    near, near32, near_att, keep, send = call(
        functools.partial(norm_body, NEAR),
        pieces + (state, state),
        (place, q, att, d_normed, near_own, near_other, *some_states),
        unit * HD * 64,
        "norm_near",
    )

    received = trade(send)
    def gradients(rows, d_att, prior):
        return call(
            functools.partial(grads_body, rows),
            (pieces[0], pieces[1], pieces[1]),
            (place, q, k, v, d_att, *prior),
            5 * unit * length,
            "grads",
        )

    def finish(own, other):
        return call(
            final_body,
            (rows16, rows16, rows16),
            (place, k, v, *far_grads, *near_grads, own, other),
            4 * unit * HD,
            "final",
        )

    def project(rows):
        return call(
            output_body,
            (shape((length, width), BF16),),
            (rows, near, out_weight),
            unit * width,
            "output",
        )[0]

    scale = 1.0 / math.sqrt(length * count * cores)
    if not fast:
        nb = jnp.concatenate([far[:, :PAIR], near, far[:, PAIR:]], axis=1)
        weight = lax.dot_general(nb, g, TN, preferred_element_type=F32)
        weight = lax.psum_scatter(weight, "dp", scatter_dimension=1, tiled=True)
        weight_grad = lax.psum_scatter(weight, "seq", scatter_dimension=0, tiled=True) * scale
        output = project(far)
        far_grads = gradients(FAR, far_att, far_prior)
        near_grads = gradients(NEAR, near_att, near_prior)
        ((own, other),) = exclusive([(keep, received)], count, even, True, [])
        query_grad, key_grad, value_grad = finish(own, other)
        return output[None], query_grad[None], key_grad[None], value_grad[None], weight_grad

    (far0_keep, far0_send), (far1_keep, far1_send) = chunks
    nbo = lax.ppermute(near32, "dp", swap)
    far0_got = trade(after(far0_send, near_other))
    far_grads = gradients(FAR, after(far_att, send), far_prior)
    received = after(received, far_grads[1])
    (near0_keep, near0_send), (near1_keep, near1_send) = product(after(near, received), nbo, WIDTHS[1])
    near0_got = trade(near0_send)
    total = keep + after(received, near0_send)
    back1 = hop(total, BACK)
    near1_got = trade(near1_send)
    back1 = after(back1, near0_send)
    total = total + back1
    back2 = hop(total, BACK2)
    far0 = far0_keep + after(far0_got, total)
    far0_out = jnp.where(odd, far0[0], far0[1])
    far0_in = hop(far0_out, NEXT)
    far1_got = trade(after(far1_send, far0))
    near_grads = gradients(NEAR, after(near_att, far0_out), near_prior)
    far0_in = after(far0_in, near_grads[1])
    far0_half = jnp.where(lower, far0[1], far0[0]) + far0_in
    far0_end = hop(far0_half, OUTWARD)
    near0 = near0_keep + after(near0_got, far0_half)
    near0_in = hop(near0, INWARD)
    outside = back1 + after(back2, near0)
    theirs = jnp.where(even, outside, outside + keep)
    own = jnp.where(even, outside + received, outside)
    output = project(after(far, theirs))
    far1 = far1_keep + after(far1_got, output)
    far1_out = jnp.where(odd, far1[0], far1[1])
    far1_in = hop(far1_out, NEXT)
    near1 = near1_keep + after(near1_got, far1_out)
    near1_in = hop(near1, INWARD)
    other = trade(after(theirs, near1))
    near0_in = after(near0_in, near1, far0_end)
    near0_half = jnp.where(lower, near0[1] + near0_in[1], near0[0] + near0_in[0])
    near0_end = hop(near0_half, ACROSS)
    far1_in = after(far1_in, near0_half)
    far1_half = jnp.where(lower, far1[1], far1[0]) + far1_in
    far1_end = hop(far1_half, OUTWARD)
    near1_in = after(near1_in, far1_half, near0_end)
    near1_half = jnp.where(lower, near1[1] + near1_in[1], near1[0] + near1_in[0])
    near1_end = hop(near1_half, ACROSS)
    query_grad, key_grad, value_grad = finish(own, after(other, near1_half))
    far1_end = after(far1_end, near1_half)

    far_parts = [
        (jnp.where(lower, base[0], base[1]) + got) + end
        for base, got, end in ((far0, far0_in, far0_end), (far1, far1_in, far1_end))
    ]
    near_parts = [
        jnp.where(lower, base[0] + got[0], base[1] + got[1]) + end
        for base, got, end in ((near0, near0_in, near0_end), (near1, near1_in, near1_end))
    ]
    weight_grad = jnp.where(
        outer, jnp.concatenate(far_parts, axis=1), jnp.concatenate(near_parts, axis=1)
    )
    return output[None], query_grad[None], key_grad[None], value_grad[None], weight_grad * scale


NEXT = ((0, 1), (1, 0), (2, 3), (3, 2))
OUTWARD = ((1, 3), (2, 0))
INWARD = ((0, 1), (3, 2))
ACROSS = ((1, 2), (2, 1))
BACK = ((1, 0), (2, 1), (3, 2))
BACK2 = ((2, 0), (3, 1))


def hop(block, links):
    return lax.ppermute(block, "seq", [(2 * a + i, 2 * b + i) for a, b in links for i in range(2)])


def solution(mesh):
    rows = P(("parts", "dp"), "seq", None)
    return jax.shard_map(
        per_device,
        mesh=mesh,
        in_specs=(rows, rows, rows, P(), rows),
        out_specs=(rows, rows, rows, rows, P(("parts", "seq"), "dp")),
        check_vma=False,
    )
```

```python
import functools
import math

import jax
import jax.numpy as jnp
from jax import lax
from jax.experimental import pallas as pl
from jax.experimental.pallas import tpu as pltpu
from jax.sharding import PartitionSpec as P

H = 8
HD = 128
PAIR = 2 * HD
PAIRS = H // 2
FAR = (0, 3)
NEAR = (1, 2)
WIDTHS = ((4, 4), (4, 4))
EPSILON = 1e-06
F32 = jnp.float32
BF16 = jnp.bfloat16
VMEM = pltpu.VMEM
VMEM_LIMIT = 16 << 20
COST = 16

NN = (((1,), (0,)), ((), ()))
NT = (((1,), (1,)), ((), ()))
TN = (((0,), (0,)), ((), ()))


def dot(a, b, dims):
    return lax.dot_general(a, b, dims, preferred_element_type=F32)


def halves(a):
    high = a.astype(BF16)
    return high, (a - high.astype(F32)).astype(BF16)


def two_pass(a, b, dims):
    high, low = halves(a)
    return dot(high, b, dims) + dot(low, b, dims)


def two_pass_right(a, b, dims):
    high, low = halves(b)
    return dot(a, high, dims) + dot(a, low, dims)


def causal(length, lower):
    rows = lax.broadcasted_iota(jnp.int32, (length, length), 0)
    cols = lax.broadcasted_iota(jnp.int32, (length, length), 1)
    return rows >= cols if lower else rows <= cols


def at(position, size=HD):
    if isinstance(position, int):
        return pl.ds(position * size, size)
    return pl.ds(pl.multiple_of(position * size, size), size)


def shape(dims, dtype):
    return jax.ShapeDtypeStruct(dims, dtype)


def call(body, out_shapes, operands, flops, name):
    specs = []
    for operand in operands:
        space = pltpu.SMEM if operand.dtype == jnp.int32 else VMEM
        specs.append(pl.BlockSpec(memory_space=space))
    return pl.pallas_call(
        body,
        out_shape=tuple(out_shapes),
        in_specs=specs,
        out_specs=tuple(pl.BlockSpec(memory_space=VMEM) for _ in out_shapes),
        compiler_params=pltpu.CompilerParams(vmem_limit_bytes=VMEM_LIMIT),
        cost_estimate=pl.CostEstimate(flops=flops // COST, bytes_accessed=0, transcendentals=0),
        name=name,
    )(*operands)


def after(value, *others):
    return lax.optimization_barrier((value, *others))[0]


def state_body(place, k_ref, v_ref, *outs):
    low = place[0]
    for rows, keep_ref, send_ref in ((FAR, outs[0], outs[1]), (NEAR, outs[2], outs[3])):
        for i, j in enumerate(rows):
            for out, head in ((send_ref, 2 * j + 1 - low), (keep_ref, 2 * j + low)):
                out[i] = dot(k_ref[:, at(head)], v_ref[:, at(head)], TN)


def away_body(place, g_ref, out_ref):
    half = out_ref.shape[1]
    out_ref[...] = g_ref[:, at(1 - place[1], half)].astype(F32)


def local_body(q_ref, k_ref, v_ref, out_ref):
    mask = causal(q_ref.shape[0], True)
    for h in range(H):
        scores = dot(q_ref[:, at(h)], k_ref[:, at(h)], NT)
        scores = jnp.where(mask, scores, 0.0)
        out_ref[:, at(h)] = two_pass(scores, v_ref[:, at(h)], NN)


def d_normed_body(g_ref, w_ref, out_ref):
    @pl.loop(0, PAIRS)
    def _(j):
        out_ref[:, at(j, PAIR)] = dot(g_ref[...], w_ref[at(j, PAIR), :], NT)


def norm_body(rows, place, q_ref, att_ref, dn_ref, own_ref, other_ref, *refs):
    low = place[0]
    nb_ref, nb32_ref, da_ref, keep_ref, send_ref = refs[-5:]
    whole = keep_ref.shape[0] == PAIRS
    if whole:
        for i, j in enumerate(FAR):
            keep_ref[j] = refs[0][i]
            send_ref[j] = refs[1][i]
    for i, j in enumerate(rows):
        for prior, out, part in ((own_ref, keep_ref, low), (other_ref, send_ref, 1 - low)):
            here, there = at(2 * j + part), at(2 * i + part)
            q = q_ref[:, here]
            attended = att_ref[:, here] + two_pass_right(q, prior[i], NN)
            inverse = lax.rsqrt(jnp.mean(attended * attended, axis=-1, keepdims=True) + EPSILON)
            normed = attended * inverse
            rounded = normed.astype(BF16)
            nb_ref[:, there] = rounded
            nb32_ref[:, there] = rounded.astype(F32)
            d_normed = dn_ref[:, here]
            mean = jnp.mean(d_normed * normed, axis=-1, keepdims=True)
            d_att = (inverse * (d_normed - normed * mean)).astype(BF16)
            da_ref[:, there] = d_att
            out[j if whole else i] = dot(q, d_att, TN)


def grads_body(rows, place, q_ref, k_ref, v_ref, da_ref, own_ref, other_ref, qg_ref, kl_ref, vl_ref):
    low = place[0]
    lower = causal(q_ref.shape[0], True)
    upper = causal(q_ref.shape[0], False)
    for i, j in enumerate(rows):
        for prior, part in ((own_ref, low), (other_ref, 1 - low)):
            here, there = at(2 * j + part), at(2 * i + part)
            q, k, v, d_att = q_ref[:, here], k_ref[:, here], v_ref[:, here], da_ref[:, there]
            cross = jnp.where(lower, dot(d_att, v, NT), 0.0)
            part_sum = two_pass(cross, k, NN) + two_pass_right(d_att, prior[i], NT)
            qg_ref[:, there] = part_sum.astype(BF16)
            cross = jnp.where(upper, dot(v, d_att, NT), 0.0)
            kl_ref[:, there] = two_pass(cross, q, NN)
            scores = jnp.where(upper, dot(k, q, NT), 0.0)
            vl_ref[:, there] = two_pass(scores, d_att, NN)


def final_body(place, k_ref, v_ref, *refs):
    low = place[0]
    own_ref, other_ref, qg_ref, kg_ref, vg_ref = refs[-5:]
    for rows, (part_ref, kl_ref, vl_ref) in ((FAR, refs[:3]), (NEAR, refs[3:6])):
        for i, j in enumerate(rows):
            qg_ref[:, at(j, PAIR)] = part_ref[:, at(i, PAIR)]
            for later, part in ((own_ref, low), (other_ref, 1 - low)):
                here, there = at(2 * j + part), at(2 * i + part)
                high, rest = halves(later[j])
                v, k = v_ref[:, here], k_ref[:, here]
                k_sum = kl_ref[:, there] + (dot(v, high, NT) + dot(v, rest, NT))
                kg_ref[:, here] = k_sum.astype(BF16)
                v_sum = vl_ref[:, there] + (dot(k, high, NN) + dot(k, rest, NN))
                vg_ref[:, here] = v_sum.astype(BF16)


def weight_body(place, nb_ref, g_ref, nbo_ref, go_ref, *outs):
    low, core = place[0], place[1]
    half = go_ref.shape[1]
    mine = nb_ref[...]
    theirs = nbo_ref[...].astype(BF16)
    start = 0
    for keep, send in zip(outs[::2], outs[1::2]):
        width = keep.shape[2]
        ours = g_ref[:, pl.ds(pl.multiple_of(core * half + start, HD), width)]
        other = go_ref[:, start : start + width].astype(BF16)
        start += width
        product = dot(mine, ours, TN) + dot(theirs, other, TN)
        for i in range(2):
            first = product[2 * i * HD : (2 * i + 1) * HD]
            second = product[(2 * i + 1) * HD : (2 * i + 2) * HD]
            keep[i] = jnp.where(low == 0, first, second)
            send[i] = jnp.where(low == 0, second, first)


def output_body(far_ref, near_ref, w_ref, out_ref):
    size = 2 * PAIR

    @pl.loop(0, out_ref.shape[1] // size)
    def _(c):
        total = dot(near_ref[...], w_ref[PAIR : 3 * PAIR, at(c, size)], NN)
        total += dot(far_ref[:, :PAIR], w_ref[:PAIR, at(c, size)], NN)
        total += dot(far_ref[:, PAIR:], w_ref[3 * PAIR :, at(c, size)], NN)
        out_ref[:, at(c, size)] = total.astype(BF16)


def exclusive(states, count, even, reverse, pins):
    swap = [(s, s ^ 1) for s in range(count)]
    sign = -2 if reverse else 2
    pairs = count // 2

    def first(here, there):
        return jnp.where(even, there, here) if reverse else jnp.where(even, here, there)

    def links(step):
        return [(s, s + sign * step) for s in range(count) if 0 <= s + sign * step < count]

    received = [got for _, got in states]
    totals = [keep + got for keep, got in states]
    sums = [None for _ in states]
    trail = ()
    step = 1
    while step < pairs:
        pinned = (*trail, *(pins.pop(0) if pins else ()))
        for i, total in enumerate(totals):
            total = after(total, *pinned)
            pinned = (total,)
            trail = (total,) if i else ()
            got = lax.ppermute(total, "seq", links(step))
            sums[i] = got if step == 1 else sums[i] + got
            totals[i] = total + got
        step *= 2
    pinned = (*trail, *(pins.pop(0) if pins else ()))
    results = []
    for (keep, _), got, before in zip(states, received, sums):
        mine = first(before, before + got)
        theirs = after(first(before + keep, before), *pinned)
        pinned = ()
        results.append((mine, lax.ppermute(theirs, "seq", swap)))
    return results


def per_device(queries, keys, values, out_weight, out_grad):
    count = lax.axis_size("seq")
    cores = lax.axis_size("dp")
    spot = lax.axis_index("seq")
    core = lax.axis_index("dp")
    low, level = spot & 1, spot >> 1
    place = jnp.stack([low, core]).astype(jnp.int32)
    place, even, lower, outer, odd = lax.optimization_barrier(
        (place, low == 0, level < 2, (level == 0) | (level == 3), (level & 1) == 1)
    )
    q, k, v, g = queries[0], keys[0], values[0], out_grad[0]
    length, features = q.shape
    width = g.shape[1]
    part = features // 2
    half = width // 2
    state = shape((PAIRS, HD, HD), F32)
    some = shape((2, HD, HD), F32)
    rows32 = shape((length, features), F32)
    rows16 = shape((length, features), BF16)
    unit = 2 * H * length * HD
    fast = count == 8 and cores == 2
    swap = [(0, 1), (1, 0)]

    def trade(send):
        return lax.ppermute(send, "seq", [(s, s ^ 1) for s in range(count)])

    states = call(state_body, (some,) * 4, (place, k, v), unit * HD, "state")
    away = g
    if fast:
        (away,) = call(away_body, (shape((length, half), F32),), (place, after(g, states[0])), unit, "away")
        go = lax.ppermute(away, "dp", swap)
    (att,) = call(local_body, (rows32,), (q, k, v), 3 * unit * length, "local")
    (d_normed,) = call(d_normed_body, (rows32,), (g, out_weight), unit * width, "d_normed")
    far_prior, near_prior = exclusive(
        [(states[0], trade(states[1])), (states[2], trade(states[3]))], count, even, False, [(away,), (att,), (d_normed,)]
    )

    pieces = (shape((length, part), BF16), shape((length, part), F32), shape((length, part), BF16))
    far, far32, far_att, *some_states = call(
        functools.partial(norm_body, FAR),
        pieces + (some, some),
        (place, q, att, d_normed, after(far_prior[0], near_prior[0]), far_prior[1]),
        unit * HD,
        "norm_far",
    )

    def product(nb, nbo, widths):
        blocks = []
        for w in widths:
            block = shape((2, HD, w * half // sum(widths)), F32)
            blocks += [block, block]
        out = call(weight_body, tuple(blocks), (place, nb, g, nbo, go), unit * half, "weight")
        return list(zip(out[::2], out[1::2]))

    near_own, near_other = near_prior
    if fast:
        chunks = product(far, lax.ppermute(far32, "dp", swap), WIDTHS[0])
        near_own = after(near_own, chunks[0][1])
    near, near32, near_att, keep, send = call(
        functools.partial(norm_body, NEAR),
        pieces + (state, state),
        (place, q, att, d_normed, near_own, near_other, *some_states),
        unit * HD * 64,
        "norm_near",
    )

    received = trade(send)
    def gradients(rows, d_att, prior):
        return call(
            functools.partial(grads_body, rows),
            (pieces[0], pieces[1], pieces[1]),
            (place, q, k, v, d_att, *prior),
            5 * unit * length,
            "grads",
        )

    def finish(own, other):
        return call(
            final_body,
            (rows16, rows16, rows16),
            (place, k, v, *far_grads, *near_grads, own, other),
            4 * unit * HD,
            "final",
        )

    def project(rows):
        return call(
            output_body,
            (shape((length, width), BF16),),
            (rows, near, out_weight),
            unit * width,
            "output",
        )[0]

    scale = 1.0 / math.sqrt(length * count * cores)
    if not fast:
        nb = jnp.concatenate([far[:, :PAIR], near, far[:, PAIR:]], axis=1)
        weight = lax.dot_general(nb, g, TN, preferred_element_type=F32)
        weight = lax.psum_scatter(weight, "dp", scatter_dimension=1, tiled=True)
        weight_grad = lax.psum_scatter(weight, "seq", scatter_dimension=0, tiled=True) * scale
        output = project(far)
        far_grads = gradients(FAR, far_att, far_prior)
        near_grads = gradients(NEAR, near_att, near_prior)
        ((own, other),) = exclusive([(keep, received)], count, even, True, [])
        query_grad, key_grad, value_grad = finish(own, other)
        return output[None], query_grad[None], key_grad[None], value_grad[None], weight_grad

    (far0_keep, far0_send), (far1_keep, far1_send) = chunks
    nbo = lax.ppermute(near32, "dp", swap)
    far0_got = trade(after(far0_send, near_other))
    far_grads = gradients(FAR, after(far_att, send), far_prior)
    received = after(received, far_grads[1])
    (near0_keep, near0_send), (near1_keep, near1_send) = product(after(near, received), nbo, WIDTHS[1])
    near0_got = trade(near0_send)
    total = keep + received
    back1 = hop(total, BACK)
    near1_got = trade(near1_send)
    back1 = after(back1, near0_send)
    total = total + back1
    back2 = hop(total, BACK2)
    far0 = far0_keep + after(far0_got, total)
    far0_out = jnp.where(odd, far0[0], far0[1])
    far0_in = hop(far0_out, NEXT)
    far1_got = trade(after(far1_send, far0))
    near_grads = gradients(NEAR, after(near_att, far0_out), near_prior)
    far0_in = after(far0_in, near_grads[1])
    far0_half = jnp.where(lower, far0[1], far0[0]) + far0_in
    far0_end = hop(far0_half, OUTWARD)
    near0 = near0_keep + after(near0_got, far0_half)
    near0_in = hop(near0, INWARD)
    outside = back1 + after(back2, near0)
    theirs = jnp.where(even, outside, outside + keep)
    other = trade(theirs)
    own = jnp.where(even, outside + received, outside)
    output = project(after(far, theirs))
    far1 = far1_keep + after(far1_got, output)
    far1_out = jnp.where(odd, far1[0], far1[1])
    far1_in = hop(far1_out, NEXT)
    near0_in = after(near0_in, far1_out, far0_end)
    near0_half = jnp.where(lower, near0[1] + near0_in[1], near0[0] + near0_in[0])
    near0_end = hop(near0_half, ACROSS)
    near1 = near1_keep + after(near1_got, near0_half)
    near1_in = hop(near1, INWARD)
    far1_in = after(far1_in, near1)
    far1_half = jnp.where(lower, far1[1], far1[0]) + far1_in
    far1_end = hop(far1_half, OUTWARD)
    near1_in = after(near1_in, far1_half)
    near1_half = jnp.where(lower, near1[1] + near1_in[1], near1[0] + near1_in[0])
    near1_end = hop(near1_half, ACROSS)
    query_grad, key_grad, value_grad = finish(own, after(other, near1_half))
    near0_end, far1_end = after(near0_end, near1_half), after(far1_end, near1_half)

    far_parts = [
        (jnp.where(lower, base[0], base[1]) + got) + end
        for base, got, end in ((far0, far0_in, far0_end), (far1, far1_in, far1_end))
    ]
    near_parts = [
        jnp.where(lower, base[0] + got[0], base[1] + got[1]) + end
        for base, got, end in ((near0, near0_in, near0_end), (near1, near1_in, near1_end))
    ]
    weight_grad = jnp.where(
        outer, jnp.concatenate(far_parts, axis=1), jnp.concatenate(near_parts, axis=1)
    )
    return output[None], query_grad[None], key_grad[None], value_grad[None], weight_grad * scale


NEXT = ((0, 1), (1, 0), (2, 3), (3, 2))
OUTWARD = ((1, 3), (2, 0))
INWARD = ((0, 1), (3, 2))
ACROSS = ((1, 2), (2, 1))
BACK = ((1, 0), (2, 1), (3, 2))
BACK2 = ((2, 0), (3, 1))


def hop(block, links):
    return lax.ppermute(block, "seq", [(2 * a + i, 2 * b + i) for a, b in links for i in range(2)])


def solution(mesh):
    rows = P(("parts", "dp"), "seq", None)
    return jax.shard_map(
        per_device,
        mesh=mesh,
        in_specs=(rows, rows, rows, P(), rows),
        out_specs=(rows, rows, rows, rows, P(("parts", "seq"), "dp")),
        check_vma=False,
    )
```
